32 devices in a mesh: grid: 8 (over z, core), vec: 4 (over y, x).
Axes of the slice: x: 2, y: 2, z: 4, core: 2. Of those that a mesh axis runs over, the one named last changes fastest.
Arguments:
- orbitals: bfloat16 [884736, 512], P(('grid', 'vec')), may hold values from -1.296875 to 1.296875
- inverse_panel: bfloat16 [2048, 32], replicated, may hold values from -0.125 to 0.125
- points: int32 [2048], replicated, may hold values from 0 to 884735, as said below
Outputs:
- projected: float32 [2048, 32], P(('grid', 'vec'))
The draws below stay inside these ranges and needn't reach their ends.
Inputs may be any that keep to these rules, and one draw needn't show every extreme that they name: `points`: distinct cell indices.
All inputs are finite; a program needn't handle non-finite values.
Results may differ from the reference program's by a relative error of at most 0.005.
Values may be sent and summed in bfloat16 or wider, within the bound.
A program may use at most 256 MiB of HBM per device.

```python
import math
import jax
import jax.numpy as jnp
from jax import lax

NG = 96
NORB = 512
NPTS = 2048
COLS = 32


def draw_points(key, part):
    return jax.random.permutation(key, NG ** 3)[:NPTS].astype(jnp.int32)


def block_scale(stream_key, shape, cuts, least, high):
    level = 1.0
    for position, parts in cuts:
        draws = jax.random.uniform(jax.random.fold_in(jax.random.fold_in(stream_key, 6), position), (parts,), jnp.float32, least / len(cuts), high / len(cuts))
        level = level * jnp.repeat(jnp.exp(draws), shape[position] // parts).reshape((-1,) + (1,) * (len(shape) - 1 - position))
    return level


def normal_values(stream_key, dims, width, limit, shards=(), held_as=jnp.bfloat16):
    values = jax.random.normal(stream_key, dims, jnp.float32) * width
    if len(shards) > 0:
        values = block_scale(stream_key, dims, shards, -0.22, 0.18) * values
    return jnp.clip(values, min=-limit, max=limit).astype(held_as)


def setup_inputs(seed: int = 0) -> dict:
    seeds = jax.random.split(jax.random.key(seed), 4)
    return {
        "orbitals": normal_values(seeds[0], (NG**3, NORB), 0.21, 1.296875, ((0, 32),)),
        "inverse_panel": normal_values(seeds[1], (NPTS, COLS), NPTS ** -0.5, 0.125),
        "points": draw_points(jax.random.fold_in(seeds[3], 71), 0),
    }


SCREEN = 2.25

def wave_tables(count):
    index = lax.iota(jnp.int32, count)
    phase = index[:, None] * index[None, :] % count
    angle = phase.astype(jnp.float32) * (2.0 * math.pi / count)
    return (jnp.cos(angle).astype(jnp.bfloat16), jnp.sin(angle).astype(jnp.bfloat16))

def wavenumber(index, count):
    return jnp.where(index < count // 2, index, index - count).astype(jnp.float32)

def screened(wave_x, wave_y, wave_z):
    squared = wave_x[:, None, None] * wave_x[:, None, None] + wave_y[None, :, None] * wave_y[None, :, None] + wave_z[None, None, :] * wave_z[None, None, :]
    factor = NG / (2.0 * math.pi) * (NG / (2.0 * math.pi))
    return jnp.where(squared > 0.5, factor / (squared + SCREEN), jnp.float32(0.0))

def contract(data, table, form):
    return jnp.einsum(form, data.astype(jnp.float32), table.astype(jnp.float32))

def poisson(column, cos_tab, sin_tab, kernel):
    bf = jnp.bfloat16
    z_re = contract(column, cos_tab, 'xyz,zk->xyk').astype(bf)
    z_im = (-contract(column, sin_tab, 'xyz,zk->xyk')).astype(bf)
    y_re = (contract(z_re, cos_tab, 'xyz,yk->xkz') + contract(z_im, sin_tab, 'xyz,yk->xkz')).astype(bf)
    y_im = (contract(z_im, cos_tab, 'xyz,yk->xkz') - contract(z_re, sin_tab, 'xyz,yk->xkz')).astype(bf)
    x_re = contract(y_re, cos_tab, 'xyz,xk->kyz') + contract(y_im, sin_tab, 'xyz,xk->kyz')
    x_im = contract(y_im, cos_tab, 'xyz,xk->kyz') - contract(y_re, sin_tab, 'xyz,xk->kyz')
    q_re = (x_re * kernel).astype(bf)
    q_im = (x_im * kernel).astype(bf)
    i_re = (contract(q_re, cos_tab, 'xyz,xk->kyz') - contract(q_im, sin_tab, 'xyz,xk->kyz')).astype(bf)
    i_im = (contract(q_im, cos_tab, 'xyz,xk->kyz') + contract(q_re, sin_tab, 'xyz,xk->kyz')).astype(bf)
    h_re = (contract(i_re, cos_tab, 'xyz,yk->xkz') - contract(i_im, sin_tab, 'xyz,yk->xkz')).astype(bf)
    h_im = (contract(i_im, cos_tab, 'xyz,yk->xkz') + contract(i_re, sin_tab, 'xyz,yk->xkz')).astype(bf)
    final = contract(h_re, cos_tab, 'xyz,zk->xyk') - contract(h_im, sin_tab, 'xyz,zk->xyk')
    return (final / float(NG ** 3)).astype(bf)

def reference(orbitals, inverse_panel, points):
    point_rows = orbitals[points]
    blocks = orbitals.reshape(NG, NG * NG, NORB)

    def make_pair(block):
        correlation = jnp.dot(block, point_rows.T, preferred_element_type=jnp.float32)
        return (correlation * correlation).astype(jnp.bfloat16)

    def fit_block(block):
        return jnp.dot(make_pair(block), inverse_panel, preferred_element_type=jnp.float32).astype(jnp.bfloat16)
    fitted = lax.map(fit_block, blocks)
    field = jnp.moveaxis(fitted.reshape(NG, NG, NG, COLS), 3, 0)
    cos_tab, sin_tab = wave_tables(NG)
    waves = wavenumber(lax.iota(jnp.int32, NG), NG)
    kernel = screened(waves, waves, waves)
    potential = lax.map(lambda column: poisson(column, cos_tab, sin_tab, kernel), field)
    pot_blocks = jnp.moveaxis(potential.reshape(COLS, NG, NG * NG), 1, 0)

    def accumulate(total, pieces):
        block, pot_block = pieces
        pair = make_pair(block)
        term = lax.dot_general(pair, pot_block, (((0,), (1,)), ((), ())), preferred_element_type=jnp.float32)
        return (total + term, None)
    total, _ = lax.scan(accumulate, jnp.zeros((NPTS, COLS), jnp.float32), (blocks, pot_blocks))
    return total * jnp.float32(1.0 / math.sqrt(float(NG ** 3)))
```

```python
import math

import jax
import jax.numpy as jnp
from jax import lax
from jax.experimental import pallas as pl
from jax.experimental.pallas import tpu as pltpu
from jax.sharding import PartitionSpec as P

NG = 96


SCREEN = 2.25


def wave_tables(count):
    index = lax.iota(jnp.int32, count)
    phase = index[:, None] * index[None, :] % count
    angle = phase.astype(jnp.float32) * (2.0 * math.pi / count)
    return (jnp.cos(angle).astype(jnp.bfloat16), jnp.sin(angle).astype(jnp.bfloat16))


def wavenumber(index, count):
    return jnp.where(index < count // 2, index, index - count).astype(jnp.float32)


def screened(wave_x, wave_y, wave_z):
    squared = (
        wave_x[:, None, None] * wave_x[:, None, None]
        + wave_y[None, :, None] * wave_y[None, :, None]
        + wave_z[None, None, :] * wave_z[None, None, :]
    )
    factor = NG / (2.0 * math.pi) * (NG / (2.0 * math.pi))
    return jnp.where(squared > 0.5, factor / (squared + SCREEN), jnp.float32(0.0))


def mult(data, table, form):
    return jnp.einsum(form, data, table, preferred_element_type=jnp.float32)


LANES = 128


def exchange_kernel(axes, total, gather, x_ref, o_ref, held, send_sem, recv_sem, own_sem):
    if len(axes) == 2:
        vec_count = lax.axis_size("vec")
        count = lax.axis_size("grid") * vec_count
        me = lax.axis_index("grid") * vec_count + lax.axis_index("vec")
    else:
        count = lax.axis_size(axes[0])
        me = lax.axis_index(axes[0])
    land = held if total else o_ref

    def place(index):
        if len(axes) == 2:
            return (index // vec_count, lax.rem(index, vec_count))
        if axes[0] == "grid":
            return (index, lax.axis_index("vec"))
        return (lax.axis_index("grid"), index)

    def part(index):
        return x_ref if gather else x_ref.at[index]

    barrier = pltpu.get_barrier_semaphore()

    def greet(step, carry):
        pl.semaphore_signal(
            barrier,
            inc=1,
            device_id=place(lax.rem(me + step, count)),
            device_id_type=pl.DeviceIdType.MESH,
        )
        return carry

    lax.fori_loop(1, count, greet, 0)
    own = pltpu.make_async_copy(part(me), land.at[me], own_sem)
    own.start()
    pl.semaphore_wait(barrier, count - 1)

    def copy(step, source, slot):
        peer = lax.rem(me + step, count)
        return pltpu.make_async_remote_copy(
            src_ref=part(source),
            dst_ref=land.at[slot],
            send_sem=send_sem.at[step],
            recv_sem=recv_sem.at[step],
            device_id=place(peer),
            device_id_type=pl.DeviceIdType.MESH,
        )

    def send(step, carry):
        copy(step, lax.rem(me + step, count), me).start()
        return carry

    lax.fori_loop(1, count, send, 0)
    own.wait()

    def receive(step, carry):
        source = lax.rem(me + count - step, count)
        copy(step, source, source).wait_recv()
        return carry

    lax.fori_loop(1, count, receive, 0)
    if total:
        o_ref[...] = jnp.sum(held[...].astype(jnp.float32), axis=0).astype(o_ref.dtype)

    def drain(step, carry):
        copy(step, lax.rem(me + step, count), me).wait_send()
        return carry

    lax.fori_loop(1, count, drain, 0)


def exchange(blocks, ident, total=False, axes=("grid", "vec"), gather=False):
    rows, lanes = blocks.shape[-2:]
    count = 1
    for axis in axes:
        count *= lax.axis_size(axis)
    shape = (rows, lanes) if total else (count, rows, lanes)
    held_shape = blocks.shape if total else (1, 8, LANES)

    def body(*refs):
        exchange_kernel(axes, total, gather, *refs)

    return pl.pallas_call(
        body,
        out_shape=jax.ShapeDtypeStruct(shape, blocks.dtype),
        in_specs=[pl.BlockSpec(memory_space=pltpu.VMEM)],
        out_specs=pl.BlockSpec(memory_space=pltpu.VMEM),
        scratch_shapes=[
            pltpu.VMEM(held_shape, blocks.dtype),
            pltpu.SemaphoreType.DMA((count,)),
            pltpu.SemaphoreType.DMA((count,)),
            pltpu.SemaphoreType.DMA(()),
        ],
        compiler_params=pltpu.CompilerParams(
            collective_id=ident, has_side_effects=True, vmem_limit_bytes=32 << 20
        ),
        name="exchange_total" if total else "exchange_gather" if gather else "exchange_blocks",
    )(blocks)


def share_rows(picked, grid_count, vec_count):
    npoints, norb = picked.shape
    if npoints % (grid_count * vec_count * 16) != 0:
        return lax.psum(picked.astype(jnp.float32), ("grid", "vec")).astype(picked.dtype)
    mine = exchange(
        picked.reshape(vec_count, npoints // vec_count, norb), 4, total=True, axes=("vec",)
    )
    mine = exchange(
        mine.reshape(grid_count, npoints // vec_count // grid_count, norb),
        5,
        total=True,
        axes=("grid",),
    )
    block = exchange(mine, 6, axes=("grid",), gather=True).reshape(npoints // vec_count, norb)
    return exchange(block, 7, axes=("vec",), gather=True).reshape(npoints, norb)


def project(pair, pot_rows):
    scale = 1.0 / math.sqrt(float(NG**3))
    term = lax.dot_general(
        pair, pot_rows, (((0,), (1,)), ((), ())), preferred_element_type=jnp.float32
    )
    term = term * jnp.float32(scale)
    npoints, cols = term.shape
    count = lax.axis_size("grid") * lax.axis_size("vec")
    share = npoints // count
    if share * cols % LANES == 0:
        blocks = term.reshape(count, share * cols // LANES, LANES)
        return exchange(blocks, 3, True).reshape(share, cols)
    partial_block = lax.psum_scatter(term, "grid", scatter_dimension=0, tiled=True)
    return lax.psum_scatter(partial_block, "vec", scatter_dimension=0, tiled=True)


def peers_of():
    vec_count = lax.axis_size("vec")
    count = lax.axis_size("grid") * vec_count
    me = lax.axis_index("grid") * vec_count + lax.axis_index("vec")

    def place(index):
        return (index // vec_count, lax.rem(index, vec_count))

    return count, me, place


def greet_all(count, me, place):
    barrier = pltpu.get_barrier_semaphore()

    def greet(step, carry):
        pl.semaphore_signal(
            barrier,
            inc=1,
            device_id=place(lax.rem(me + step, count)),
            device_id_type=pl.DeviceIdType.MESH,
        )
        return carry

    lax.fori_loop(1, count, greet, 0)


def wait_greeted(count):
    pl.semaphore_wait(pltpu.get_barrier_semaphore(), count - 1)


NT = (((1,), (1,)), ((), ()))
NN = (((1,), (0,)), ((), ()))
LINES = 16
SPAN = LINES * NG
TAKE = 512


def pair_fit_kernel(
    orb_ref, rows_ref, panel_ref, pair_ref, field_ref, fit_rows, out_buf, send_sem, recv_sem, own_sem
):
    bf = jnp.bfloat16
    block = pl.program_id(0)
    blocks = pl.num_programs(0)
    count, me, place = peers_of()
    npoints = rows_ref.shape[0]
    cols = panel_ref.shape[0]
    per_plane = NG // LINES

    def target(index):
        line = pl.multiple_of(lax.rem(index, per_plane) * LINES, LINES)
        return field_ref.at[me, index // per_plane, pl.ds(line, LINES)]

    def copy(index, step):
        slot = lax.rem(index, 2)
        peer = lax.rem(me + step, count)
        return pltpu.make_async_remote_copy(
            src_ref=out_buf.at[slot, peer],
            dst_ref=target(index),
            send_sem=send_sem.at[slot, step],
            recv_sem=recv_sem.at[me],
            device_id=place(peer),
            device_id_type=pl.DeviceIdType.MESH,
        )

    def own(index):
        slot = lax.rem(index, 2)
        return pltpu.make_async_copy(out_buf.at[slot, me], target(index), own_sem.at[slot])

    def send(index):
        def body(step, carry):
            copy(index, step).start()
            return carry

        own(index).start()
        lax.fori_loop(1, count, body, 0)

    def drain(index):
        def body(step, carry):
            copy(index, step).wait_send()
            return carry

        own(index).wait()
        lax.fori_loop(1, count, body, 0)

    @pl.when(block == 0)
    def _():
        greet_all(count, me, place)

    @pl.when(block == 1)
    def _():
        wait_greeted(count)

    @pl.when(block >= 1)
    def _():
        send(block - 1)

    for first in range(0, npoints, TAKE):
        part = lax.dot_general(
            rows_ref[first : first + TAKE, :], orb_ref[...], NT, preferred_element_type=jnp.float32
        )
        pair_ref[0, first : first + TAKE, :] = (part * part).astype(bf)
    fit = lax.dot_general(panel_ref[...], pair_ref[0], NN, preferred_element_type=jnp.float32)

    for line in range(LINES):
        begin = line * NG
        low = begin // LANES * LANES
        turn = begin - low
        if low + 2 * LANES <= SPAN:
            wide = fit[:, low : low + 2 * LANES]
        else:
            wide = jnp.concatenate([fit[:, low : low + LANES]] * 2, axis=1)
        if turn:
            wide = pltpu.roll(wide, 2 * LANES - turn, 1)
        fit_rows[pl.ds(line, cols, stride=LINES), :] = wide[:, :LANES]

    @pl.when(block >= 2)
    def _():
        drain(block - 2)

    out_buf[lax.rem(block, 2)] = fit_rows[...].astype(bf).reshape(cols, LINES, LANES)

    @pl.when(block == blocks - 1)
    def _():
        send(block)

        def receive(step, carry):
            source = lax.rem(me + count - step, count)
            land = field_ref.at[source]
            pltpu.make_async_copy(land, land, recv_sem.at[source]).wait()
            return carry

        lax.fori_loop(1, count, receive, 0)
        drain(block - 1)
        drain(block)


def pair_and_fit(orbitals, point_rows, panel):
    bf = jnp.bfloat16
    rows, norb = orbitals.shape
    npoints = point_rows.shape[0]
    cols = panel.shape[0]
    blocks = rows // SPAN
    planes = rows // (NG * NG)
    count = lax.axis_size("grid") * lax.axis_size("vec")
    return pl.pallas_call(
        pair_fit_kernel,
        grid=(blocks,),
        in_specs=[
            pl.BlockSpec((SPAN, norb), lambda i: (i, 0)),
            pl.BlockSpec((npoints, norb), lambda i: (0, 0)),
            pl.BlockSpec((cols, npoints), lambda i: (0, 0)),
        ],
        out_specs=[
            pl.BlockSpec((1, npoints, SPAN), lambda i: (i, 0, 0)),
            pl.BlockSpec(memory_space=pl.ANY),
        ],
        out_shape=[
            jax.ShapeDtypeStruct((blocks, npoints, SPAN), bf),
            jax.ShapeDtypeStruct((count, planes, NG, LANES), bf),
        ],
        scratch_shapes=[
            pltpu.VMEM((cols * LINES, LANES), jnp.float32),
            pltpu.VMEM((2, cols, LINES, LANES), bf),
            pltpu.SemaphoreType.DMA((2, count)),
            pltpu.SemaphoreType.DMA((count,)),
            pltpu.SemaphoreType.DMA((2,)),
        ],
        compiler_params=pltpu.CompilerParams(
            collective_id=1, has_side_effects=True, vmem_limit_bytes=50 << 20
        ),
        name="pair_fit_send",
    )(orbitals, point_rows, panel)


GROUP = 8
HALF = 64
PIECE = NG * NG // LANES // 3


def solve_kernel(field_ref, tz_ref, ty_ref, tyi_ref, tzi_ref, out_ref, by_y, by_x, flat, dense):
    bf = jnp.bfloat16
    f32 = jnp.float32
    lane = lax.broadcasted_iota(jnp.int32, (NG, LANES), 1)
    row = lax.broadcasted_iota(jnp.int32, (NG, LANES), 0)
    sign = jnp.where(lane < HALF, 1.0, -1.0).astype(f32)
    wave_z = lax.rem(lane, HALF).astype(f32)
    wave_x = jnp.where(row < NG // 2, row, row - NG).astype(f32)
    plane_sq = wave_x * wave_x + wave_z * wave_z
    factor = NG / (2.0 * math.pi) * (NG / (2.0 * math.pi))

    def both(parts):
        top = jnp.concatenate([part.astype(bf) for part in parts], axis=1)
        turned = [(pltpu.roll(part, HALF, 1) * sign).astype(bf) for part in parts]
        return jnp.concatenate([top, jnp.concatenate(turned, axis=1)], axis=0)

    def cut(wide, k):
        return wide[:, k * LANES : (k + 1) * LANES]

    def forward(step, carry):
        first = step * GROUP
        data = field_ref[pl.ds(first, GROUP)].reshape(GROUP * NG, LANES)
        a = lax.dot_general(data, tz_ref[...], NN, preferred_element_type=f32).astype(bf)
        top = [a[k * NG : (k + 1) * NG, :LANES] for k in range(GROUP)]
        low = [a[k * NG : (k + 1) * NG, LANES:] for k in range(GROUP)]
        stack = jnp.concatenate(
            [jnp.concatenate(top, axis=1), jnp.concatenate(low, axis=1)], axis=0
        )
        b = lax.dot_general(ty_ref[...], stack, NN, preferred_element_type=f32)
        for k in range(GROUP):
            by_y[pl.ds(first + k, NG, stride=NG), :] = cut(b, k)
        return carry

    lax.fori_loop(0, NG // GROUP, forward, 0)

    def middle(step, carry):
        first = step * GROUP
        parts = [by_y[pl.ds((first + k) * NG, NG), :] for k in range(GROUP)]
        h = lax.dot_general(ty_ref[...], both(parts), NN, preferred_element_type=f32)
        scaled = []
        for k in range(GROUP):
            index = first + k
            wave_y = jnp.where(index < NG // 2, index, index - NG).astype(f32)
            squared = plane_sq + wave_y * wave_y
            kernel = jnp.where(squared > 0.5, factor / (squared + SCREEN), 0.0)
            scaled.append(cut(h, k) * kernel)
        g = lax.dot_general(tyi_ref[...], both(scaled), NN, preferred_element_type=f32)
        for k in range(GROUP):
            by_x[pl.ds(first + k, NG, stride=NG), :] = cut(g, k)
        return carry

    lax.fori_loop(0, NG // GROUP, middle, 0)

    planes = NG // out_ref.shape[0]
    quarter = NG // 4

    def backward(step, carry):
        first = step * GROUP
        parts = [by_x[pl.ds((first + k) * NG, NG), :] for k in range(GROUP)]
        p = lax.dot_general(tyi_ref[...], both(parts), NN, preferred_element_type=f32).astype(bf)
        rows = jnp.concatenate([cut(p, k) for k in range(GROUP)], axis=0)
        final = lax.dot_general(rows, tzi_ref[...], NN, preferred_element_type=f32)
        flat[...] = final * f32(1.0 / float(NG**3))
        for k in range(GROUP):
            y0, y1, y2, y3 = [
                flat[pl.ds(k * NG + j, quarter, stride=4), :] for j in range(4)
            ]
            spot = lane[:quarter]
            dense[pl.ds(0, quarter, stride=3), :] = jnp.where(
                spot < 96, y0, pltpu.roll(y1, 96, 1)
            )
            dense[pl.ds(1, quarter, stride=3), :] = jnp.where(
                spot < 64, pltpu.roll(y1, 96, 1), pltpu.roll(y2, 64, 1)
            )
            dense[pl.ds(2, quarter, stride=3), :] = jnp.where(
                spot < 32, pltpu.roll(y2, 64, 1), pltpu.roll(y3, 32, 1)
            )
            index = first + k
            for m in range(3):
                out_ref[index // planes, lax.rem(index, planes) * 3 + m] = dense[
                    m * PIECE : (m + 1) * PIECE, :
                ].astype(bf)
        return carry

    lax.fori_loop(0, NG // GROUP, backward, 0)


def solve_field(field, count):
    bf = jnp.bfloat16
    f32 = jnp.float32
    cos_tab, sin_tab = wave_tables(NG)
    keep = NG // 2 + 1

    def wide(table):
        return jnp.pad(table[:, :keep], ((0, LANES - NG), (0, HALF - keep)))

    cz, sz = wide(cos_tab), wide(sin_tab)
    tz = jnp.concatenate([cz, -sz, -sz, -cz], axis=1)
    ty = jnp.concatenate([cos_tab, sin_tab], axis=1)
    tyi = jnp.concatenate([cos_tab, -sin_tab], axis=1)
    spot = lax.iota(jnp.int32, HALF)[:, None]
    weight = jnp.where((spot == 0) | (spot == NG // 2), 1.0, 2.0).astype(bf)
    tzi = jnp.concatenate([cz.T * weight, -(sz.T * weight)], axis=0)
    pieces = NG // count * 3
    return pl.pallas_call(
        solve_kernel,
        out_shape=jax.ShapeDtypeStruct((count, pieces, PIECE, LANES), bf),
        in_specs=[pl.BlockSpec(memory_space=pltpu.VMEM)] * 5,
        out_specs=pl.BlockSpec(memory_space=pltpu.VMEM),
        scratch_shapes=[
            pltpu.VMEM((NG * NG, LANES), f32),
            pltpu.VMEM((NG * NG, LANES), f32),
            pltpu.VMEM((GROUP * NG, LANES), f32),
            pltpu.VMEM((3 * PIECE, LANES), f32),
        ],
        compiler_params=pltpu.CompilerParams(vmem_limit_bytes=40 << 20),
        name="solve_field",
    )(field.reshape(NG, NG, LANES), tz, ty, tyi, tzi)


RING = 6


def project_kernel(
    pot_ref, pair_ref, o_ref, ring, land, wide, total, parts, held,
    send_sem, recv_sem, own_sem, pair_sem, part_send, part_recv,
):
    bf = jnp.bfloat16
    f32 = jnp.float32
    count, me, place = peers_of()
    blocks, npoints, _ = pair_ref.shape
    pieces = pot_ref.shape[1]
    cols = count
    share = npoints // count
    per_piece = blocks // pieces
    strips = SPAN // LANES

    def fetch(block):
        slot = lax.rem(block, RING)
        return pltpu.make_async_copy(pair_ref.at[block], ring.at[slot], pair_sem.at[slot])

    def prime(block, carry):
        fetch(block).start()
        return carry

    greet_all(count, me, place)
    lax.fori_loop(0, RING, prime, 0)
    wait_greeted(count)

    def copy(piece, step):
        peer = lax.rem(me + step, count)
        return pltpu.make_async_remote_copy(
            src_ref=pot_ref.at[peer, piece],
            dst_ref=land.at[piece, me],
            send_sem=send_sem.at[piece],
            recv_sem=recv_sem.at[piece],
            device_id=place(peer),
            device_id_type=pl.DeviceIdType.MESH,
        )

    def own(piece):
        return pltpu.make_async_copy(pot_ref.at[me, piece], land.at[piece, me], own_sem.at[piece])

    def send_piece(piece, carry):
        def body(step, inner):
            copy(piece, step).start()
            return inner

        own(piece).start()
        return lax.fori_loop(1, count, body, carry)

    lax.fori_loop(0, pieces, send_piece, 0)
    total[...] = jnp.zeros_like(total)

    def work(piece, carry):
        own(piece).wait()
        others = land.at[piece, pl.ds(0, count - 1)]
        pltpu.make_async_copy(others, others, recv_sem.at[piece]).wait()
        wide[...] = land[piece].astype(f32).reshape(cols * PIECE, LANES)
        for half in range(per_piece):
            block = piece * per_piece + half
            slot = lax.rem(block, RING)
            fetch(block).wait()
            lines = [
                wide[pl.ds(half * strips + j, cols, stride=PIECE), :].astype(bf)
                for j in range(strips)
            ]
            total[...] += lax.dot_general(
                jnp.concatenate(lines, axis=1), ring[slot], NT, preferred_element_type=f32
            )

            @pl.when(block + RING < blocks)
            def _():
                fetch(block + RING).start()

        return carry

    lax.fori_loop(0, pieces, work, 0)

    scale = f32(1.0 / math.sqrt(float(NG**3)))
    low_lane = lax.broadcasted_iota(jnp.int32, (cols // 2, LANES), 1) < share
    for k in range(npoints // LANES):
        tile = total[:, k * LANES : (k + 1) * LANES] * scale
        top, low = tile[: cols // 2], tile[cols // 2 :]
        parts[2 * k] = jnp.where(low_lane, top, pltpu.roll(low, share, 1))
        parts[2 * k + 1] = jnp.where(low_lane, pltpu.roll(top, share, 1), low)

    def part_copy(step, source, slot):
        peer = lax.rem(me + step, count)
        return pltpu.make_async_remote_copy(
            src_ref=parts.at[source],
            dst_ref=held.at[slot],
            send_sem=part_send.at[step],
            recv_sem=part_recv.at[step],
            device_id=place(peer),
            device_id_type=pl.DeviceIdType.MESH,
        )

    def part_start(step, carry):
        part_copy(step, lax.rem(me + step, count), me).start()
        return carry

    lax.fori_loop(1, count, part_start, 0)
    held[me] = parts[me]

    def drain_piece(piece, carry):
        sent = pot_ref.at[pl.ds(0, count - 1), piece]
        pltpu.make_async_copy(sent, sent, send_sem.at[piece]).wait()
        return carry

    lax.fori_loop(0, pieces, drain_piece, 0)

    def part_receive(step, carry):
        source = lax.rem(me + count - step, count)
        part_copy(step, source, source).wait_recv()
        return carry

    lax.fori_loop(1, count, part_receive, 0)
    summed = jnp.sum(held[...], axis=0)
    both = jnp.concatenate([summed, pltpu.roll(summed, share, 1)], axis=0)
    o_ref[...] = both.T[:share, :]

    def part_drain(step, carry):
        part_copy(step, lax.rem(me + step, count), me).wait_send()
        return carry

    lax.fori_loop(1, count, part_drain, 0)


def send_and_project(potential, pair):
    bf = jnp.bfloat16
    f32 = jnp.float32
    count, pieces = potential.shape[:2]
    blocks, npoints, span = pair.shape
    cols = count
    share = npoints // count
    return pl.pallas_call(
        project_kernel,
        out_shape=jax.ShapeDtypeStruct((share, cols), f32),
        in_specs=[pl.BlockSpec(memory_space=pltpu.VMEM), pl.BlockSpec(memory_space=pl.ANY)],
        out_specs=pl.BlockSpec(memory_space=pltpu.VMEM),
        scratch_shapes=[
            pltpu.VMEM((RING, npoints, span), bf),
            pltpu.VMEM((pieces, count, PIECE, LANES), bf),
            pltpu.VMEM((cols * PIECE, LANES), f32),
            pltpu.VMEM((cols, npoints), f32),
            pltpu.VMEM((count, cols // 2, LANES), f32),
            pltpu.VMEM((count, cols // 2, LANES), f32),
            pltpu.SemaphoreType.DMA((pieces,)),
            pltpu.SemaphoreType.DMA((pieces,)),
            pltpu.SemaphoreType.DMA((pieces,)),
            pltpu.SemaphoreType.DMA((RING,)),
            pltpu.SemaphoreType.DMA((count,)),
            pltpu.SemaphoreType.DMA((count,)),
        ],
        compiler_params=pltpu.CompilerParams(
            collective_id=2, has_side_effects=True, vmem_limit_bytes=54 << 20
        ),
        name="send_project",
    )(potential, pair)


def fits_planes(rows, npoints, cols, count):
    blocks = rows // SPAN
    return (
        cols == count
        and rows % (NG * NG) == 0
        and NG % (rows // (NG * NG)) == 0
        and blocks >= max(RING, 3)
        and npoints % TAKE == 0
        and 2 * npoints == count * LANES
    )


def shards(orbitals, inverse_panel, points):
    bf = jnp.bfloat16
    row_count = orbitals.shape[0]
    grid_count = lax.axis_size("grid")
    vec_count = lax.axis_size("vec")
    npoints = points.shape[0]
    offset = (lax.axis_index("grid") * vec_count + lax.axis_index("vec")) * row_count
    local_pos = points - offset
    inside = (local_pos >= 0) & (local_pos < row_count)
    picked = jnp.take(orbitals, jnp.clip(local_pos, 0, row_count - 1), axis=0)
    picked = jnp.where(inside[:, None], picked, jnp.zeros_like(picked))
    point_rows = share_rows(picked, grid_count, vec_count)

    if fits_planes(row_count, npoints, inverse_panel.shape[1], grid_count * vec_count):
        pair, field = pair_and_fit(orbitals, point_rows, inverse_panel.T)
        return send_and_project(solve_field(field, grid_count * vec_count), pair)

    def pair_block(block):
        correlation = lax.dot_general(
            block, point_rows, (((1,), (1,)), ((), ())), preferred_element_type=jnp.float32
        )
        return (correlation * correlation).astype(bf)

    pair = lax.map(pair_block, orbitals.reshape(4, row_count // 4, orbitals.shape[1])).reshape(
        row_count, npoints
    )
    fit_cols = lax.dot_general(
        inverse_panel, pair, (((0,), (1,)), ((), ())), preferred_element_type=jnp.float32
    ).astype(bf)
    slab = lax.all_to_all(fit_cols, "vec", split_axis=0, concat_axis=1, tiled=True)
    col_local = slab.shape[0]
    planes = NG // grid_count
    field = slab.reshape(col_local, planes, NG, NG)
    cos_tab, sin_tab = wave_tables(NG)
    z_re = mult(field, cos_tab, "vxyz,zk->vxyk").astype(bf)
    z_im = (-mult(field, sin_tab, "vxyz,zk->vxyk")).astype(bf)
    y_re = (mult(z_re, cos_tab, "vxyz,yk->vxkz") + mult(z_im, sin_tab, "vxyz,yk->vxkz")).astype(bf)
    y_im = (mult(z_im, cos_tab, "vxyz,yk->vxkz") - mult(z_re, sin_tab, "vxyz,yk->vxkz")).astype(bf)
    stacked = jnp.stack([y_re, y_im])
    waves = wavenumber(lax.iota(jnp.int32, NG), NG)
    y_waves = wavenumber(lax.axis_index("grid") * planes + lax.iota(jnp.int32, planes), NG)
    kernel = screened(waves, y_waves, waves)[None]
    piece = lax.all_to_all(stacked, "grid", split_axis=3, concat_axis=2, tiled=True)
    p_re = piece[0]
    p_im = piece[1]
    x_re = mult(p_re, cos_tab, "vxyz,xk->vkyz") + mult(p_im, sin_tab, "vxyz,xk->vkyz")
    x_im = mult(p_im, cos_tab, "vxyz,xk->vkyz") - mult(p_re, sin_tab, "vxyz,xk->vkyz")
    q_re = (x_re * kernel).astype(bf)
    q_im = (x_im * kernel).astype(bf)
    i_re = (mult(q_re, cos_tab, "vxyz,xk->vkyz") - mult(q_im, sin_tab, "vxyz,xk->vkyz")).astype(bf)
    i_im = (mult(q_im, cos_tab, "vxyz,xk->vkyz") + mult(q_re, sin_tab, "vxyz,xk->vkyz")).astype(bf)
    spectrum = lax.all_to_all(
        jnp.stack([i_re, i_im]), "grid", split_axis=2, concat_axis=3, tiled=True
    )
    s_re = spectrum[0]
    s_im = spectrum[1]
    h_re = (mult(s_re, cos_tab, "vxyz,yk->vxkz") - mult(s_im, sin_tab, "vxyz,yk->vxkz")).astype(bf)
    h_im = (mult(s_im, cos_tab, "vxyz,yk->vxkz") + mult(s_re, sin_tab, "vxyz,yk->vxkz")).astype(bf)
    final = mult(h_re, cos_tab, "vxyz,zk->vxyk") - mult(h_im, sin_tab, "vxyz,zk->vxyk")
    potential = (final / float(NG**3)).astype(bf).reshape(col_local, planes * NG * NG)
    pot_rows = lax.all_to_all(potential, "vec", split_axis=1, concat_axis=0, tiled=True)
    return project(pair, pot_rows)


def solution(mesh):
    in_specs = (P(("grid", "vec"), None), P(), P())
    out_specs = P(("grid", "vec"), None)
    return jax.shard_map(shards, mesh=mesh, in_specs=in_specs, out_specs=out_specs, check_vma=False)
```

```python
import math

import jax
import jax.numpy as jnp
from jax import lax
from jax.experimental import pallas as pl
from jax.experimental.pallas import tpu as pltpu
from jax.sharding import PartitionSpec as P

NG = 96


SCREEN = 2.25


def wave_tables(count):
    index = lax.iota(jnp.int32, count)
    phase = index[:, None] * index[None, :] % count
    angle = phase.astype(jnp.float32) * (2.0 * math.pi / count)
    return (jnp.cos(angle).astype(jnp.bfloat16), jnp.sin(angle).astype(jnp.bfloat16))


def wavenumber(index, count):
    return jnp.where(index < count // 2, index, index - count).astype(jnp.float32)


def screened(wave_x, wave_y, wave_z):
    squared = (
        wave_x[:, None, None] * wave_x[:, None, None]
        + wave_y[None, :, None] * wave_y[None, :, None]
        + wave_z[None, None, :] * wave_z[None, None, :]
    )
    factor = NG / (2.0 * math.pi) * (NG / (2.0 * math.pi))
    return jnp.where(squared > 0.5, factor / (squared + SCREEN), jnp.float32(0.0))


def mult(data, table, form):
    return jnp.einsum(form, data, table, preferred_element_type=jnp.float32)


LANES = 128


def exchange_kernel(axes, total, gather, x_ref, o_ref, held, send_sem, recv_sem, own_sem):
    if len(axes) == 2:
        vec_count = lax.axis_size("vec")
        count = lax.axis_size("grid") * vec_count
        me = lax.axis_index("grid") * vec_count + lax.axis_index("vec")
    else:
        count = lax.axis_size(axes[0])
        me = lax.axis_index(axes[0])
    land = held if total else o_ref

    def place(index):
        if len(axes) == 2:
            return (index // vec_count, lax.rem(index, vec_count))
        if axes[0] == "grid":
            return (index, lax.axis_index("vec"))
        return (lax.axis_index("grid"), index)

    def part(index):
        return x_ref if gather else x_ref.at[index]

    barrier = pltpu.get_barrier_semaphore()

    def greet(step, carry):
        pl.semaphore_signal(
            barrier,
            inc=1,
            device_id=place(lax.rem(me + step, count)),
            device_id_type=pl.DeviceIdType.MESH,
        )
        return carry

    lax.fori_loop(1, count, greet, 0)
    own = pltpu.make_async_copy(part(me), land.at[me], own_sem)
    own.start()
    pl.semaphore_wait(barrier, count - 1)

    def copy(step, source, slot):
        peer = lax.rem(me + step, count)
        return pltpu.make_async_remote_copy(
            src_ref=part(source),
            dst_ref=land.at[slot],
            send_sem=send_sem.at[step],
            recv_sem=recv_sem.at[step],
            device_id=place(peer),
            device_id_type=pl.DeviceIdType.MESH,
        )

    def send(step, carry):
        copy(step, lax.rem(me + step, count), me).start()
        return carry

    lax.fori_loop(1, count, send, 0)
    own.wait()

    def receive(step, carry):
        source = lax.rem(me + count - step, count)
        copy(step, source, source).wait_recv()
        return carry

    lax.fori_loop(1, count, receive, 0)
    if total:
        o_ref[...] = jnp.sum(held[...].astype(jnp.float32), axis=0).astype(o_ref.dtype)

    def drain(step, carry):
        copy(step, lax.rem(me + step, count), me).wait_send()
        return carry

    lax.fori_loop(1, count, drain, 0)


def exchange(blocks, ident, total=False, axes=("grid", "vec"), gather=False):
    rows, lanes = blocks.shape[-2:]
    count = 1
    for axis in axes:
        count *= lax.axis_size(axis)
    shape = (rows, lanes) if total else (count, rows, lanes)
    held_shape = blocks.shape if total else (1, 8, LANES)

    def body(*refs):
        exchange_kernel(axes, total, gather, *refs)

    return pl.pallas_call(
        body,
        out_shape=jax.ShapeDtypeStruct(shape, blocks.dtype),
        in_specs=[pl.BlockSpec(memory_space=pltpu.VMEM)],
        out_specs=pl.BlockSpec(memory_space=pltpu.VMEM),
        scratch_shapes=[
            pltpu.VMEM(held_shape, blocks.dtype),
            pltpu.SemaphoreType.DMA((count,)),
            pltpu.SemaphoreType.DMA((count,)),
            pltpu.SemaphoreType.DMA(()),
        ],
        compiler_params=pltpu.CompilerParams(
            collective_id=ident, has_side_effects=True, vmem_limit_bytes=32 << 20
        ),
        name="exchange_total" if total else "exchange_gather" if gather else "exchange_blocks",
    )(blocks)


def share_kernel(chunks, x_ref, o_ref, near, wide, far, sum1, sum2, sum3, sends, recvs, own_sem):
    bf = jnp.bfloat16
    f32 = jnp.float32
    vec_count = lax.axis_size("vec")
    deep = lax.axis_size("grid") // 2
    grid_at, mine = lax.axis_index("grid"), lax.axis_index("vec")
    level, core = grid_at // 2, lax.rem(grid_at, 2)
    other = 1 - core
    across = vec_count - 1

    def partner(step):
        return (level * 2 + other, mine)

    def beside(step):
        return (grid_at, lax.rem(mine + step, vec_count))

    def above(step):
        return (lax.rem(level + step, deep) * 2 + core, mine)

    peers = [partner(1)]
    peers += [beside(step) for step in range(1, vec_count)]
    peers += [above(step) for step in range(1, deep)]
    barrier = pltpu.get_barrier_semaphore()
    for peer in peers:
        pl.semaphore_signal(barrier, inc=1, device_id=peer, device_id_type=pl.DeviceIdType.MESH)
    pl.semaphore_wait(barrier, len(peers))

    def send(source, target, slot, peer):
        return pltpu.make_async_remote_copy(
            src_ref=source,
            dst_ref=target,
            send_sem=sends.at[slot],
            recv_sem=recvs.at[slot],
            device_id=peer,
            device_id_type=pl.DeviceIdType.MESH,
        )

    per_chunk = 2 + 2 * across + 2 * (deep - 1)

    def copies(stage, c):
        base = c * per_chunk
        if stage == 0:
            return [send(x_ref.at[c, other], near.at[c], base, partner(1))]
        if stage == 1:
            return [
                send(
                    sum1.at[c, lax.rem(mine + step, vec_count)],
                    wide.at[c, step - 1],
                    base + step,
                    beside(step),
                )
                for step in range(1, vec_count)
            ]
        if stage == 2:
            return [
                send(
                    sum2.at[c, lax.rem(level + step, deep)],
                    far.at[c, step - 1],
                    base + across + step,
                    above(step),
                )
                for step in range(1, deep)
            ]
        base += across + deep
        if stage == 3:
            spot = o_ref.at[c, core, mine, level]
            return [send(sum3.at[c], spot, base + step - 1, above(step)) for step in range(1, deep)]
        base += deep - 1
        if stage == 4:
            spot = o_ref.at[c, core, mine]
            return [send(spot, spot, base + step - 1, beside(step)) for step in range(1, vec_count)]
        spot = o_ref.at[c, core]
        return [send(spot, spot, base + across, partner(1))]

    def own(c):
        return pltpu.make_async_copy(sum3.at[c], o_ref.at[c, core, mine, level], own_sem.at[c])

    def prepare(stage, c):
        for move in copies(stage - 1, c):
            move.wait_recv()
        if stage == 1:
            sum1[c] = (x_ref[c, core].astype(f32) + near[c].astype(f32)).astype(bf)
        if stage == 2:
            total = sum1[c, mine].astype(f32)
            for step in range(across):
                total += wide[c, step].astype(f32)
            sum2[c] = total.astype(bf)
        if stage == 3:
            total = sum2[c, level].astype(f32)
            for step in range(deep - 1):
                total += far[c, step].astype(f32)
            sum3[c] = total.astype(bf)
            own(c).start()
        if stage == 4:
            own(c).wait()

    for tick in range(chunks + 6):
        for stage in range(6, -1, -1):
            c = tick - stage
            if 0 <= c < chunks:
                if stage > 0:
                    prepare(stage, c)
                if stage < 6:
                    for move in copies(stage, c):
                        move.start()
    for c in range(chunks):
        for stage in range(6):
            for move in copies(stage, c):
                move.wait_send()


ROWS = 16


def share_rows(picked, grid_count, vec_count):
    bf = jnp.bfloat16
    npoints, norb = picked.shape
    count = grid_count * vec_count
    if npoints % (count * ROWS) != 0 or grid_count % 2 != 0:
        return lax.psum(picked.astype(jnp.float32), ("grid", "vec")).astype(picked.dtype)
    chunks = npoints // (count * ROWS)
    deep = grid_count // 2
    shape = (chunks, 2, vec_count, deep, ROWS, norb)
    slots = chunks * (2 + 2 * (vec_count - 1) + 2 * (deep - 1))

    def body(*refs):
        share_kernel(chunks, *refs)

    return pl.pallas_call(
        body,
        out_shape=jax.ShapeDtypeStruct(shape, bf),
        in_specs=[pl.BlockSpec(memory_space=pltpu.VMEM)],
        out_specs=pl.BlockSpec(memory_space=pltpu.VMEM),
        scratch_shapes=[
            pltpu.VMEM((chunks, vec_count, deep, ROWS, norb), bf),
            pltpu.VMEM((chunks, vec_count - 1, deep, ROWS, norb), bf),
            pltpu.VMEM((chunks, deep - 1, ROWS, norb), bf),
            pltpu.VMEM((chunks, vec_count, deep, ROWS, norb), bf),
            pltpu.VMEM((chunks, deep, ROWS, norb), bf),
            pltpu.VMEM((chunks, ROWS, norb), bf),
            pltpu.SemaphoreType.DMA((slots,)),
            pltpu.SemaphoreType.DMA((slots,)),
            pltpu.SemaphoreType.DMA((chunks,)),
        ],
        compiler_params=pltpu.CompilerParams(
            collective_id=4, has_side_effects=True, vmem_limit_bytes=32 << 20
        ),
        name="share_rows",
    )(picked.reshape(shape)).reshape(npoints, norb)


OCTET = 8


def pick_kernel(points_ref, flags_ref, offset_ref, orb_ref, o_ref, found, where, spare, sheet, sem):
    octets, _, norb = orb_ref.shape
    limit = octets * OCTET
    npoints = o_ref.shape[0]
    offset = offset_ref[0]
    sheet[...] = jnp.zeros_like(sheet)

    def fetch(slot, octet):
        return pltpu.make_async_copy(orb_ref.at[octet], found.at[slot], sem)

    def look(i, held):
        position = points_ref[i] - offset
        inside = (position >= 0) & (position < limit)

        @pl.when(inside)
        def _():
            fetch(held, position // OCTET).start()
            where[held] = i
            spare[held] = lax.rem(position, OCTET)

        return held + inside.astype(jnp.int32)

    def scan(group, held):
        return lax.cond(
            flags_ref[group] > 0,
            lambda h: lax.fori_loop(0, OCTET, lambda k, n: look(group * OCTET + k, n), h),
            lambda h: h,
            held,
        )

    held = lax.fori_loop(0, npoints // OCTET, scan, 0)

    def settle(slot, carry):
        fetch(slot, 0).wait()
        return carry

    lax.fori_loop(0, held, settle, 0)
    line = lax.broadcasted_iota(jnp.int32, (OCTET, norb), 0)

    def place(slot, carry):
        octet = found[slot].astype(jnp.float32)
        row = jnp.sum(jnp.where(line == spare[slot], octet, 0.0), axis=0, keepdims=True)
        sheet[pl.ds(where[slot], 1), :] = row
        return carry

    lax.fori_loop(0, held, place, 0)
    o_ref[...] = sheet[...].astype(o_ref.dtype)


def pick_rows(orbitals, points, offset):
    rows, norb = orbitals.shape
    npoints = points.shape[0]
    position = points - offset
    if rows % OCTET != 0 or npoints % OCTET != 0:
        inside = (position >= 0) & (position < rows)
        picked = jnp.take(orbitals, jnp.clip(position, 0, rows - 1), axis=0)
        return jnp.where(inside[:, None], picked, jnp.zeros_like(picked))
    inside = (position >= 0) & (position < rows)
    flags = jnp.max(inside.reshape(-1, OCTET).astype(jnp.int32), axis=1)
    return pl.pallas_call(
        pick_kernel,
        out_shape=jax.ShapeDtypeStruct((npoints, norb), orbitals.dtype),
        in_specs=[
            pl.BlockSpec(memory_space=pltpu.SMEM),
            pl.BlockSpec(memory_space=pltpu.SMEM),
            pl.BlockSpec(memory_space=pltpu.SMEM),
            pl.BlockSpec(memory_space=pl.ANY),
        ],
        out_specs=pl.BlockSpec(memory_space=pltpu.VMEM),
        scratch_shapes=[
            pltpu.VMEM((npoints, OCTET, norb), orbitals.dtype),
            pltpu.SMEM((npoints,), jnp.int32),
            pltpu.SMEM((npoints,), jnp.int32),
            pltpu.VMEM((npoints, norb), jnp.float32),
            pltpu.SemaphoreType.DMA(()),
        ],
        compiler_params=pltpu.CompilerParams(vmem_limit_bytes=40 << 20),
        name="pick_rows",
    )(points, flags, offset[None].astype(jnp.int32), orbitals.reshape(rows // OCTET, OCTET, norb))


def project(pair, pot_rows):
    scale = 1.0 / math.sqrt(float(NG**3))
    term = lax.dot_general(
        pair, pot_rows, (((0,), (1,)), ((), ())), preferred_element_type=jnp.float32
    )
    term = term * jnp.float32(scale)
    npoints, cols = term.shape
    count = lax.axis_size("grid") * lax.axis_size("vec")
    share = npoints // count
    if share * cols % LANES == 0:
        blocks = term.reshape(count, share * cols // LANES, LANES)
        return exchange(blocks, 3, True).reshape(share, cols)
    partial_block = lax.psum_scatter(term, "grid", scatter_dimension=0, tiled=True)
    return lax.psum_scatter(partial_block, "vec", scatter_dimension=0, tiled=True)


def peers_of():
    vec_count = lax.axis_size("vec")
    count = lax.axis_size("grid") * vec_count
    me = lax.axis_index("grid") * vec_count + lax.axis_index("vec")

    def place(index):
        return (index // vec_count, lax.rem(index, vec_count))

    return count, me, place


def greet_all(count, me, place):
    barrier = pltpu.get_barrier_semaphore()

    def greet(step, carry):
        pl.semaphore_signal(
            barrier,
            inc=1,
            device_id=place(lax.rem(me + step, count)),
            device_id_type=pl.DeviceIdType.MESH,
        )
        return carry

    lax.fori_loop(1, count, greet, 0)


def wait_greeted(count):
    pl.semaphore_wait(pltpu.get_barrier_semaphore(), count - 1)


NT = (((1,), (1,)), ((), ()))
NN = (((1,), (0,)), ((), ()))
LINES = 16
SPAN = LINES * NG
TAKE = 512
JOIN = 3


def pair_fit_kernel(
    orb_ref, rows_ref, panel_ref, pair_ref, field_ref, fit_buf, fit_rows, out_buf,
    send_sem, recv_sem, own_sem,
):
    bf = jnp.bfloat16
    block = pl.program_id(0)
    blocks = pl.num_programs(0)
    count, me, place = peers_of()
    npoints = rows_ref.shape[0]
    cols = panel_ref.shape[0]
    per_plane = NG // LINES
    groups = blocks // JOIN
    tall = JOIN * LINES

    def send(group, begin, lines):
        slot = lax.rem(group, 2)
        start = pl.multiple_of(lax.rem(group * JOIN, per_plane) * LINES + begin, LINES)
        target = field_ref.at[me, group * JOIN // per_plane, pl.ds(start, lines)]

        def body(step, carry):
            peer = lax.rem(me + step, count)
            pltpu.make_async_remote_copy(
                src_ref=out_buf.at[slot, peer, pl.ds(begin, lines)],
                dst_ref=target,
                send_sem=send_sem.at[slot],
                recv_sem=recv_sem.at[me],
                device_id=place(peer),
                device_id_type=pl.DeviceIdType.MESH,
            ).start()
            return carry

        pltpu.make_async_copy(
            out_buf.at[slot, me, pl.ds(begin, lines)], target, own_sem.at[slot]
        ).start()
        lax.fori_loop(1, count, body, 0, unroll=True)

    def drain(group):
        slot = lax.rem(group, 2)
        sent = out_buf.at[slot, pl.ds(0, count - 1)]
        mine = out_buf.at[slot, me]
        pltpu.make_async_copy(mine, mine, own_sem.at[slot]).wait()
        pltpu.make_async_copy(sent, sent, send_sem.at[slot]).wait()

    @pl.when(block == 0)
    def _():
        greet_all(count, me, place)

    @pl.when(block == 1)
    def _():
        wait_greeted(count)

    before = jnp.maximum(block - 1, 0)

    @pl.when((block > 2 * JOIN) & (lax.rem(before, JOIN) == 0))
    def _():
        drain(before // JOIN - 2)

    def multiply(first):
        part = lax.dot_general(
            rows_ref[first : first + TAKE, :], orb_ref[...], NT, preferred_element_type=jnp.float32
        )
        pair_ref[0, first : first + TAKE, :] = (part * part).astype(bf)

    def arrange(index):
        for line in range(LINES):
            begin = line * NG
            low = begin // LANES * LANES
            turn = begin - low
            wide = fit_buf[:, low : min(low + 2 * LANES, SPAN)]
            if wide.shape[1] == LANES:
                wide = jnp.concatenate([wide, wide], axis=1)
            if turn:
                wide = pltpu.roll(wide, 2 * LANES - turn, 1)
            fit_rows[pl.ds(line, cols, stride=LINES), :] = wide[:, :LANES]
        slot = lax.rem(index // JOIN, 2)
        begin = pl.multiple_of(lax.rem(index, JOIN) * LINES, LINES)
        out_buf[slot, :, pl.ds(begin, LINES), :] = (
            fit_rows[...].astype(bf).reshape(cols, LINES, LANES)
        )

    @pl.when(block == 0)
    def _():
        fit_buf[...] = jnp.zeros_like(fit_buf)

    multiply(0)
    arrange(before)
    for first in range(TAKE, npoints // 2, TAKE):
        multiply(first)

    @pl.when((block >= JOIN) & (lax.rem(block, JOIN) == 0))
    def _():
        send(block // JOIN - 1, 0, tall)

    for late in range(JOIN - 1):

        @pl.when(block == blocks - JOIN + 1 + late)
        def _(late=late):
            send(groups - 1, late * LINES, LINES)

    for first in range(npoints // 2, npoints, TAKE):
        multiply(first)
    fit_buf[...] = lax.dot_general(
        panel_ref[...], pair_ref[0], NN, preferred_element_type=jnp.float32
    )

    @pl.when(block == blocks - 1)
    def _():
        arrange(block)
        send(groups - 1, (JOIN - 1) * LINES, LINES)

        def receive(step, carry):
            source = lax.rem(me + count - step, count)
            land = field_ref.at[source]
            pltpu.make_async_copy(land, land, recv_sem.at[source]).wait()
            return carry

        lax.fori_loop(1, count, receive, 0)
        drain(groups - 2)
        drain(groups - 1)


def pair_and_fit(orbitals, point_rows, panel):
    bf = jnp.bfloat16
    rows, norb = orbitals.shape
    npoints = point_rows.shape[0]
    cols = panel.shape[0]
    blocks = rows // SPAN
    planes = rows // (NG * NG)
    count = lax.axis_size("grid") * lax.axis_size("vec")
    return pl.pallas_call(
        pair_fit_kernel,
        grid=(blocks,),
        in_specs=[
            pl.BlockSpec((SPAN, norb), lambda i: (i, 0)),
            pl.BlockSpec((npoints, norb), lambda i: (0, 0)),
            pl.BlockSpec((cols, npoints), lambda i: (0, 0)),
        ],
        out_specs=[
            pl.BlockSpec((1, npoints, SPAN), lambda i: (i, 0, 0)),
            pl.BlockSpec(memory_space=pl.ANY),
        ],
        out_shape=[
            jax.ShapeDtypeStruct((blocks, npoints, SPAN), bf),
            jax.ShapeDtypeStruct((count, planes, NG, LANES), bf),
        ],
        scratch_shapes=[
            pltpu.VMEM((cols, SPAN), jnp.float32),
            pltpu.VMEM((cols * LINES, LANES), jnp.float32),
            pltpu.VMEM((2, cols, JOIN * LINES, LANES), bf),
            pltpu.SemaphoreType.DMA((2,)),
            pltpu.SemaphoreType.DMA((count,)),
            pltpu.SemaphoreType.DMA((2,)),
        ],
        compiler_params=pltpu.CompilerParams(
            collective_id=1, has_side_effects=True, vmem_limit_bytes=50 << 20
        ),
        name="pair_fit_send",
    )(orbitals, point_rows, panel)


GROUP = 8
HALF = 64
PIECE = NG * NG // LANES // 3


def solve_kernel(field_ref, tz_ref, ty_ref, tyi_ref, tzi_ref, out_ref, by_y, by_x, flat, dense):
    bf = jnp.bfloat16
    f32 = jnp.float32
    lane = lax.broadcasted_iota(jnp.int32, (NG, LANES), 1)
    row = lax.broadcasted_iota(jnp.int32, (NG, LANES), 0)
    sign = jnp.where(lane < HALF, 1.0, -1.0).astype(f32)
    wave_z = lax.rem(lane, HALF).astype(f32)
    wave_x = jnp.where(row < NG // 2, row, row - NG).astype(f32)
    plane_sq = wave_x * wave_x + wave_z * wave_z
    factor = NG / (2.0 * math.pi) * (NG / (2.0 * math.pi))

    def both(parts):
        top = jnp.concatenate([part.astype(bf) for part in parts], axis=1)
        turned = [(pltpu.roll(part, HALF, 1) * sign).astype(bf) for part in parts]
        return jnp.concatenate([top, jnp.concatenate(turned, axis=1)], axis=0)

    def cut(wide, k):
        return wide[:, k * LANES : (k + 1) * LANES]

    def forward(step, carry):
        first = step * GROUP
        data = field_ref[pl.ds(first, GROUP)].reshape(GROUP * NG, LANES)
        a = lax.dot_general(data, tz_ref[...], NN, preferred_element_type=f32).astype(bf)
        top = [a[k * NG : (k + 1) * NG, :LANES] for k in range(GROUP)]
        low = [a[k * NG : (k + 1) * NG, LANES:] for k in range(GROUP)]
        stack = jnp.concatenate(
            [jnp.concatenate(top, axis=1), jnp.concatenate(low, axis=1)], axis=0
        )
        b = lax.dot_general(ty_ref[...], stack, NN, preferred_element_type=f32)
        for k in range(GROUP):
            by_y[pl.ds(first + k, NG, stride=NG), :] = cut(b, k)
        return carry

    lax.fori_loop(0, NG // GROUP, forward, 0)

    def middle(step, carry):
        first = step * GROUP
        parts = [by_y[pl.ds((first + k) * NG, NG), :] for k in range(GROUP)]
        h = lax.dot_general(ty_ref[...], both(parts), NN, preferred_element_type=f32)
        scaled = []
        for k in range(GROUP):
            index = first + k
            wave_y = jnp.where(index < NG // 2, index, index - NG).astype(f32)
            squared = plane_sq + wave_y * wave_y
            kernel = jnp.where(squared > 0.5, factor / (squared + SCREEN), 0.0)
            scaled.append(cut(h, k) * kernel)
        g = lax.dot_general(tyi_ref[...], both(scaled), NN, preferred_element_type=f32)
        for k in range(GROUP):
            by_x[pl.ds(first + k, NG, stride=NG), :] = cut(g, k)
        return carry

    lax.fori_loop(0, NG // GROUP, middle, 0)

    planes = NG // out_ref.shape[0]
    quarter = NG // 4

    def backward(step, carry):
        first = step * GROUP
        parts = [by_x[pl.ds((first + k) * NG, NG), :] for k in range(GROUP)]
        p = lax.dot_general(tyi_ref[...], both(parts), NN, preferred_element_type=f32).astype(bf)
        rows = jnp.concatenate([cut(p, k) for k in range(GROUP)], axis=0)
        final = lax.dot_general(rows, tzi_ref[...], NN, preferred_element_type=f32)
        flat[...] = final * f32(1.0 / float(NG**3))
        for k in range(GROUP):
            y0, y1, y2, y3 = [
                flat[pl.ds(k * NG + j, quarter, stride=4), :] for j in range(4)
            ]
            spot = lane[:quarter]
            dense[pl.ds(0, quarter, stride=3), :] = jnp.where(
                spot < 96, y0, pltpu.roll(y1, 96, 1)
            )
            dense[pl.ds(1, quarter, stride=3), :] = jnp.where(
                spot < 64, pltpu.roll(y1, 96, 1), pltpu.roll(y2, 64, 1)
            )
            dense[pl.ds(2, quarter, stride=3), :] = jnp.where(
                spot < 32, pltpu.roll(y2, 64, 1), pltpu.roll(y3, 32, 1)
            )
            index = first + k
            for m in range(3):
                out_ref[index // planes, lax.rem(index, planes) * 3 + m] = dense[
                    m * PIECE : (m + 1) * PIECE, :
                ].astype(bf)
        return carry

    lax.fori_loop(0, NG // GROUP, backward, 0)


def solve_field(field, count):
    bf = jnp.bfloat16
    f32 = jnp.float32
    cos_tab, sin_tab = wave_tables(NG)
    keep = NG // 2 + 1

    def wide(table):
        return jnp.pad(table[:, :keep], ((0, LANES - NG), (0, HALF - keep)))

    cz, sz = wide(cos_tab), wide(sin_tab)
    tz = jnp.concatenate([cz, -sz, -sz, -cz], axis=1)
    ty = jnp.concatenate([cos_tab, sin_tab], axis=1)
    tyi = jnp.concatenate([cos_tab, -sin_tab], axis=1)
    spot = lax.iota(jnp.int32, HALF)[:, None]
    weight = jnp.where((spot == 0) | (spot == NG // 2), 1.0, 2.0).astype(bf)
    tzi = jnp.concatenate([cz.T * weight, -(sz.T * weight)], axis=0)
    pieces = NG // count * 3
    return pl.pallas_call(
        solve_kernel,
        out_shape=jax.ShapeDtypeStruct((count, pieces, PIECE, LANES), bf),
        in_specs=[pl.BlockSpec(memory_space=pltpu.VMEM)] * 5,
        out_specs=pl.BlockSpec(memory_space=pltpu.VMEM),
        scratch_shapes=[
            pltpu.VMEM((NG * NG, LANES), f32),
            pltpu.VMEM((NG * NG, LANES), f32),
            pltpu.VMEM((GROUP * NG, LANES), f32),
            pltpu.VMEM((3 * PIECE, LANES), f32),
        ],
        compiler_params=pltpu.CompilerParams(vmem_limit_bytes=40 << 20),
        name="solve_field",
    )(field.reshape(NG, NG, LANES), tz, ty, tyi, tzi)


RING = 6


def project_kernel(
    pot_ref, pair_ref, o_ref, ring, land, wide, total, parts, held,
    send_sem, recv_sem, own_sem, pair_sem, part_send, part_recv,
):
    bf = jnp.bfloat16
    f32 = jnp.float32
    count, me, place = peers_of()
    blocks, npoints, _ = pair_ref.shape
    pieces = pot_ref.shape[1]
    cols = count
    share = npoints // count
    per_piece = blocks // pieces
    strips = SPAN // LANES

    def fetch(block):
        slot = lax.rem(block, RING)
        return pltpu.make_async_copy(pair_ref.at[block], ring.at[slot], pair_sem.at[slot])

    def prime(block, carry):
        fetch(block).start()
        return carry

    greet_all(count, me, place)
    lax.fori_loop(0, RING, prime, 0)
    wait_greeted(count)

    def copy(piece, step):
        peer = lax.rem(me + step, count)
        return pltpu.make_async_remote_copy(
            src_ref=pot_ref.at[peer, piece],
            dst_ref=land.at[piece, me],
            send_sem=send_sem.at[piece],
            recv_sem=recv_sem.at[piece],
            device_id=place(peer),
            device_id_type=pl.DeviceIdType.MESH,
        )

    def own(piece):
        return pltpu.make_async_copy(pot_ref.at[me, piece], land.at[piece, me], own_sem.at[piece])

    def send_piece(piece, carry):
        def body(step, inner):
            copy(piece, step).start()
            return inner

        own(piece).start()
        return lax.fori_loop(1, count, body, carry)

    lax.fori_loop(0, pieces, send_piece, 0)
    total[...] = jnp.zeros_like(total)

    def work(piece, carry):
        own(piece).wait()
        others = land.at[piece, pl.ds(0, count - 1)]
        pltpu.make_async_copy(others, others, recv_sem.at[piece]).wait()
        wide[...] = land[piece].astype(f32).reshape(cols * PIECE, LANES)
        for half in range(per_piece):
            block = piece * per_piece + half
            slot = lax.rem(block, RING)
            fetch(block).wait()
            lines = [
                wide[pl.ds(half * strips + j, cols, stride=PIECE), :].astype(bf)
                for j in range(strips)
            ]
            total[...] += lax.dot_general(
                jnp.concatenate(lines, axis=1), ring[slot], NT, preferred_element_type=f32
            )

            @pl.when(block + RING < blocks)
            def _():
                fetch(block + RING).start()

        return carry

    lax.fori_loop(0, pieces, work, 0)

    scale = f32(1.0 / math.sqrt(float(NG**3)))
    low_lane = lax.broadcasted_iota(jnp.int32, (cols // 2, LANES), 1) < share
    for k in range(npoints // LANES):
        tile = total[:, k * LANES : (k + 1) * LANES] * scale
        top, low = tile[: cols // 2], tile[cols // 2 :]
        parts[2 * k] = jnp.where(low_lane, top, pltpu.roll(low, share, 1))
        parts[2 * k + 1] = jnp.where(low_lane, pltpu.roll(top, share, 1), low)

    def part_copy(step, source, slot):
        peer = lax.rem(me + step, count)
        return pltpu.make_async_remote_copy(
            src_ref=parts.at[source],
            dst_ref=held.at[slot],
            send_sem=part_send.at[step],
            recv_sem=part_recv.at[step],
            device_id=place(peer),
            device_id_type=pl.DeviceIdType.MESH,
        )

    def part_start(step, carry):
        part_copy(step, lax.rem(me + step, count), me).start()
        return carry

    lax.fori_loop(1, count, part_start, 0)
    held[me] = parts[me]

    def drain_piece(piece, carry):
        sent = pot_ref.at[pl.ds(0, count - 1), piece]
        pltpu.make_async_copy(sent, sent, send_sem.at[piece]).wait()
        return carry

    lax.fori_loop(0, pieces, drain_piece, 0)

    def part_receive(step, carry):
        source = lax.rem(me + count - step, count)
        part_copy(step, source, source).wait_recv()
        return carry

    lax.fori_loop(1, count, part_receive, 0)
    summed = jnp.sum(held[...], axis=0)
    both = jnp.concatenate([summed, pltpu.roll(summed, share, 1)], axis=0)
    o_ref[...] = both.T[:share, :]

    def part_drain(step, carry):
        part_copy(step, lax.rem(me + step, count), me).wait_send()
        return carry

    lax.fori_loop(1, count, part_drain, 0)


def send_and_project(potential, pair):
    bf = jnp.bfloat16
    f32 = jnp.float32
    count, pieces = potential.shape[:2]
    blocks, npoints, span = pair.shape
    cols = count
    share = npoints // count
    return pl.pallas_call(
        project_kernel,
        out_shape=jax.ShapeDtypeStruct((share, cols), f32),
        in_specs=[pl.BlockSpec(memory_space=pltpu.VMEM), pl.BlockSpec(memory_space=pl.ANY)],
        out_specs=pl.BlockSpec(memory_space=pltpu.VMEM),
        scratch_shapes=[
            pltpu.VMEM((RING, npoints, span), bf),
            pltpu.VMEM((pieces, count, PIECE, LANES), bf),
            pltpu.VMEM((cols * PIECE, LANES), f32),
            pltpu.VMEM((cols, npoints), f32),
            pltpu.VMEM((count, cols // 2, LANES), f32),
            pltpu.VMEM((count, cols // 2, LANES), f32),
            pltpu.SemaphoreType.DMA((pieces,)),
            pltpu.SemaphoreType.DMA((pieces,)),
            pltpu.SemaphoreType.DMA((pieces,)),
            pltpu.SemaphoreType.DMA((RING,)),
            pltpu.SemaphoreType.DMA((count,)),
            pltpu.SemaphoreType.DMA((count,)),
        ],
        compiler_params=pltpu.CompilerParams(
            collective_id=2, has_side_effects=True, vmem_limit_bytes=54 << 20
        ),
        name="send_project",
    )(potential, pair)


def fits_planes(rows, npoints, cols, count):
    blocks = rows // SPAN
    return (
        cols == count
        and rows % (NG * NG) == 0
        and NG % (rows // (NG * NG)) == 0
        and blocks >= max(RING, 2 * JOIN)
        and NG // LINES % JOIN == 0
        and npoints % TAKE == 0
        and 2 * npoints == count * LANES
    )


def shards(orbitals, inverse_panel, points):
    bf = jnp.bfloat16
    row_count = orbitals.shape[0]
    grid_count = lax.axis_size("grid")
    vec_count = lax.axis_size("vec")
    npoints = points.shape[0]
    offset = (lax.axis_index("grid") * vec_count + lax.axis_index("vec")) * row_count
    picked = pick_rows(orbitals, points, offset)
    point_rows = share_rows(picked, grid_count, vec_count)

    if fits_planes(row_count, npoints, inverse_panel.shape[1], grid_count * vec_count):
        pair, field = pair_and_fit(orbitals, point_rows, inverse_panel.T)
        return send_and_project(solve_field(field, grid_count * vec_count), pair)

    def pair_block(block):
        correlation = lax.dot_general(
            block, point_rows, (((1,), (1,)), ((), ())), preferred_element_type=jnp.float32
        )
        return (correlation * correlation).astype(bf)

    pair = lax.map(pair_block, orbitals.reshape(4, row_count // 4, orbitals.shape[1])).reshape(
        row_count, npoints
    )
    fit_cols = lax.dot_general(
        inverse_panel, pair, (((0,), (1,)), ((), ())), preferred_element_type=jnp.float32
    ).astype(bf)
    slab = lax.all_to_all(fit_cols, "vec", split_axis=0, concat_axis=1, tiled=True)
    col_local = slab.shape[0]
    planes = NG // grid_count
    field = slab.reshape(col_local, planes, NG, NG)
    cos_tab, sin_tab = wave_tables(NG)
    z_re = mult(field, cos_tab, "vxyz,zk->vxyk").astype(bf)
    z_im = (-mult(field, sin_tab, "vxyz,zk->vxyk")).astype(bf)
    y_re = (mult(z_re, cos_tab, "vxyz,yk->vxkz") + mult(z_im, sin_tab, "vxyz,yk->vxkz")).astype(bf)
    y_im = (mult(z_im, cos_tab, "vxyz,yk->vxkz") - mult(z_re, sin_tab, "vxyz,yk->vxkz")).astype(bf)
    stacked = jnp.stack([y_re, y_im])
    waves = wavenumber(lax.iota(jnp.int32, NG), NG)
    y_waves = wavenumber(lax.axis_index("grid") * planes + lax.iota(jnp.int32, planes), NG)
    kernel = screened(waves, y_waves, waves)[None]
    piece = lax.all_to_all(stacked, "grid", split_axis=3, concat_axis=2, tiled=True)
    p_re = piece[0]
    p_im = piece[1]
    x_re = mult(p_re, cos_tab, "vxyz,xk->vkyz") + mult(p_im, sin_tab, "vxyz,xk->vkyz")
    x_im = mult(p_im, cos_tab, "vxyz,xk->vkyz") - mult(p_re, sin_tab, "vxyz,xk->vkyz")
    q_re = (x_re * kernel).astype(bf)
    q_im = (x_im * kernel).astype(bf)
    i_re = (mult(q_re, cos_tab, "vxyz,xk->vkyz") - mult(q_im, sin_tab, "vxyz,xk->vkyz")).astype(bf)
    i_im = (mult(q_im, cos_tab, "vxyz,xk->vkyz") + mult(q_re, sin_tab, "vxyz,xk->vkyz")).astype(bf)
    spectrum = lax.all_to_all(
        jnp.stack([i_re, i_im]), "grid", split_axis=2, concat_axis=3, tiled=True
    )
    s_re = spectrum[0]
    s_im = spectrum[1]
    h_re = (mult(s_re, cos_tab, "vxyz,yk->vxkz") - mult(s_im, sin_tab, "vxyz,yk->vxkz")).astype(bf)
    h_im = (mult(s_im, cos_tab, "vxyz,yk->vxkz") + mult(s_re, sin_tab, "vxyz,yk->vxkz")).astype(bf)
    final = mult(h_re, cos_tab, "vxyz,zk->vxyk") - mult(h_im, sin_tab, "vxyz,zk->vxyk")
    potential = (final / float(NG**3)).astype(bf).reshape(col_local, planes * NG * NG)
    pot_rows = lax.all_to_all(potential, "vec", split_axis=1, concat_axis=0, tiled=True)
    return project(pair, pot_rows)


def solution(mesh):
    in_specs = (P(("grid", "vec"), None), P(), P())
    out_specs = P(("grid", "vec"), None)
    return jax.shard_map(shards, mesh=mesh, in_specs=in_specs, out_specs=out_specs, check_vma=False)
```

```python
import math

import jax
import jax.numpy as jnp
from jax import lax
from jax.experimental import pallas as pl
from jax.experimental.pallas import tpu as pltpu
from jax.sharding import PartitionSpec as P

NG = 96


SCREEN = 2.25


def wave_tables(count):
    index = lax.iota(jnp.int32, count)
    phase = index[:, None] * index[None, :] % count
    angle = phase.astype(jnp.float32) * (2.0 * math.pi / count)
    return (jnp.cos(angle).astype(jnp.bfloat16), jnp.sin(angle).astype(jnp.bfloat16))


def wavenumber(index, count):
    return jnp.where(index < count // 2, index, index - count).astype(jnp.float32)


def screened(wave_x, wave_y, wave_z):
    squared = (
        wave_x[:, None, None] * wave_x[:, None, None]
        + wave_y[None, :, None] * wave_y[None, :, None]
        + wave_z[None, None, :] * wave_z[None, None, :]
    )
    factor = NG / (2.0 * math.pi) * (NG / (2.0 * math.pi))
    return jnp.where(squared > 0.5, factor / (squared + SCREEN), jnp.float32(0.0))


def mult(data, table, form):
    return jnp.einsum(form, data, table, preferred_element_type=jnp.float32)


LANES = 128


def exchange_kernel(axes, total, gather, x_ref, o_ref, held, send_sem, recv_sem, own_sem):
    if len(axes) == 2:
        vec_count = lax.axis_size("vec")
        count = lax.axis_size("grid") * vec_count
        me = lax.axis_index("grid") * vec_count + lax.axis_index("vec")
    else:
        count = lax.axis_size(axes[0])
        me = lax.axis_index(axes[0])
    land = held if total else o_ref

    def place(index):
        if len(axes) == 2:
            return (index // vec_count, lax.rem(index, vec_count))
        if axes[0] == "grid":
            return (index, lax.axis_index("vec"))
        return (lax.axis_index("grid"), index)

    def part(index):
        return x_ref if gather else x_ref.at[index]

    barrier = pltpu.get_barrier_semaphore()

    def greet(step, carry):
        pl.semaphore_signal(
            barrier,
            inc=1,
            device_id=place(lax.rem(me + step, count)),
            device_id_type=pl.DeviceIdType.MESH,
        )
        return carry

    lax.fori_loop(1, count, greet, 0)
    own = pltpu.make_async_copy(part(me), land.at[me], own_sem)
    own.start()
    pl.semaphore_wait(barrier, count - 1)

    def copy(step, source, slot):
        peer = lax.rem(me + step, count)
        return pltpu.make_async_remote_copy(
            src_ref=part(source),
            dst_ref=land.at[slot],
            send_sem=send_sem.at[step],
            recv_sem=recv_sem.at[step],
            device_id=place(peer),
            device_id_type=pl.DeviceIdType.MESH,
        )

    def send(step, carry):
        copy(step, lax.rem(me + step, count), me).start()
        return carry

    lax.fori_loop(1, count, send, 0)
    own.wait()

    def receive(step, carry):
        source = lax.rem(me + count - step, count)
        copy(step, source, source).wait_recv()
        return carry

    lax.fori_loop(1, count, receive, 0)
    if total:
        o_ref[...] = jnp.sum(held[...].astype(jnp.float32), axis=0).astype(o_ref.dtype)

    def drain(step, carry):
        copy(step, lax.rem(me + step, count), me).wait_send()
        return carry

    lax.fori_loop(1, count, drain, 0)


def exchange(blocks, ident, total=False, axes=("grid", "vec"), gather=False):
    rows, lanes = blocks.shape[-2:]
    count = 1
    for axis in axes:
        count *= lax.axis_size(axis)
    shape = (rows, lanes) if total else (count, rows, lanes)
    held_shape = blocks.shape if total else (1, 8, LANES)

    def body(*refs):
        exchange_kernel(axes, total, gather, *refs)

    return pl.pallas_call(
        body,
        out_shape=jax.ShapeDtypeStruct(shape, blocks.dtype),
        in_specs=[pl.BlockSpec(memory_space=pltpu.VMEM)],
        out_specs=pl.BlockSpec(memory_space=pltpu.VMEM),
        scratch_shapes=[
            pltpu.VMEM(held_shape, blocks.dtype),
            pltpu.SemaphoreType.DMA((count,)),
            pltpu.SemaphoreType.DMA((count,)),
            pltpu.SemaphoreType.DMA(()),
        ],
        compiler_params=pltpu.CompilerParams(
            collective_id=ident, has_side_effects=True, vmem_limit_bytes=32 << 20
        ),
        name="exchange_total" if total else "exchange_gather" if gather else "exchange_blocks",
    )(blocks)


def share_kernel(chunks, x_ref, o_ref, near, wide, far, sum1, sum2, sum3, sends, recvs, own_sem):
    bf = jnp.bfloat16
    f32 = jnp.float32
    vec_count = lax.axis_size("vec")
    deep = lax.axis_size("grid") // 2
    grid_at, mine = lax.axis_index("grid"), lax.axis_index("vec")
    level, core = grid_at // 2, lax.rem(grid_at, 2)
    other = 1 - core
    across = vec_count - 1

    def partner(step):
        return (level * 2 + other, mine)

    def beside(step):
        return (grid_at, lax.rem(mine + step, vec_count))

    def above(step):
        return (lax.rem(level + step, deep) * 2 + core, mine)

    peers = [partner(1)]
    peers += [beside(step) for step in range(1, vec_count)]
    peers += [above(step) for step in range(1, deep)]
    barrier = pltpu.get_barrier_semaphore()
    for peer in peers:
        pl.semaphore_signal(barrier, inc=1, device_id=peer, device_id_type=pl.DeviceIdType.MESH)
    pl.semaphore_wait(barrier, len(peers))

    def send(source, target, slot, peer):
        return pltpu.make_async_remote_copy(
            src_ref=source,
            dst_ref=target,
            send_sem=sends.at[slot],
            recv_sem=recvs.at[slot],
            device_id=peer,
            device_id_type=pl.DeviceIdType.MESH,
        )

    per_chunk = 2 + 2 * across + 2 * (deep - 1)

    def copies(stage, c):
        base = c * per_chunk
        if stage == 0:
            return [send(x_ref.at[c, other], near.at[c], base, partner(1))]
        if stage == 1:
            return [
                send(
                    sum1.at[c, lax.rem(mine + step, vec_count)],
                    wide.at[c, step - 1],
                    base + step,
                    beside(step),
                )
                for step in range(1, vec_count)
            ]
        if stage == 2:
            return [
                send(
                    sum2.at[c, lax.rem(level + step, deep)],
                    far.at[c, step - 1],
                    base + across + step,
                    above(step),
                )
                for step in range(1, deep)
            ]
        base += across + deep
        if stage == 3:
            spot = o_ref.at[c, core, mine, level]
            return [send(sum3.at[c], spot, base + step - 1, above(step)) for step in range(1, deep)]
        base += deep - 1
        if stage == 4:
            spot = o_ref.at[c, core, mine]
            return [send(spot, spot, base + step - 1, beside(step)) for step in range(1, vec_count)]
        spot = o_ref.at[c, core]
        return [send(spot, spot, base + across, partner(1))]

    def own(c):
        return pltpu.make_async_copy(sum3.at[c], o_ref.at[c, core, mine, level], own_sem.at[c])

    def prepare(stage, c):
        for move in copies(stage - 1, c):
            move.wait_recv()
        if stage == 1:
            sum1[c] = (x_ref[c, core].astype(f32) + near[c].astype(f32)).astype(bf)
        if stage == 2:
            total = sum1[c, mine].astype(f32)
            for step in range(across):
                total += wide[c, step].astype(f32)
            sum2[c] = total.astype(bf)
        if stage == 3:
            total = sum2[c, level].astype(f32)
            for step in range(deep - 1):
                total += far[c, step].astype(f32)
            sum3[c] = total.astype(bf)
            own(c).start()
        if stage == 4:
            own(c).wait()

    for tick in range(chunks + 6):
        for stage in range(6, -1, -1):
            c = tick - stage
            if 0 <= c < chunks:
                if stage > 0:
                    prepare(stage, c)
                if stage < 6:
                    for move in copies(stage, c):
                        move.start()
    for c in range(chunks):
        for stage in range(6):
            for move in copies(stage, c):
                move.wait_send()


ROWS = 16


def share_rows(picked, grid_count, vec_count):
    bf = jnp.bfloat16
    npoints, norb = picked.shape
    count = grid_count * vec_count
    if npoints % (count * ROWS) != 0 or grid_count % 2 != 0:
        return lax.psum(picked.astype(jnp.float32), ("grid", "vec")).astype(picked.dtype)
    chunks = npoints // (count * ROWS)
    deep = grid_count // 2
    shape = (chunks, 2, vec_count, deep, ROWS, norb)
    slots = chunks * (2 + 2 * (vec_count - 1) + 2 * (deep - 1))

    def body(*refs):
        share_kernel(chunks, *refs)

    return pl.pallas_call(
        body,
        out_shape=jax.ShapeDtypeStruct(shape, bf),
        in_specs=[pl.BlockSpec(memory_space=pltpu.VMEM)],
        out_specs=pl.BlockSpec(memory_space=pltpu.VMEM),
        scratch_shapes=[
            pltpu.VMEM((chunks, vec_count, deep, ROWS, norb), bf),
            pltpu.VMEM((chunks, vec_count - 1, deep, ROWS, norb), bf),
            pltpu.VMEM((chunks, deep - 1, ROWS, norb), bf),
            pltpu.VMEM((chunks, vec_count, deep, ROWS, norb), bf),
            pltpu.VMEM((chunks, deep, ROWS, norb), bf),
            pltpu.VMEM((chunks, ROWS, norb), bf),
            pltpu.SemaphoreType.DMA((slots,)),
            pltpu.SemaphoreType.DMA((slots,)),
            pltpu.SemaphoreType.DMA((chunks,)),
        ],
        compiler_params=pltpu.CompilerParams(
            collective_id=4, has_side_effects=True, vmem_limit_bytes=32 << 20
        ),
        name="share_rows",
    )(picked.reshape(shape)).reshape(npoints, norb)


OCTET = 8


def pick_kernel(points_ref, flags_ref, offset_ref, orb_ref, o_ref, found, where, spare, sheet, sem):
    octets, _, norb = orb_ref.shape
    limit = octets * OCTET
    npoints = o_ref.shape[0]
    offset = offset_ref[0]
    sheet[...] = jnp.zeros_like(sheet)

    def fetch(slot, octet):
        return pltpu.make_async_copy(orb_ref.at[octet], found.at[slot], sem)

    def look(i, held):
        position = points_ref[i] - offset
        inside = (position >= 0) & (position < limit)

        @pl.when(inside)
        def _():
            fetch(held, position // OCTET).start()
            where[held] = i
            spare[held] = lax.rem(position, OCTET)

        return held + inside.astype(jnp.int32)

    def scan(group, held):
        return lax.cond(
            flags_ref[group] > 0,
            lambda h: lax.fori_loop(0, OCTET, lambda k, n: look(group * OCTET + k, n), h),
            lambda h: h,
            held,
        )

    held = lax.fori_loop(0, npoints // OCTET, scan, 0)

    def settle(slot, carry):
        fetch(slot, 0).wait()
        return carry

    lax.fori_loop(0, held, settle, 0)
    line = lax.broadcasted_iota(jnp.int32, (OCTET, norb), 0)

    def place(slot, carry):
        octet = found[slot].astype(jnp.float32)
        row = jnp.sum(jnp.where(line == spare[slot], octet, 0.0), axis=0, keepdims=True)
        sheet[pl.ds(where[slot], 1), :] = row
        return carry

    lax.fori_loop(0, held, place, 0)
    o_ref[...] = sheet[...].astype(o_ref.dtype)


def pick_rows(orbitals, points, offset):
    rows, norb = orbitals.shape
    npoints = points.shape[0]
    position = points - offset
    if rows % OCTET != 0 or npoints % OCTET != 0:
        inside = (position >= 0) & (position < rows)
        picked = jnp.take(orbitals, jnp.clip(position, 0, rows - 1), axis=0)
        return jnp.where(inside[:, None], picked, jnp.zeros_like(picked))
    inside = (position >= 0) & (position < rows)
    flags = jnp.max(inside.reshape(-1, OCTET).astype(jnp.int32), axis=1)
    return pl.pallas_call(
        pick_kernel,
        out_shape=jax.ShapeDtypeStruct((npoints, norb), orbitals.dtype),
        in_specs=[
            pl.BlockSpec(memory_space=pltpu.SMEM),
            pl.BlockSpec(memory_space=pltpu.SMEM),
            pl.BlockSpec(memory_space=pltpu.SMEM),
            pl.BlockSpec(memory_space=pl.ANY),
        ],
        out_specs=pl.BlockSpec(memory_space=pltpu.VMEM),
        scratch_shapes=[
            pltpu.VMEM((npoints, OCTET, norb), orbitals.dtype),
            pltpu.SMEM((npoints,), jnp.int32),
            pltpu.SMEM((npoints,), jnp.int32),
            pltpu.VMEM((npoints, norb), jnp.float32),
            pltpu.SemaphoreType.DMA(()),
        ],
        compiler_params=pltpu.CompilerParams(vmem_limit_bytes=40 << 20),
        name="pick_rows",
    )(points, flags, offset[None].astype(jnp.int32), orbitals.reshape(rows // OCTET, OCTET, norb))


def project(pair, pot_rows):
    scale = 1.0 / math.sqrt(float(NG**3))
    term = lax.dot_general(
        pair, pot_rows, (((0,), (1,)), ((), ())), preferred_element_type=jnp.float32
    )
    term = term * jnp.float32(scale)
    npoints, cols = term.shape
    count = lax.axis_size("grid") * lax.axis_size("vec")
    share = npoints // count
    if share * cols % LANES == 0:
        blocks = term.reshape(count, share * cols // LANES, LANES)
        return exchange(blocks, 3, True).reshape(share, cols)
    partial_block = lax.psum_scatter(term, "grid", scatter_dimension=0, tiled=True)
    return lax.psum_scatter(partial_block, "vec", scatter_dimension=0, tiled=True)


def peers_of():
    vec_count = lax.axis_size("vec")
    count = lax.axis_size("grid") * vec_count
    me = lax.axis_index("grid") * vec_count + lax.axis_index("vec")

    def place(index):
        return (index // vec_count, lax.rem(index, vec_count))

    return count, me, place


def greet_all(count, me, place):
    barrier = pltpu.get_barrier_semaphore()

    def greet(step, carry):
        pl.semaphore_signal(
            barrier,
            inc=1,
            device_id=place(lax.rem(me + step, count)),
            device_id_type=pl.DeviceIdType.MESH,
        )
        return carry

    lax.fori_loop(1, count, greet, 0)


def wait_greeted(count):
    pl.semaphore_wait(pltpu.get_barrier_semaphore(), count - 1)


NT = (((1,), (1,)), ((), ()))
NN = (((1,), (0,)), ((), ()))
LINES = 16
SPAN = LINES * NG
TAKE = 512
JOIN = 3


def pair_fit_kernel(
    orb_ref, rows_ref, panel_ref, pair_ref, field_ref, fit_buf, fit_rows, out_buf,
    send_sem, recv_sem, own_sem,
):
    bf = jnp.bfloat16
    block = pl.program_id(0)
    blocks = pl.num_programs(0)
    count, me, place = peers_of()
    npoints = rows_ref.shape[0]
    cols = panel_ref.shape[0]
    per_plane = NG // LINES
    groups = blocks // JOIN
    tall = JOIN * LINES

    def send(group, begin, lines):
        slot = lax.rem(group, 2)
        start = pl.multiple_of(lax.rem(group * JOIN, per_plane) * LINES + begin, LINES)
        target = field_ref.at[me, group * JOIN // per_plane, pl.ds(start, lines)]

        def body(step, carry):
            peer = lax.rem(me + step, count)
            pltpu.make_async_remote_copy(
                src_ref=out_buf.at[slot, peer, pl.ds(begin, lines)],
                dst_ref=target,
                send_sem=send_sem.at[slot],
                recv_sem=recv_sem.at[me],
                device_id=place(peer),
                device_id_type=pl.DeviceIdType.MESH,
            ).start()
            return carry

        pltpu.make_async_copy(
            out_buf.at[slot, me, pl.ds(begin, lines)], target, own_sem.at[slot]
        ).start()
        lax.fori_loop(1, count, body, 0, unroll=True)

    def drain(group):
        slot = lax.rem(group, 2)
        sent = out_buf.at[slot, pl.ds(0, count - 1)]
        mine = out_buf.at[slot, me]
        pltpu.make_async_copy(mine, mine, own_sem.at[slot]).wait()
        pltpu.make_async_copy(sent, sent, send_sem.at[slot]).wait()

    @pl.when(block == 0)
    def _():
        greet_all(count, me, place)

    @pl.when(block == 1)
    def _():
        wait_greeted(count)

    before = jnp.maximum(block - 1, 0)

    @pl.when((block > 2 * JOIN) & (lax.rem(before, JOIN) == 0))
    def _():
        drain(before // JOIN - 2)

    def multiply(first):
        part = lax.dot_general(
            rows_ref[first : first + TAKE, :], orb_ref[...], NT, preferred_element_type=jnp.float32
        )
        pair_ref[0, first : first + TAKE, :] = (part * part).astype(bf)

    def arrange(index):
        for line in range(LINES):
            begin = line * NG
            low = begin // LANES * LANES
            turn = begin - low
            wide = fit_buf[:, low : min(low + 2 * LANES, SPAN)]
            if wide.shape[1] == LANES:
                wide = jnp.concatenate([wide, wide], axis=1)
            if turn:
                wide = pltpu.roll(wide, 2 * LANES - turn, 1)
            fit_rows[pl.ds(line, cols, stride=LINES), :] = wide[:, :LANES]
        slot = lax.rem(index // JOIN, 2)
        begin = pl.multiple_of(lax.rem(index, JOIN) * LINES, LINES)
        out_buf[slot, :, pl.ds(begin, LINES), :] = (
            fit_rows[...].astype(bf).reshape(cols, LINES, LANES)
        )

    @pl.when(block == 0)
    def _():
        fit_buf[...] = jnp.zeros_like(fit_buf)

    multiply(0)
    arrange(before)
    for first in range(TAKE, npoints // 2, TAKE):
        multiply(first)

    @pl.when((block >= JOIN) & (lax.rem(block, JOIN) == 0))
    def _():
        send(block // JOIN - 1, 0, tall)

    for late in range(JOIN - 1):

        @pl.when(block == blocks - JOIN + 1 + late)
        def _(late=late):
            send(groups - 1, late * LINES, LINES)

    for first in range(npoints // 2, npoints, TAKE):
        multiply(first)
    fit_buf[...] = lax.dot_general(
        panel_ref[...], pair_ref[0], NN, preferred_element_type=jnp.float32
    )

    @pl.when(block == blocks - 1)
    def _():
        arrange(block)
        send(groups - 1, (JOIN - 1) * LINES, LINES)

        def receive(step, carry):
            source = lax.rem(me + count - step, count)
            land = field_ref.at[source]
            pltpu.make_async_copy(land, land, recv_sem.at[source]).wait()
            return carry

        lax.fori_loop(1, count, receive, 0)
        drain(groups - 2)
        drain(groups - 1)


def pair_and_fit(orbitals, point_rows, panel):
    bf = jnp.bfloat16
    rows, norb = orbitals.shape
    npoints = point_rows.shape[0]
    cols = panel.shape[0]
    blocks = rows // SPAN
    planes = rows // (NG * NG)
    count = lax.axis_size("grid") * lax.axis_size("vec")
    return pl.pallas_call(
        pair_fit_kernel,
        grid=(blocks,),
        in_specs=[
            pl.BlockSpec((SPAN, norb), lambda i: (i, 0)),
            pl.BlockSpec((npoints, norb), lambda i: (0, 0)),
            pl.BlockSpec((cols, npoints), lambda i: (0, 0)),
        ],
        out_specs=[
            pl.BlockSpec((1, npoints, SPAN), lambda i: (i, 0, 0)),
            pl.BlockSpec(memory_space=pl.ANY),
        ],
        out_shape=[
            jax.ShapeDtypeStruct((blocks, npoints, SPAN), bf),
            jax.ShapeDtypeStruct((count, planes, NG, LANES), bf),
        ],
        scratch_shapes=[
            pltpu.VMEM((cols, SPAN), jnp.float32),
            pltpu.VMEM((cols * LINES, LANES), jnp.float32),
            pltpu.VMEM((2, cols, JOIN * LINES, LANES), bf),
            pltpu.SemaphoreType.DMA((2,)),
            pltpu.SemaphoreType.DMA((count,)),
            pltpu.SemaphoreType.DMA((2,)),
        ],
        compiler_params=pltpu.CompilerParams(
            collective_id=1, has_side_effects=True, vmem_limit_bytes=50 << 20
        ),
        name="pair_fit_send",
    )(orbitals, point_rows, panel)


GROUP = 24
HALF = 64
PIECE = NG * NG // LANES // 3
RING = 4


def solve_project_kernel(
    field_ref, tz_ref, ty_ref, tyi_ref, tzi_ref, pair_ref, o_ref,
    field, by_y, by_x, flat, dense, pot, ring, land, wide, total, parts, held,
    field_sem, send_sem, recv_sem, own_sem, pair_sem, part_send, part_recv,
):
    bf = jnp.bfloat16
    f32 = jnp.float32
    count, me, place = peers_of()
    blocks, npoints, _ = pair_ref.shape
    pieces = pot.shape[0]
    cols = count
    share = npoints // count
    planes = NG // count
    per_piece = blocks // pieces
    strips = SPAN // LANES

    def load(step):
        part = pl.ds(step * GROUP, GROUP)
        return pltpu.make_async_copy(field_ref.at[part], field.at[part], field_sem.at[step])

    def fetch(block):
        slot = lax.rem(block, RING)
        return pltpu.make_async_copy(pair_ref.at[block], ring.at[slot], pair_sem.at[slot])

    for step in range(NG // GROUP):
        load(step).start()
    greet_all(count, me, place)

    lane = lax.broadcasted_iota(jnp.int32, (NG, LANES), 1)
    row = lax.broadcasted_iota(jnp.int32, (NG, LANES), 0)
    sign = jnp.where(lane < HALF, 1.0, -1.0).astype(f32)
    wave_z = lax.rem(lane, HALF).astype(f32)
    wave_x = jnp.where(row < NG // 2, row, row - NG).astype(f32)
    plane_sq = wave_x * wave_x + wave_z * wave_z
    factor = NG / (2.0 * math.pi) * (NG / (2.0 * math.pi))

    def both(shapes):
        top = jnp.concatenate([part.astype(bf) for part in shapes], axis=1)
        turned = [(pltpu.roll(part, HALF, 1) * sign).astype(bf) for part in shapes]
        return jnp.concatenate([top, jnp.concatenate(turned, axis=1)], axis=0)

    def cut(sheet, k):
        return sheet[:, k * LANES : (k + 1) * LANES]

    def forward(step, carry):
        first = step * GROUP
        load(step).wait()
        data = field[pl.ds(first, GROUP)].reshape(GROUP * NG, LANES)
        a = lax.dot_general(data, tz_ref[...], NN, preferred_element_type=f32).astype(bf)
        top = [a[k * NG : (k + 1) * NG, :LANES] for k in range(GROUP)]
        low = [a[k * NG : (k + 1) * NG, LANES:] for k in range(GROUP)]
        stack = jnp.concatenate(
            [jnp.concatenate(top, axis=1), jnp.concatenate(low, axis=1)], axis=0
        )
        b = lax.dot_general(ty_ref[...], stack, NN, preferred_element_type=f32)
        for k in range(GROUP):
            by_y[pl.ds(first + k, NG, stride=NG), :] = cut(b, k)
        return carry

    lax.fori_loop(0, NG // GROUP, forward, 0)

    def prime(block, carry):
        fetch(block).start()
        return carry

    lax.fori_loop(0, RING, prime, 0)

    def middle(step, carry):
        first = step * GROUP
        rows = [by_y[pl.ds((first + k) * NG, NG), :] for k in range(GROUP)]
        h = lax.dot_general(ty_ref[...], both(rows), NN, preferred_element_type=f32)
        scaled = []
        for k in range(GROUP):
            index = first + k
            wave_y = jnp.where(index < NG // 2, index, index - NG).astype(f32)
            squared = plane_sq + wave_y * wave_y
            kernel = jnp.where(squared > 0.5, factor / (squared + SCREEN), 0.0)
            scaled.append(cut(h, k) * kernel)
        g = lax.dot_general(tyi_ref[...], both(scaled), NN, preferred_element_type=f32)
        for k in range(GROUP):
            by_x[pl.ds(first + k, NG, stride=NG), :] = cut(g, k)
        return carry

    lax.fori_loop(0, NG // GROUP, middle, 0)
    wait_greeted(count)

    def own(piece):
        return pltpu.make_async_copy(pot.at[piece, me], land.at[piece, me], own_sem.at[piece])

    def send_piece(piece):
        def body(step, carry):
            peer = lax.rem(me + step, count)
            pltpu.make_async_remote_copy(
                src_ref=pot.at[piece, peer],
                dst_ref=land.at[piece, me],
                send_sem=send_sem.at[piece],
                recv_sem=recv_sem.at[piece],
                device_id=place(peer),
                device_id_type=pl.DeviceIdType.MESH,
            ).start()
            return carry

        own(piece).start()
        lax.fori_loop(1, count, body, 0)

    quarter = NG // 4
    spot = lane[:quarter]

    def backward(local, carry):
        rows = [by_x[pl.ds((local + planes * k) * NG, NG), :] for k in range(count)]
        p = lax.dot_general(tyi_ref[...], both(rows), NN, preferred_element_type=f32).astype(bf)
        tall = jnp.concatenate([cut(p, k) for k in range(count)], axis=0)
        final = lax.dot_general(tall, tzi_ref[...], NN, preferred_element_type=f32)
        flat[...] = final * f32(1.0 / float(NG**3))
        for k in range(count):
            y0, y1, y2, y3 = [flat[pl.ds(k * NG + j, quarter, stride=4), :] for j in range(4)]
            y1, y2, y3 = pltpu.roll(y1, 96, 1), pltpu.roll(y2, 64, 1), pltpu.roll(y3, 32, 1)
            base = k % 4 * 3 * PIECE
            dense[pl.ds(base, quarter, stride=3), :] = jnp.where(spot < 96, y0, y1)
            dense[pl.ds(base + 1, quarter, stride=3), :] = jnp.where(spot < 64, y1, y2)
            dense[pl.ds(base + 2, quarter, stride=3), :] = jnp.where(spot < 32, y2, y3)
            for m in range(3):
                pot[local * 3 + m, k] = dense[base + m * PIECE : base + (m + 1) * PIECE, :].astype(bf)
        for m in range(3):
            send_piece(local * 3 + m)
        return carry

    lax.fori_loop(0, planes, backward, 0)
    total[...] = jnp.zeros_like(total)

    def work(piece, carry):
        own(piece).wait()
        others = land.at[piece, pl.ds(0, count - 1)]
        pltpu.make_async_copy(others, others, recv_sem.at[piece]).wait()
        wide[...] = land[piece].astype(f32).reshape(cols * PIECE, LANES)
        for half in range(per_piece):
            block = piece * per_piece + half
            slot = lax.rem(block, RING)
            fetch(block).wait()
            lines = [
                wide[pl.ds(half * strips + j, cols, stride=PIECE), :].astype(bf)
                for j in range(strips)
            ]
            total[...] += lax.dot_general(
                jnp.concatenate(lines, axis=1), ring[slot], NT, preferred_element_type=f32
            )

            @pl.when(block + RING < blocks)
            def _():
                fetch(block + RING).start()

        return carry

    lax.fori_loop(0, pieces, work, 0)

    scale = f32(1.0 / math.sqrt(float(NG**3)))
    low_lane = lax.broadcasted_iota(jnp.int32, (cols // 2, LANES), 1) < share
    for k in range(npoints // LANES):
        tile = total[:, k * LANES : (k + 1) * LANES] * scale
        top, low = tile[: cols // 2], tile[cols // 2 :]
        parts[2 * k] = jnp.where(low_lane, top, pltpu.roll(low, share, 1))
        parts[2 * k + 1] = jnp.where(low_lane, pltpu.roll(top, share, 1), low)

    def part_copy(step, source, slot):
        peer = lax.rem(me + step, count)
        return pltpu.make_async_remote_copy(
            src_ref=parts.at[source],
            dst_ref=held.at[slot],
            send_sem=part_send.at[step],
            recv_sem=part_recv.at[step],
            device_id=place(peer),
            device_id_type=pl.DeviceIdType.MESH,
        )

    def part_start(step, carry):
        part_copy(step, lax.rem(me + step, count), me).start()
        return carry

    lax.fori_loop(1, count, part_start, 0)
    held[me] = parts[me]

    def drain_piece(piece, carry):
        sent = pot.at[piece, pl.ds(0, count - 1)]
        pltpu.make_async_copy(sent, sent, send_sem.at[piece]).wait()
        return carry

    lax.fori_loop(0, pieces, drain_piece, 0)

    def part_receive(step, carry):
        source = lax.rem(me + count - step, count)
        part_copy(step, source, source).wait_recv()
        return carry

    lax.fori_loop(1, count, part_receive, 0)
    summed = jnp.sum(held[...], axis=0)
    pile = jnp.concatenate([summed, pltpu.roll(summed, share, 1)], axis=0)
    o_ref[...] = pile.T[:share, :]

    def part_drain(step, carry):
        part_copy(step, lax.rem(me + step, count), me).wait_send()
        return carry

    lax.fori_loop(1, count, part_drain, 0)


def solve_and_project(field, pair, count):
    bf = jnp.bfloat16
    f32 = jnp.float32
    cos_tab, sin_tab = wave_tables(NG)
    keep = NG // 2 + 1

    def padded(table):
        return jnp.pad(table[:, :keep], ((0, LANES - NG), (0, HALF - keep)))

    cz, sz = padded(cos_tab), padded(sin_tab)
    tz = jnp.concatenate([cz, -sz, -sz, -cz], axis=1)
    ty = jnp.concatenate([cos_tab, sin_tab], axis=1)
    tyi = jnp.concatenate([cos_tab, -sin_tab], axis=1)
    spot = lax.iota(jnp.int32, HALF)[:, None]
    weight = jnp.where((spot == 0) | (spot == NG // 2), 1.0, 2.0).astype(bf)
    tzi = jnp.concatenate([cz.T * weight, -(sz.T * weight)], axis=0)
    pieces = NG // count * 3
    blocks, npoints, span = pair.shape
    cols = count
    any_spec = pl.BlockSpec(memory_space=pl.ANY)
    vmem_spec = pl.BlockSpec(memory_space=pltpu.VMEM)
    return pl.pallas_call(
        solve_project_kernel,
        out_shape=jax.ShapeDtypeStruct((npoints // count, cols), f32),
        in_specs=[any_spec] + [vmem_spec] * 4 + [any_spec],
        out_specs=vmem_spec,
        scratch_shapes=[
            pltpu.VMEM((NG, NG, LANES), bf),
            pltpu.VMEM((NG * NG, LANES), f32),
            pltpu.VMEM((NG * NG, LANES), f32),
            pltpu.VMEM((count * NG, LANES), f32),
            pltpu.VMEM((4 * 3 * PIECE, LANES), f32),
            pltpu.VMEM((pieces, count, PIECE, LANES), bf),
            pltpu.VMEM((RING, npoints, span), bf),
            pltpu.VMEM((pieces, count, PIECE, LANES), bf),
            pltpu.VMEM((cols * PIECE, LANES), f32),
            pltpu.VMEM((cols, npoints), f32),
            pltpu.VMEM((count, cols // 2, LANES), f32),
            pltpu.VMEM((count, cols // 2, LANES), f32),
            pltpu.SemaphoreType.DMA((NG // GROUP,)),
            pltpu.SemaphoreType.DMA((pieces,)),
            pltpu.SemaphoreType.DMA((pieces,)),
            pltpu.SemaphoreType.DMA((pieces,)),
            pltpu.SemaphoreType.DMA((RING,)),
            pltpu.SemaphoreType.DMA((count,)),
            pltpu.SemaphoreType.DMA((count,)),
        ],
        compiler_params=pltpu.CompilerParams(
            collective_id=2, has_side_effects=True, vmem_limit_bytes=60 << 20
        ),
        name="solve_project",
    )(field.reshape(NG, NG, LANES), tz, ty, tyi, tzi, pair)


def fits_planes(rows, npoints, cols, count):
    blocks = rows // SPAN
    return (
        cols == count
        and rows % (NG * NG) == 0
        and NG % (rows // (NG * NG)) == 0
        and blocks >= max(RING, 2 * JOIN)
        and NG // LINES % JOIN == 0
        and npoints % TAKE == 0
        and 2 * npoints == count * LANES
    )


def shards(orbitals, inverse_panel, points):
    bf = jnp.bfloat16
    row_count = orbitals.shape[0]
    grid_count = lax.axis_size("grid")
    vec_count = lax.axis_size("vec")
    npoints = points.shape[0]
    offset = (lax.axis_index("grid") * vec_count + lax.axis_index("vec")) * row_count
    picked = pick_rows(orbitals, points, offset)
    point_rows = share_rows(picked, grid_count, vec_count)

    if fits_planes(row_count, npoints, inverse_panel.shape[1], grid_count * vec_count):
        pair, field = pair_and_fit(orbitals, point_rows, inverse_panel.T)
        return solve_and_project(field, pair, grid_count * vec_count)

    def pair_block(block):
        correlation = lax.dot_general(
            block, point_rows, (((1,), (1,)), ((), ())), preferred_element_type=jnp.float32
        )
        return (correlation * correlation).astype(bf)

    pair = lax.map(pair_block, orbitals.reshape(4, row_count // 4, orbitals.shape[1])).reshape(
        row_count, npoints
    )
    fit_cols = lax.dot_general(
        inverse_panel, pair, (((0,), (1,)), ((), ())), preferred_element_type=jnp.float32
    ).astype(bf)
    slab = lax.all_to_all(fit_cols, "vec", split_axis=0, concat_axis=1, tiled=True)
    col_local = slab.shape[0]
    planes = NG // grid_count
    field = slab.reshape(col_local, planes, NG, NG)
    cos_tab, sin_tab = wave_tables(NG)
    z_re = mult(field, cos_tab, "vxyz,zk->vxyk").astype(bf)
    z_im = (-mult(field, sin_tab, "vxyz,zk->vxyk")).astype(bf)
    y_re = (mult(z_re, cos_tab, "vxyz,yk->vxkz") + mult(z_im, sin_tab, "vxyz,yk->vxkz")).astype(bf)
    y_im = (mult(z_im, cos_tab, "vxyz,yk->vxkz") - mult(z_re, sin_tab, "vxyz,yk->vxkz")).astype(bf)
    stacked = jnp.stack([y_re, y_im])
    waves = wavenumber(lax.iota(jnp.int32, NG), NG)
    y_waves = wavenumber(lax.axis_index("grid") * planes + lax.iota(jnp.int32, planes), NG)
    kernel = screened(waves, y_waves, waves)[None]
    piece = lax.all_to_all(stacked, "grid", split_axis=3, concat_axis=2, tiled=True)
    p_re = piece[0]
    p_im = piece[1]
    x_re = mult(p_re, cos_tab, "vxyz,xk->vkyz") + mult(p_im, sin_tab, "vxyz,xk->vkyz")
    x_im = mult(p_im, cos_tab, "vxyz,xk->vkyz") - mult(p_re, sin_tab, "vxyz,xk->vkyz")
    q_re = (x_re * kernel).astype(bf)
    q_im = (x_im * kernel).astype(bf)
    i_re = (mult(q_re, cos_tab, "vxyz,xk->vkyz") - mult(q_im, sin_tab, "vxyz,xk->vkyz")).astype(bf)
    i_im = (mult(q_im, cos_tab, "vxyz,xk->vkyz") + mult(q_re, sin_tab, "vxyz,xk->vkyz")).astype(bf)
    spectrum = lax.all_to_all(
        jnp.stack([i_re, i_im]), "grid", split_axis=2, concat_axis=3, tiled=True
    )
    s_re = spectrum[0]
    s_im = spectrum[1]
    h_re = (mult(s_re, cos_tab, "vxyz,yk->vxkz") - mult(s_im, sin_tab, "vxyz,yk->vxkz")).astype(bf)
    h_im = (mult(s_im, cos_tab, "vxyz,yk->vxkz") + mult(s_re, sin_tab, "vxyz,yk->vxkz")).astype(bf)
    final = mult(h_re, cos_tab, "vxyz,zk->vxyk") - mult(h_im, sin_tab, "vxyz,zk->vxyk")
    potential = (final / float(NG**3)).astype(bf).reshape(col_local, planes * NG * NG)
    pot_rows = lax.all_to_all(potential, "vec", split_axis=1, concat_axis=0, tiled=True)
    return project(pair, pot_rows)


def solution(mesh):
    in_specs = (P(("grid", "vec"), None), P(), P())
    out_specs = P(("grid", "vec"), None)
    return jax.shard_map(shards, mesh=mesh, in_specs=in_specs, out_specs=out_specs, check_vma=False)
```

```python
import math

import jax
import jax.numpy as jnp
import numpy as np
from jax import lax
from jax.experimental import pallas as pl
from jax.experimental.pallas import tpu as pltpu
from jax.sharding import PartitionSpec as P

NG = 96


SCREEN = 2.25


def wave_tables(count):
    index = lax.iota(jnp.int32, count)
    phase = index[:, None] * index[None, :] % count
    angle = phase.astype(jnp.float32) * (2.0 * math.pi / count)
    return (jnp.cos(angle).astype(jnp.bfloat16), jnp.sin(angle).astype(jnp.bfloat16))


def literal_tables(count):
    index = np.arange(count)
    phase = index[:, None] * index[None, :] % count
    angle = phase.astype(np.float32) * np.float32(2.0 * math.pi / count)
    return np.cos(angle).astype(jnp.bfloat16), np.sin(angle).astype(jnp.bfloat16)


def wavenumber(index, count):
    return jnp.where(index < count // 2, index, index - count).astype(jnp.float32)


def screened(wave_x, wave_y, wave_z):
    squared = (
        wave_x[:, None, None] * wave_x[:, None, None]
        + wave_y[None, :, None] * wave_y[None, :, None]
        + wave_z[None, None, :] * wave_z[None, None, :]
    )
    factor = NG / (2.0 * math.pi) * (NG / (2.0 * math.pi))
    return jnp.where(squared > 0.5, factor / (squared + SCREEN), jnp.float32(0.0))


def mult(data, table, form):
    return jnp.einsum(form, data, table, preferred_element_type=jnp.float32)


LANES = 128


def exchange_kernel(axes, total, gather, x_ref, o_ref, held, send_sem, recv_sem, own_sem):
    if len(axes) == 2:
        vec_count = lax.axis_size("vec")
        count = lax.axis_size("grid") * vec_count
        me = lax.axis_index("grid") * vec_count + lax.axis_index("vec")
    else:
        count = lax.axis_size(axes[0])
        me = lax.axis_index(axes[0])
    land = held if total else o_ref

    def place(index):
        if len(axes) == 2:
            return (index // vec_count, lax.rem(index, vec_count))
        if axes[0] == "grid":
            return (index, lax.axis_index("vec"))
        return (lax.axis_index("grid"), index)

    def part(index):
        return x_ref if gather else x_ref.at[index]

    barrier = pltpu.get_barrier_semaphore()

    def greet(step, carry):
        pl.semaphore_signal(
            barrier,
            inc=1,
            device_id=place(lax.rem(me + step, count)),
            device_id_type=pl.DeviceIdType.MESH,
        )
        return carry

    lax.fori_loop(1, count, greet, 0)
    own = pltpu.make_async_copy(part(me), land.at[me], own_sem)
    own.start()
    pl.semaphore_wait(barrier, count - 1)

    def copy(step, source, slot):
        peer = lax.rem(me + step, count)
        return pltpu.make_async_remote_copy(
            src_ref=part(source),
            dst_ref=land.at[slot],
            send_sem=send_sem.at[step],
            recv_sem=recv_sem.at[step],
            device_id=place(peer),
            device_id_type=pl.DeviceIdType.MESH,
        )

    def send(step, carry):
        copy(step, lax.rem(me + step, count), me).start()
        return carry

    lax.fori_loop(1, count, send, 0)
    own.wait()

    def receive(step, carry):
        source = lax.rem(me + count - step, count)
        copy(step, source, source).wait_recv()
        return carry

    lax.fori_loop(1, count, receive, 0)
    if total:
        o_ref[...] = jnp.sum(held[...].astype(jnp.float32), axis=0).astype(o_ref.dtype)

    def drain(step, carry):
        copy(step, lax.rem(me + step, count), me).wait_send()
        return carry

    lax.fori_loop(1, count, drain, 0)


def exchange(blocks, ident, total=False, axes=("grid", "vec"), gather=False):
    rows, lanes = blocks.shape[-2:]
    count = 1
    for axis in axes:
        count *= lax.axis_size(axis)
    shape = (rows, lanes) if total else (count, rows, lanes)
    held_shape = blocks.shape if total else (1, 8, LANES)

    def body(*refs):
        exchange_kernel(axes, total, gather, *refs)

    return pl.pallas_call(
        body,
        out_shape=jax.ShapeDtypeStruct(shape, blocks.dtype),
        in_specs=[pl.BlockSpec(memory_space=pltpu.VMEM)],
        out_specs=pl.BlockSpec(memory_space=pltpu.VMEM),
        scratch_shapes=[
            pltpu.VMEM(held_shape, blocks.dtype),
            pltpu.SemaphoreType.DMA((count,)),
            pltpu.SemaphoreType.DMA((count,)),
            pltpu.SemaphoreType.DMA(()),
        ],
        compiler_params=pltpu.CompilerParams(
            collective_id=ident, has_side_effects=True, vmem_limit_bytes=32 << 20
        ),
        name="exchange_total" if total else "exchange_gather" if gather else "exchange_blocks",
    )(blocks)


def share_kernel(chunks, early, refs):
    if early:
        x_ref, panel_ref, orb_ref, o_ref, early_ref, fit_ref = refs[:6]
        orbs, pairs, orb_sem, pair_sem = refs[-4:]
        near, wide, far, sum1, sum2, sum3, sends, recvs, own_sem = refs[6:-4]
    else:
        x_ref, o_ref, near, wide, far, sum1, sum2, sum3, sends, recvs, own_sem = refs
    bf = jnp.bfloat16
    f32 = jnp.float32
    vec_count = lax.axis_size("vec")
    deep = lax.axis_size("grid") // 2
    grid_at, mine = lax.axis_index("grid"), lax.axis_index("vec")
    level, core = grid_at // 2, lax.rem(grid_at, 2)
    other = 1 - core
    across = vec_count - 1

    def partner(step):
        return (level * 2 + other, mine)

    def beside(step):
        return (grid_at, lax.rem(mine + step, vec_count))

    def above(step):
        return (lax.rem(level + step, deep) * 2 + core, mine)

    peers = [partner(1)]
    peers += [beside(step) for step in range(1, vec_count)]
    peers += [above(step) for step in range(1, deep)]
    barrier = pltpu.get_barrier_semaphore()
    for peer in peers:
        pl.semaphore_signal(barrier, inc=1, device_id=peer, device_id_type=pl.DeviceIdType.MESH)
    pl.semaphore_wait(barrier, len(peers))

    def send(source, target, slot, peer):
        return pltpu.make_async_remote_copy(
            src_ref=source,
            dst_ref=target,
            send_sem=sends.at[slot],
            recv_sem=recvs.at[slot],
            device_id=peer,
            device_id_type=pl.DeviceIdType.MESH,
        )

    per_chunk = 2 + 2 * across + 2 * (deep - 1)

    def copies(stage, c):
        base = c * per_chunk
        if stage == 0:
            return [send(x_ref.at[c, other], near.at[c], base, partner(1))]
        if stage == 1:
            return [
                send(
                    sum1.at[c, lax.rem(mine + step, vec_count)],
                    wide.at[c, step - 1],
                    base + step,
                    beside(step),
                )
                for step in range(1, vec_count)
            ]
        if stage == 2:
            return [
                send(
                    sum2.at[c, lax.rem(level + step, deep)],
                    far.at[c, step - 1],
                    base + across + step,
                    above(step),
                )
                for step in range(1, deep)
            ]
        base += across + deep
        if stage == 3:
            spot = o_ref.at[c, core, mine, level]
            return [send(sum3.at[c], spot, base + step - 1, above(step)) for step in range(1, deep)]
        base += deep - 1
        if stage == 4:
            spot = o_ref.at[c, core, mine]
            return [send(spot, spot, base + step - 1, beside(step)) for step in range(1, vec_count)]
        spot = o_ref.at[c, core]
        return [send(spot, spot, base + across, partner(1))]

    def own(c):
        return pltpu.make_async_copy(sum3.at[c], o_ref.at[c, core, mine, level], own_sem.at[c])

    def prepare(stage, c):
        for move in copies(stage - 1, c):
            move.wait_recv()
        if stage == 1:
            sum1[c] = (x_ref[c, core].astype(f32) + near[c].astype(f32)).astype(bf)
        if stage == 2:
            total = sum1[c, mine].astype(f32)
            for step in range(across):
                total += wide[c, step].astype(f32)
            sum2[c] = total.astype(bf)
        if stage == 3:
            total = sum2[c, level].astype(f32)
            for step in range(deep - 1):
                total += far[c, step].astype(f32)
            sum3[c] = total.astype(bf)
            own(c).start()
        if stage == 4:
            own(c).wait()

    def fetch():
        return pltpu.make_async_copy(orb_ref.at[pl.ds(0, early)], orbs, orb_sem)

    def keep(c):
        height = pairs.shape[1] // chunks
        part = pl.ds(c * height, height)
        return pltpu.make_async_copy(
            pairs.at[:, part], early_ref.at[:, part], pair_sem.at[c]
        )

    def multiply(c):
        height = pairs.shape[1] // chunks
        rows = o_ref[c].reshape(height, o_ref.shape[-1])

        def body(e, carry):
            part = lax.dot_general(rows, orbs[e], NT, preferred_element_type=f32)
            pairs[e, c * height : (c + 1) * height, :] = (part * part).astype(bf)
            return carry

        lax.fori_loop(0, early, body, 0)

    if early:
        fetch().start()
    for tick in range(chunks + 6):
        for stage in range(6, -1, -1):
            c = tick - stage
            if 0 <= c < chunks:
                if stage > 0:
                    prepare(stage, c)
                if stage < 6:
                    for move in copies(stage, c):
                        move.start()
        if early and tick >= 6:
            if tick == 6:
                fetch().wait()
            multiply(tick - 6)
            keep(tick - 6).start()
    if early:

        def fit(e, carry):
            fit_ref[e] = lax.dot_general(
                panel_ref[...], pairs[e], NN, preferred_element_type=f32
            )
            return carry

        lax.fori_loop(0, early, fit, 0)
        for c in range(chunks):
            keep(c).wait()
    for c in range(chunks):
        for stage in range(6):
            for move in copies(stage, c):
                move.wait_send()


ROWS = 16


def share_rows(picked, grid_count, vec_count, panel=None, orbitals=None):
    bf = jnp.bfloat16
    npoints, norb = picked.shape
    count = grid_count * vec_count
    if npoints % (count * ROWS) != 0 or grid_count % 2 != 0:
        return lax.psum(picked.astype(jnp.float32), ("grid", "vec")).astype(picked.dtype)
    early = 0 if panel is None else EARLY
    chunks = npoints // (count * ROWS)
    deep = grid_count // 2
    shape = (chunks, 2, vec_count, deep, ROWS, norb)
    slots = chunks * (2 + 2 * (vec_count - 1) + 2 * (deep - 1))
    vmem_spec = pl.BlockSpec(memory_space=pltpu.VMEM)
    any_spec = pl.BlockSpec(memory_space=pl.ANY)
    args = [picked.reshape(shape)]
    in_specs, out_specs = [vmem_spec], [vmem_spec]
    out_shape = [jax.ShapeDtypeStruct(shape, bf)]
    scratch = [
        pltpu.VMEM((chunks, vec_count, deep, ROWS, norb), bf),
        pltpu.VMEM((chunks, vec_count - 1, deep, ROWS, norb), bf),
        pltpu.VMEM((chunks, deep - 1, ROWS, norb), bf),
        pltpu.VMEM((chunks, vec_count, deep, ROWS, norb), bf),
        pltpu.VMEM((chunks, deep, ROWS, norb), bf),
        pltpu.VMEM((chunks, ROWS, norb), bf),
        pltpu.SemaphoreType.DMA((slots,)),
        pltpu.SemaphoreType.DMA((slots,)),
        pltpu.SemaphoreType.DMA((chunks,)),
    ]
    if early:
        cols = panel.shape[0]
        args += [panel, orbitals.reshape(-1, SPAN, norb)]
        in_specs += [vmem_spec, any_spec]
        out_specs += [any_spec, vmem_spec]
        out_shape += [
            jax.ShapeDtypeStruct((early, npoints, SPAN), bf),
            jax.ShapeDtypeStruct((early, cols, SPAN), jnp.float32),
        ]
        scratch += [
            pltpu.VMEM((early, SPAN, norb), bf),
            pltpu.VMEM((early, npoints, SPAN), bf),
            pltpu.SemaphoreType.DMA(()),
            pltpu.SemaphoreType.DMA((chunks,)),
        ]

    def body(*refs):
        share_kernel(chunks, early, refs)

    outs = pl.pallas_call(
        body,
        out_shape=out_shape,
        in_specs=in_specs,
        out_specs=out_specs,
        scratch_shapes=scratch,
        compiler_params=pltpu.CompilerParams(
            collective_id=4, has_side_effects=True, vmem_limit_bytes=46 << 20
        ),
        name="share_rows",
    )(*args)
    rows = outs[0].reshape(npoints, norb)
    return (rows, outs[1], outs[2]) if early else rows


OCTET = 8


def pick_kernel(points_ref, flags_ref, offset_ref, orb_ref, o_ref, found, where, spare, sheet, sem):
    octets, _, norb = orb_ref.shape
    limit = octets * OCTET
    npoints = o_ref.shape[0]
    offset = offset_ref[0]
    sheet[...] = jnp.zeros_like(sheet)

    def fetch(slot, octet):
        return pltpu.make_async_copy(orb_ref.at[octet], found.at[slot], sem)

    def look(i, held):
        position = points_ref[i] - offset
        inside = (position >= 0) & (position < limit)

        @pl.when(inside)
        def _():
            fetch(held, position // OCTET).start()
            where[held] = i
            spare[held] = lax.rem(position, OCTET)

        return held + inside.astype(jnp.int32)

    def scan(group, held):
        return lax.cond(
            flags_ref[group] > 0,
            lambda h: lax.fori_loop(
                0, OCTET, lambda k, n: look(group * OCTET + k, n), h, unroll=True
            ),
            lambda h: h,
            held,
        )

    held = lax.fori_loop(0, npoints // OCTET, scan, 0)

    def settle(slot, carry):
        fetch(slot, 0).wait()
        return carry

    lax.fori_loop(0, held, settle, 0)
    line = lax.broadcasted_iota(jnp.int32, (OCTET, norb), 0)

    def place(slot, carry):
        octet = found[slot].astype(jnp.float32)
        row = jnp.sum(jnp.where(line == spare[slot], octet, 0.0), axis=0, keepdims=True)
        sheet[pl.ds(where[slot], 1), :] = row
        return carry

    lax.fori_loop(0, held, place, 0)
    o_ref[...] = sheet[...].astype(o_ref.dtype)


def pick_rows(orbitals, points, offset):
    rows, norb = orbitals.shape
    npoints = points.shape[0]
    position = points - offset
    if rows % OCTET != 0 or npoints % OCTET != 0:
        inside = (position >= 0) & (position < rows)
        picked = jnp.take(orbitals, jnp.clip(position, 0, rows - 1), axis=0)
        return jnp.where(inside[:, None], picked, jnp.zeros_like(picked))
    inside = (position >= 0) & (position < rows)
    flags = jnp.max(inside.reshape(-1, OCTET).astype(jnp.int32), axis=1)
    return pl.pallas_call(
        pick_kernel,
        out_shape=jax.ShapeDtypeStruct((npoints, norb), orbitals.dtype),
        in_specs=[
            pl.BlockSpec(memory_space=pltpu.SMEM),
            pl.BlockSpec(memory_space=pltpu.SMEM),
            pl.BlockSpec(memory_space=pltpu.SMEM),
            pl.BlockSpec(memory_space=pl.ANY),
        ],
        out_specs=pl.BlockSpec(memory_space=pltpu.VMEM),
        scratch_shapes=[
            pltpu.VMEM((npoints, OCTET, norb), orbitals.dtype),
            pltpu.SMEM((npoints,), jnp.int32),
            pltpu.SMEM((npoints,), jnp.int32),
            pltpu.VMEM((npoints, norb), jnp.float32),
            pltpu.SemaphoreType.DMA(()),
        ],
        compiler_params=pltpu.CompilerParams(vmem_limit_bytes=28 << 20),
        name="pick_rows",
    )(points, flags, offset[None].astype(jnp.int32), orbitals.reshape(rows // OCTET, OCTET, norb))


def project(pair, pot_rows):
    scale = 1.0 / math.sqrt(float(NG**3))
    term = lax.dot_general(
        pair, pot_rows, (((0,), (1,)), ((), ())), preferred_element_type=jnp.float32
    )
    term = term * jnp.float32(scale)
    npoints, cols = term.shape
    count = lax.axis_size("grid") * lax.axis_size("vec")
    share = npoints // count
    if share * cols % LANES == 0:
        blocks = term.reshape(count, share * cols // LANES, LANES)
        return exchange(blocks, 3, True).reshape(share, cols)
    partial_block = lax.psum_scatter(term, "grid", scatter_dimension=0, tiled=True)
    return lax.psum_scatter(partial_block, "vec", scatter_dimension=0, tiled=True)


def peers_of():
    vec_count = lax.axis_size("vec")
    count = lax.axis_size("grid") * vec_count
    me = lax.axis_index("grid") * vec_count + lax.axis_index("vec")

    def place(index):
        return (index // vec_count, lax.rem(index, vec_count))

    return count, me, place


def greet_all(count, me, place):
    barrier = pltpu.get_barrier_semaphore()

    def greet(step, carry):
        pl.semaphore_signal(
            barrier,
            inc=1,
            device_id=place(lax.rem(me + step, count)),
            device_id_type=pl.DeviceIdType.MESH,
        )
        return carry

    lax.fori_loop(1, count, greet, 0)


def wait_greeted(count):
    pl.semaphore_wait(pltpu.get_barrier_semaphore(), count - 1)


NT = (((1,), (1,)), ((), ()))
NN = (((1,), (0,)), ((), ()))
LINES = 16
SPAN = LINES * NG
TAKE = 512
JOIN = 3
EARLY = 4


def pair_fit_kernel(
    orb_ref, rows_ref, panel_ref, early_ref, pair_ref, field_ref, fit_buf, fit_rows, out_buf,
    send_sem, recv_sem, own_sem,
):
    bf = jnp.bfloat16
    block = pl.program_id(0) + EARLY
    blocks = pl.num_programs(0) + EARLY
    count, me, place = peers_of()
    npoints = rows_ref.shape[0]
    cols = panel_ref.shape[0]
    per_plane = NG // LINES
    groups = blocks // JOIN
    tall = JOIN * LINES

    def send(group, begin, lines):
        slot = lax.rem(group, 2)
        start = pl.multiple_of(lax.rem(group * JOIN, per_plane) * LINES + begin, LINES)
        target = field_ref.at[me, group * JOIN // per_plane, pl.ds(start, lines)]

        def body(step, carry):
            peer = lax.rem(me + step, count)
            pltpu.make_async_remote_copy(
                src_ref=out_buf.at[slot, peer, pl.ds(begin, lines)],
                dst_ref=target,
                send_sem=send_sem.at[slot],
                recv_sem=recv_sem.at[me],
                device_id=place(peer),
                device_id_type=pl.DeviceIdType.MESH,
            ).start()
            return carry

        pltpu.make_async_copy(
            out_buf.at[slot, me, pl.ds(begin, lines)], target, own_sem.at[slot]
        ).start()
        lax.fori_loop(1, count, body, 0, unroll=True)

    def drain(group):
        slot = lax.rem(group, 2)
        sent = out_buf.at[slot, pl.ds(0, count - 1)]
        mine = out_buf.at[slot, me]
        pltpu.make_async_copy(mine, mine, own_sem.at[slot]).wait()
        pltpu.make_async_copy(sent, sent, send_sem.at[slot]).wait()

    @pl.when(block == EARLY)
    def _():
        greet_all(count, me, place)

    before = block - 1

    @pl.when((block > 2 * JOIN) & (lax.rem(before, JOIN) == 0))
    def _():
        drain(before // JOIN - 2)

    def multiply(first):
        part = lax.dot_general(
            rows_ref[first : first + TAKE, :], orb_ref[...], NT, preferred_element_type=jnp.float32
        )
        pair_ref[0, first : first + TAKE, :] = (part * part).astype(bf)

    def arrange(index):
        for line in range(LINES):
            begin = line * NG
            low = begin // LANES * LANES
            turn = begin - low
            wide = fit_buf[:, low : min(low + 2 * LANES, SPAN)]
            if wide.shape[1] == LANES:
                wide = jnp.concatenate([wide, wide], axis=1)
            if turn:
                wide = pltpu.roll(wide, 2 * LANES - turn, 1)
            fit_rows[pl.ds(line, cols, stride=LINES), :] = wide[:, :LANES]
        slot = index // JOIN % 2
        begin = index % JOIN * LINES
        if not isinstance(index, int):
            begin = pl.multiple_of(begin, LINES)
        out_buf[slot, :, pl.ds(begin, LINES), :] = (
            fit_rows[...].astype(bf).reshape(cols, LINES, LANES)
        )

    @pl.when(block == EARLY)
    def _():
        for index in range(EARLY - 1):
            fit_buf[...] = early_ref[index]
            arrange(index)
        fit_buf[...] = early_ref[EARLY - 1]

    multiply(0)
    arrange(before)
    for first in range(TAKE, npoints // 2, TAKE):
        multiply(first)

    @pl.when(block == EARLY)
    def _():
        wait_greeted(count)
        send(0, 0, tall)

    @pl.when((block > EARLY) & (lax.rem(block, JOIN) == 0))
    def _():
        send(block // JOIN - 1, 0, tall)

    for late in range(JOIN - 1):

        @pl.when(block == blocks - JOIN + 1 + late)
        def _(late=late):
            send(groups - 1, late * LINES, LINES)

    for first in range(npoints // 2, npoints, TAKE):
        multiply(first)
    fit_buf[...] = lax.dot_general(
        panel_ref[...], pair_ref[0], NN, preferred_element_type=jnp.float32
    )

    @pl.when(block == blocks - 1)
    def _():
        arrange(block)
        send(groups - 1, (JOIN - 1) * LINES, LINES)

        def receive(step, carry):
            source = lax.rem(me + count - step, count)
            land = field_ref.at[source]
            pltpu.make_async_copy(land, land, recv_sem.at[source]).wait()
            return carry

        lax.fori_loop(1, count, receive, 0)
        drain(groups - 2)
        drain(groups - 1)


def pair_and_fit(orbitals, point_rows, panel, early_fit):
    bf = jnp.bfloat16
    rows, norb = orbitals.shape
    npoints = point_rows.shape[0]
    cols = panel.shape[0]
    blocks = rows // SPAN - EARLY
    planes = rows // (NG * NG)
    count = lax.axis_size("grid") * lax.axis_size("vec")
    return pl.pallas_call(
        pair_fit_kernel,
        grid=(blocks,),
        in_specs=[
            pl.BlockSpec((SPAN, norb), lambda i: (i + EARLY, 0)),
            pl.BlockSpec((npoints, norb), lambda i: (0, 0)),
            pl.BlockSpec((cols, npoints), lambda i: (0, 0)),
            pl.BlockSpec((EARLY, cols, SPAN), lambda i: (0, 0, 0)),
        ],
        out_specs=[
            pl.BlockSpec((1, npoints, SPAN), lambda i: (i, 0, 0)),
            pl.BlockSpec(memory_space=pl.ANY),
        ],
        out_shape=[
            jax.ShapeDtypeStruct((blocks, npoints, SPAN), bf),
            jax.ShapeDtypeStruct((count, planes, NG, LANES), bf),
        ],
        scratch_shapes=[
            pltpu.VMEM((cols, SPAN), jnp.float32),
            pltpu.VMEM((cols * LINES, LANES), jnp.float32),
            pltpu.VMEM((2, cols, JOIN * LINES, LANES), bf),
            pltpu.SemaphoreType.DMA((2,)),
            pltpu.SemaphoreType.DMA((count,)),
            pltpu.SemaphoreType.DMA((2,)),
        ],
        compiler_params=pltpu.CompilerParams(
            collective_id=1, has_side_effects=True, vmem_limit_bytes=36 << 20
        ),
        name="pair_fit_send",
    )(orbitals, point_rows, panel, early_fit)


GROUP = 24
HALF = 64
PIECE = NG * NG // LANES // 3
RING = EARLY


def solve_project_kernel(
    field_ref, tz_ref, ty_ref, tyi_ref, tzi_ref, early_ref, pair_ref, o_ref,
    field, by_y, by_x, flat, dense, pot, ring, land, wide, total, parts, held,
    field_sem, send_sem, recv_sem, own_sem, pair_sem, part_send, part_recv,
):
    bf = jnp.bfloat16
    f32 = jnp.float32
    count, me, place = peers_of()
    rest, npoints, _ = pair_ref.shape
    blocks = rest + EARLY
    pieces = pot.shape[0]
    cols = count
    share = npoints // count
    planes = NG // count
    per_piece = blocks // pieces
    strips = SPAN // LANES

    def load(step):
        part = pl.ds(step * GROUP, GROUP)
        return pltpu.make_async_copy(field_ref.at[part], field.at[part], field_sem.at[step])

    def fetch(ref, block):
        slot = lax.rem(block, RING)
        return pltpu.make_async_copy(ref.at[block], ring.at[slot], pair_sem.at[slot])

    for step in range(NG // GROUP):
        load(step).start()
    greet_all(count, me, place)

    lane = lax.broadcasted_iota(jnp.int32, (NG, LANES), 1)
    row = lax.broadcasted_iota(jnp.int32, (NG, LANES), 0)
    sign = jnp.where(lane < HALF, 1.0, -1.0).astype(f32)
    wave_z = lax.rem(lane, HALF).astype(f32)
    wave_x = jnp.where(row < NG // 2, row, row - NG).astype(f32)
    plane_sq = wave_x * wave_x + wave_z * wave_z
    factor = NG / (2.0 * math.pi) * (NG / (2.0 * math.pi))

    def both(shapes):
        top = jnp.concatenate([part.astype(bf) for part in shapes], axis=1)
        turned = [(pltpu.roll(part, HALF, 1) * sign).astype(bf) for part in shapes]
        return jnp.concatenate([top, jnp.concatenate(turned, axis=1)], axis=0)

    def cut(sheet, k):
        return sheet[:, k * LANES : (k + 1) * LANES]

    def forward(step, carry):
        first = step * GROUP
        load(step).wait()
        data = field[pl.ds(first, GROUP)].reshape(GROUP * NG, LANES)
        a = lax.dot_general(data, tz_ref[...], NN, preferred_element_type=f32).astype(bf)
        top = [a[k * NG : (k + 1) * NG, :LANES] for k in range(GROUP)]
        low = [a[k * NG : (k + 1) * NG, LANES:] for k in range(GROUP)]
        stack = jnp.concatenate(
            [jnp.concatenate(top, axis=1), jnp.concatenate(low, axis=1)], axis=0
        )
        b = lax.dot_general(ty_ref[...], stack, NN, preferred_element_type=f32)
        for k in range(GROUP):
            by_y[pl.ds(first + k, NG, stride=NG), :] = cut(b, k)
        return carry

    lax.fori_loop(0, NG // GROUP, forward, 0)

    def prime(block, carry):
        fetch(early_ref, block).start()
        return carry

    lax.fori_loop(0, EARLY, prime, 0)

    def middle(step, carry):
        first = step * GROUP
        rows = [by_y[pl.ds((first + k) * NG, NG), :] for k in range(GROUP)]
        h = lax.dot_general(ty_ref[...], both(rows), NN, preferred_element_type=f32)
        scaled = []
        for k in range(GROUP):
            index = first + k
            wave_y = jnp.where(index < NG // 2, index, index - NG).astype(f32)
            squared = plane_sq + wave_y * wave_y
            kernel = jnp.where(squared > 0.5, factor / (squared + SCREEN), 0.0)
            scaled.append(cut(h, k) * kernel)
        g = lax.dot_general(tyi_ref[...], both(scaled), NN, preferred_element_type=f32)
        for k in range(GROUP):
            by_x[pl.ds(first + k, NG, stride=NG), :] = cut(g, k)
        return carry

    lax.fori_loop(0, NG // GROUP, middle, 0)
    wait_greeted(count)

    def own(piece):
        return pltpu.make_async_copy(pot.at[piece, me], land.at[piece, me], own_sem.at[piece])

    def send_piece(piece):
        def body(step, carry):
            peer = lax.rem(me + step, count)
            pltpu.make_async_remote_copy(
                src_ref=pot.at[piece, peer],
                dst_ref=land.at[piece, me],
                send_sem=send_sem.at[piece],
                recv_sem=recv_sem.at[piece],
                device_id=place(peer),
                device_id_type=pl.DeviceIdType.MESH,
            ).start()
            return carry

        own(piece).start()
        lax.fori_loop(1, count, body, 0)

    quarter = NG // 4
    spot = lane[:quarter]

    def backward(local, carry):
        rows = [by_x[pl.ds((local + planes * k) * NG, NG), :] for k in range(count)]
        p = lax.dot_general(tyi_ref[...], both(rows), NN, preferred_element_type=f32).astype(bf)
        tall = jnp.concatenate([cut(p, k) for k in range(count)], axis=0)
        final = lax.dot_general(tall, tzi_ref[...], NN, preferred_element_type=f32)
        flat[...] = final * f32(1.0 / float(NG**3))
        for k in range(count):
            y0, y1, y2, y3 = [flat[pl.ds(k * NG + j, quarter, stride=4), :] for j in range(4)]
            y1, y2, y3 = pltpu.roll(y1, 96, 1), pltpu.roll(y2, 64, 1), pltpu.roll(y3, 32, 1)
            base = k % 4 * 3 * PIECE
            dense[pl.ds(base, quarter, stride=3), :] = jnp.where(spot < 96, y0, y1)
            dense[pl.ds(base + 1, quarter, stride=3), :] = jnp.where(spot < 64, y1, y2)
            dense[pl.ds(base + 2, quarter, stride=3), :] = jnp.where(spot < 32, y2, y3)
            for m in range(3):
                pot[local * 3 + m, k] = dense[base + m * PIECE : base + (m + 1) * PIECE, :].astype(bf)
        for m in range(3):
            send_piece(local * 3 + m)
        return carry

    lax.fori_loop(0, planes, backward, 0)
    total[...] = jnp.zeros_like(total)

    def work(piece, carry):
        own(piece).wait()
        others = land.at[piece, pl.ds(0, count - 1)]
        pltpu.make_async_copy(others, others, recv_sem.at[piece]).wait()
        wide[...] = land[piece].astype(f32).reshape(cols * PIECE, LANES)
        for half in range(per_piece):
            block = piece * per_piece + half
            slot = lax.rem(block, RING)
            pltpu.make_async_copy(ring.at[slot], ring.at[slot], pair_sem.at[slot]).wait()
            lines = [
                wide[pl.ds(half * strips + j, cols, stride=PIECE), :].astype(bf)
                for j in range(strips)
            ]
            total[...] += lax.dot_general(
                jnp.concatenate(lines, axis=1), ring[slot], NT, preferred_element_type=f32
            )

            @pl.when(block < rest)
            def _():
                fetch(pair_ref, block).start()

        return carry

    lax.fori_loop(0, pieces, work, 0)

    scale = f32(1.0 / math.sqrt(float(NG**3)))
    low_lane = lax.broadcasted_iota(jnp.int32, (cols // 2, LANES), 1) < share
    for k in range(npoints // LANES):
        tile = total[:, k * LANES : (k + 1) * LANES] * scale
        top, low = tile[: cols // 2], tile[cols // 2 :]
        parts[2 * k] = jnp.where(low_lane, top, pltpu.roll(low, share, 1))
        parts[2 * k + 1] = jnp.where(low_lane, pltpu.roll(top, share, 1), low)

    def part_copy(step, source, slot):
        peer = lax.rem(me + step, count)
        return pltpu.make_async_remote_copy(
            src_ref=parts.at[source],
            dst_ref=held.at[slot],
            send_sem=part_send.at[step],
            recv_sem=part_recv.at[step],
            device_id=place(peer),
            device_id_type=pl.DeviceIdType.MESH,
        )

    def part_start(step, carry):
        part_copy(step, lax.rem(me + step, count), me).start()
        return carry

    lax.fori_loop(1, count, part_start, 0)
    held[me] = parts[me]

    def drain_piece(piece, carry):
        sent = pot.at[piece, pl.ds(0, count - 1)]
        pltpu.make_async_copy(sent, sent, send_sem.at[piece]).wait()
        return carry

    lax.fori_loop(0, pieces, drain_piece, 0)

    def part_receive(step, carry):
        source = lax.rem(me + count - step, count)
        part_copy(step, source, source).wait_recv()
        return carry

    lax.fori_loop(1, count, part_receive, 0)
    summed = jnp.sum(held[...], axis=0)
    pile = jnp.concatenate([summed, pltpu.roll(summed, share, 1)], axis=0)
    o_ref[...] = pile.T[:share, :]

    def part_drain(step, carry):
        part_copy(step, lax.rem(me + step, count), me).wait_send()
        return carry

    lax.fori_loop(1, count, part_drain, 0)


def solve_and_project(field, early, pair, count):
    bf = jnp.bfloat16
    f32 = jnp.float32
    cos_tab, sin_tab = literal_tables(NG)
    keep = NG // 2 + 1

    def padded(table):
        return np.pad(table[:, :keep], ((0, LANES - NG), (0, HALF - keep)))

    cz, sz = padded(cos_tab), padded(sin_tab)
    tz = np.concatenate([cz, -sz, -sz, -cz], axis=1)
    ty = np.concatenate([cos_tab, sin_tab], axis=1)
    tyi = np.concatenate([cos_tab, -sin_tab], axis=1)
    spot = np.arange(HALF)[:, None]
    weight = np.where((spot == 0) | (spot == NG // 2), 1.0, 2.0).astype(bf)
    tzi = np.concatenate([cz.T * weight, -(sz.T * weight)], axis=0)
    tz, ty, tyi, tzi = [jnp.asarray(table, bf) for table in (tz, ty, tyi, tzi)]
    pieces = NG // count * 3
    blocks, npoints, span = pair.shape
    cols = count
    any_spec = pl.BlockSpec(memory_space=pl.ANY)
    vmem_spec = pl.BlockSpec(memory_space=pltpu.VMEM)
    return pl.pallas_call(
        solve_project_kernel,
        out_shape=jax.ShapeDtypeStruct((npoints // count, cols), f32),
        in_specs=[any_spec] + [vmem_spec] * 4 + [any_spec] * 2,
        out_specs=vmem_spec,
        scratch_shapes=[
            pltpu.VMEM((NG, NG, LANES), bf),
            pltpu.VMEM((NG * NG, LANES), f32),
            pltpu.VMEM((NG * NG, LANES), f32),
            pltpu.VMEM((count * NG, LANES), f32),
            pltpu.VMEM((4 * 3 * PIECE, LANES), f32),
            pltpu.VMEM((pieces, count, PIECE, LANES), bf),
            pltpu.VMEM((RING, npoints, span), bf),
            pltpu.VMEM((pieces, count, PIECE, LANES), bf),
            pltpu.VMEM((cols * PIECE, LANES), f32),
            pltpu.VMEM((cols, npoints), f32),
            pltpu.VMEM((count, cols // 2, LANES), f32),
            pltpu.VMEM((count, cols // 2, LANES), f32),
            pltpu.SemaphoreType.DMA((NG // GROUP,)),
            pltpu.SemaphoreType.DMA((pieces,)),
            pltpu.SemaphoreType.DMA((pieces,)),
            pltpu.SemaphoreType.DMA((pieces,)),
            pltpu.SemaphoreType.DMA((RING,)),
            pltpu.SemaphoreType.DMA((count,)),
            pltpu.SemaphoreType.DMA((count,)),
        ],
        compiler_params=pltpu.CompilerParams(
            collective_id=2, has_side_effects=True, vmem_limit_bytes=54 << 20
        ),
        name="solve_project",
    )(field.reshape(NG, NG, LANES), tz, ty, tyi, tzi, early, pair)


def fits_planes(rows, npoints, cols, count):
    blocks = rows // SPAN
    return (
        cols == count
        and rows % (NG * NG) == 0
        and NG % (rows // (NG * NG)) == 0
        and blocks >= EARLY + 2 * JOIN
        and EARLY > JOIN
        and npoints % (count * ROWS) == 0
        and NG // LINES % JOIN == 0
        and npoints % TAKE == 0
        and 2 * npoints == count * LANES
    )


def shards(orbitals, inverse_panel, points):
    bf = jnp.bfloat16
    row_count = orbitals.shape[0]
    grid_count = lax.axis_size("grid")
    vec_count = lax.axis_size("vec")
    npoints = points.shape[0]
    offset = (lax.axis_index("grid") * vec_count + lax.axis_index("vec")) * row_count
    picked = pick_rows(orbitals, points, offset)
    cols = inverse_panel.shape[1]
    if fits_planes(row_count, npoints, cols, grid_count * vec_count):
        panel = inverse_panel.T
        point_rows, early, early_fit = share_rows(picked, grid_count, vec_count, panel, orbitals)
        pair, field = pair_and_fit(orbitals, point_rows, panel, early_fit)
        return solve_and_project(field, early, pair, grid_count * vec_count)
    point_rows = share_rows(picked, grid_count, vec_count)

    def pair_block(block):
        correlation = lax.dot_general(
            block, point_rows, (((1,), (1,)), ((), ())), preferred_element_type=jnp.float32
        )
        return (correlation * correlation).astype(bf)

    pair = lax.map(pair_block, orbitals.reshape(4, row_count // 4, orbitals.shape[1])).reshape(
        row_count, npoints
    )
    fit_cols = lax.dot_general(
        inverse_panel, pair, (((0,), (1,)), ((), ())), preferred_element_type=jnp.float32
    ).astype(bf)
    slab = lax.all_to_all(fit_cols, "vec", split_axis=0, concat_axis=1, tiled=True)
    col_local = slab.shape[0]
    planes = NG // grid_count
    field = slab.reshape(col_local, planes, NG, NG)
    cos_tab, sin_tab = wave_tables(NG)
    z_re = mult(field, cos_tab, "vxyz,zk->vxyk").astype(bf)
    z_im = (-mult(field, sin_tab, "vxyz,zk->vxyk")).astype(bf)
    y_re = (mult(z_re, cos_tab, "vxyz,yk->vxkz") + mult(z_im, sin_tab, "vxyz,yk->vxkz")).astype(bf)
    y_im = (mult(z_im, cos_tab, "vxyz,yk->vxkz") - mult(z_re, sin_tab, "vxyz,yk->vxkz")).astype(bf)
    stacked = jnp.stack([y_re, y_im])
    waves = wavenumber(lax.iota(jnp.int32, NG), NG)
    y_waves = wavenumber(lax.axis_index("grid") * planes + lax.iota(jnp.int32, planes), NG)
    kernel = screened(waves, y_waves, waves)[None]
    piece = lax.all_to_all(stacked, "grid", split_axis=3, concat_axis=2, tiled=True)
    p_re = piece[0]
    p_im = piece[1]
    x_re = mult(p_re, cos_tab, "vxyz,xk->vkyz") + mult(p_im, sin_tab, "vxyz,xk->vkyz")
    x_im = mult(p_im, cos_tab, "vxyz,xk->vkyz") - mult(p_re, sin_tab, "vxyz,xk->vkyz")
    q_re = (x_re * kernel).astype(bf)
    q_im = (x_im * kernel).astype(bf)
    i_re = (mult(q_re, cos_tab, "vxyz,xk->vkyz") - mult(q_im, sin_tab, "vxyz,xk->vkyz")).astype(bf)
    i_im = (mult(q_im, cos_tab, "vxyz,xk->vkyz") + mult(q_re, sin_tab, "vxyz,xk->vkyz")).astype(bf)
    spectrum = lax.all_to_all(
        jnp.stack([i_re, i_im]), "grid", split_axis=2, concat_axis=3, tiled=True
    )
    s_re = spectrum[0]
    s_im = spectrum[1]
    h_re = (mult(s_re, cos_tab, "vxyz,yk->vxkz") - mult(s_im, sin_tab, "vxyz,yk->vxkz")).astype(bf)
    h_im = (mult(s_im, cos_tab, "vxyz,yk->vxkz") + mult(s_re, sin_tab, "vxyz,yk->vxkz")).astype(bf)
    final = mult(h_re, cos_tab, "vxyz,zk->vxyk") - mult(h_im, sin_tab, "vxyz,zk->vxyk")
    potential = (final / float(NG**3)).astype(bf).reshape(col_local, planes * NG * NG)
    pot_rows = lax.all_to_all(potential, "vec", split_axis=1, concat_axis=0, tiled=True)
    return project(pair, pot_rows)


def solution(mesh):
    in_specs = (P(("grid", "vec"), None), P(), P())
    out_specs = P(("grid", "vec"), None)
    return jax.shard_map(shards, mesh=mesh, in_specs=in_specs, out_specs=out_specs, check_vma=False)
```

```python
import math

import jax
import jax.numpy as jnp
import numpy as np
from jax import lax
from jax.experimental import pallas as pl
from jax.experimental.pallas import tpu as pltpu
from jax.sharding import PartitionSpec as P

NG = 96


SCREEN = 2.25


def wave_tables(count):
    index = lax.iota(jnp.int32, count)
    phase = index[:, None] * index[None, :] % count
    angle = phase.astype(jnp.float32) * (2.0 * math.pi / count)
    return (jnp.cos(angle).astype(jnp.bfloat16), jnp.sin(angle).astype(jnp.bfloat16))


def literal_tables(count):
    index = np.arange(count)
    phase = index[:, None] * index[None, :] % count
    angle = phase.astype(np.float32) * np.float32(2.0 * math.pi / count)
    return np.cos(angle).astype(jnp.bfloat16), np.sin(angle).astype(jnp.bfloat16)


def wavenumber(index, count):
    return jnp.where(index < count // 2, index, index - count).astype(jnp.float32)


def screened(wave_x, wave_y, wave_z):
    squared = (
        wave_x[:, None, None] * wave_x[:, None, None]
        + wave_y[None, :, None] * wave_y[None, :, None]
        + wave_z[None, None, :] * wave_z[None, None, :]
    )
    factor = NG / (2.0 * math.pi) * (NG / (2.0 * math.pi))
    return jnp.where(squared > 0.5, factor / (squared + SCREEN), jnp.float32(0.0))


def mult(data, table, form):
    return jnp.einsum(form, data, table, preferred_element_type=jnp.float32)


LANES = 128


def exchange_kernel(axes, total, gather, x_ref, o_ref, held, send_sem, recv_sem, own_sem):
    if len(axes) == 2:
        vec_count = lax.axis_size("vec")
        count = lax.axis_size("grid") * vec_count
        me = lax.axis_index("grid") * vec_count + lax.axis_index("vec")
    else:
        count = lax.axis_size(axes[0])
        me = lax.axis_index(axes[0])
    land = held if total else o_ref

    def place(index):
        if len(axes) == 2:
            return (index // vec_count, lax.rem(index, vec_count))
        if axes[0] == "grid":
            return (index, lax.axis_index("vec"))
        return (lax.axis_index("grid"), index)

    def part(index):
        return x_ref if gather else x_ref.at[index]

    barrier = pltpu.get_barrier_semaphore()

    def greet(step, carry):
        pl.semaphore_signal(
            barrier,
            inc=1,
            device_id=place(lax.rem(me + step, count)),
            device_id_type=pl.DeviceIdType.MESH,
        )
        return carry

    lax.fori_loop(1, count, greet, 0)
    own = pltpu.make_async_copy(part(me), land.at[me], own_sem)
    own.start()
    pl.semaphore_wait(barrier, count - 1)

    def copy(step, source, slot):
        peer = lax.rem(me + step, count)
        return pltpu.make_async_remote_copy(
            src_ref=part(source),
            dst_ref=land.at[slot],
            send_sem=send_sem.at[step],
            recv_sem=recv_sem.at[step],
            device_id=place(peer),
            device_id_type=pl.DeviceIdType.MESH,
        )

    def send(step, carry):
        copy(step, lax.rem(me + step, count), me).start()
        return carry

    lax.fori_loop(1, count, send, 0)
    own.wait()

    def receive(step, carry):
        source = lax.rem(me + count - step, count)
        copy(step, source, source).wait_recv()
        return carry

    lax.fori_loop(1, count, receive, 0)
    if total:
        o_ref[...] = jnp.sum(held[...].astype(jnp.float32), axis=0).astype(o_ref.dtype)

    def drain(step, carry):
        copy(step, lax.rem(me + step, count), me).wait_send()
        return carry

    lax.fori_loop(1, count, drain, 0)


def exchange(blocks, ident, total=False, axes=("grid", "vec"), gather=False):
    rows, lanes = blocks.shape[-2:]
    count = 1
    for axis in axes:
        count *= lax.axis_size(axis)
    shape = (rows, lanes) if total else (count, rows, lanes)
    held_shape = blocks.shape if total else (1, 8, LANES)

    def body(*refs):
        exchange_kernel(axes, total, gather, *refs)

    return pl.pallas_call(
        body,
        out_shape=jax.ShapeDtypeStruct(shape, blocks.dtype),
        in_specs=[pl.BlockSpec(memory_space=pltpu.VMEM)],
        out_specs=pl.BlockSpec(memory_space=pltpu.VMEM),
        scratch_shapes=[
            pltpu.VMEM(held_shape, blocks.dtype),
            pltpu.SemaphoreType.DMA((count,)),
            pltpu.SemaphoreType.DMA((count,)),
            pltpu.SemaphoreType.DMA(()),
        ],
        compiler_params=pltpu.CompilerParams(
            collective_id=ident, has_side_effects=True, vmem_limit_bytes=32 << 20
        ),
        name="exchange_total" if total else "exchange_gather" if gather else "exchange_blocks",
    )(blocks)


def share_kernel(chunks, early, refs):
    if early:
        x_ref, panel_ref, orb_ref, o_ref, early_ref, fit_ref = refs[:6]
        orbs, pairs, orb_sem, pair_sem = refs[-4:]
        near, wide, far, sum1, sum2, sum3, sends, recvs, own_sem = refs[6:-4]
    else:
        x_ref, o_ref, near, wide, far, sum1, sum2, sum3, sends, recvs, own_sem = refs
    bf = jnp.bfloat16
    f32 = jnp.float32
    vec_count = lax.axis_size("vec")
    deep = lax.axis_size("grid") // 2
    grid_at, mine = lax.axis_index("grid"), lax.axis_index("vec")
    level, core = grid_at // 2, lax.rem(grid_at, 2)
    other = 1 - core
    across = vec_count - 1

    def partner(step):
        return (level * 2 + other, mine)

    def beside(step):
        return (grid_at, lax.rem(mine + step, vec_count))

    def above(step):
        return (lax.rem(level + step, deep) * 2 + core, mine)

    peers = [partner(1)]
    peers += [beside(step) for step in range(1, vec_count)]
    peers += [above(step) for step in range(1, deep)]
    barrier = pltpu.get_barrier_semaphore()
    for peer in peers:
        pl.semaphore_signal(barrier, inc=1, device_id=peer, device_id_type=pl.DeviceIdType.MESH)
    pl.semaphore_wait(barrier, len(peers))

    def send(source, target, slot, peer):
        return pltpu.make_async_remote_copy(
            src_ref=source,
            dst_ref=target,
            send_sem=sends.at[slot],
            recv_sem=recvs.at[slot],
            device_id=peer,
            device_id_type=pl.DeviceIdType.MESH,
        )

    per_chunk = 2 + 2 * across + 2 * (deep - 1)

    def copies(stage, c):
        base = c * per_chunk
        if stage == 0:
            return [send(x_ref.at[c, other], near.at[c], base, partner(1))]
        if stage == 1:
            return [
                send(
                    sum1.at[c, lax.rem(mine + step, vec_count)],
                    wide.at[c, step - 1],
                    base + step,
                    beside(step),
                )
                for step in range(1, vec_count)
            ]
        if stage == 2:
            return [
                send(
                    sum2.at[c, lax.rem(level + step, deep)],
                    far.at[c, step - 1],
                    base + across + step,
                    above(step),
                )
                for step in range(1, deep)
            ]
        base += across + deep
        if stage == 3:
            spot = o_ref.at[c, core, mine, level]
            return [send(sum3.at[c], spot, base + step - 1, above(step)) for step in range(1, deep)]
        base += deep - 1
        if stage == 4:
            spot = o_ref.at[c, core, mine]
            return [send(spot, spot, base + step - 1, beside(step)) for step in range(1, vec_count)]
        spot = o_ref.at[c, core]
        return [send(spot, spot, base + across, partner(1))]

    def own(c):
        return pltpu.make_async_copy(sum3.at[c], o_ref.at[c, core, mine, level], own_sem.at[c])

    def prepare(stage, c):
        for move in copies(stage - 1, c):
            move.wait_recv()
        if stage == 1:
            sum1[c] = (x_ref[c, core].astype(f32) + near[c].astype(f32)).astype(bf)
        if stage == 2:
            total = sum1[c, mine].astype(f32)
            for step in range(across):
                total += wide[c, step].astype(f32)
            sum2[c] = total.astype(bf)
        if stage == 3:
            total = sum2[c, level].astype(f32)
            for step in range(deep - 1):
                total += far[c, step].astype(f32)
            sum3[c] = total.astype(bf)
            own(c).start()
        if stage == 4:
            own(c).wait()

    def fetch():
        return pltpu.make_async_copy(orb_ref.at[pl.ds(0, early)], orbs, orb_sem)

    def keep(c):
        height = pairs.shape[1] // chunks
        part = pl.ds(c * height, height)
        return pltpu.make_async_copy(
            pairs.at[:, part], early_ref.at[:, part], pair_sem.at[c]
        )

    def multiply(c):
        height = pairs.shape[1] // chunks
        rows = o_ref[c].reshape(height, o_ref.shape[-1])

        def body(e, carry):
            part = lax.dot_general(rows, orbs[e], NT, preferred_element_type=f32)
            pairs[e, c * height : (c + 1) * height, :] = (part * part).astype(bf)
            return carry

        lax.fori_loop(0, early, body, 0)

    if early:
        fetch().start()
    for tick in range(chunks + 6):
        for stage in range(6, -1, -1):
            c = tick - stage
            if 0 <= c < chunks:
                if stage > 0:
                    prepare(stage, c)
                if stage < 6:
                    for move in copies(stage, c):
                        move.start()
        if early and tick >= 6:
            if tick == 6:
                fetch().wait()
            multiply(tick - 6)
            keep(tick - 6).start()
    if early:

        def fit(e, carry):
            fit_ref[e] = lax.dot_general(
                panel_ref[...], pairs[e], NN, preferred_element_type=f32
            )
            return carry

        lax.fori_loop(0, early, fit, 0)
        for c in range(chunks):
            keep(c).wait()
    for c in range(chunks):
        for stage in range(6):
            for move in copies(stage, c):
                move.wait_send()


ROWS = 16


def share_rows(picked, grid_count, vec_count, panel=None, orbitals=None):
    bf = jnp.bfloat16
    npoints, norb = picked.shape
    count = grid_count * vec_count
    if npoints % (count * ROWS) != 0 or grid_count % 2 != 0:
        return lax.psum(picked.astype(jnp.float32), ("grid", "vec")).astype(picked.dtype)
    early = 0 if panel is None else EARLY
    chunks = npoints // (count * ROWS)
    deep = grid_count // 2
    shape = (chunks, 2, vec_count, deep, ROWS, norb)
    slots = chunks * (2 + 2 * (vec_count - 1) + 2 * (deep - 1))
    vmem_spec = pl.BlockSpec(memory_space=pltpu.VMEM)
    any_spec = pl.BlockSpec(memory_space=pl.ANY)
    args = [picked.reshape(shape)]
    in_specs, out_specs = [vmem_spec], [vmem_spec]
    out_shape = [jax.ShapeDtypeStruct(shape, bf)]
    scratch = [
        pltpu.VMEM((chunks, vec_count, deep, ROWS, norb), bf),
        pltpu.VMEM((chunks, vec_count - 1, deep, ROWS, norb), bf),
        pltpu.VMEM((chunks, deep - 1, ROWS, norb), bf),
        pltpu.VMEM((chunks, vec_count, deep, ROWS, norb), bf),
        pltpu.VMEM((chunks, deep, ROWS, norb), bf),
        pltpu.VMEM((chunks, ROWS, norb), bf),
        pltpu.SemaphoreType.DMA((slots,)),
        pltpu.SemaphoreType.DMA((slots,)),
        pltpu.SemaphoreType.DMA((chunks,)),
    ]
    if early:
        cols = panel.shape[0]
        args += [panel, orbitals.reshape(-1, SPAN, norb)]
        in_specs += [vmem_spec, any_spec]
        out_specs += [any_spec, vmem_spec]
        out_shape += [
            jax.ShapeDtypeStruct((early, npoints, SPAN), bf),
            jax.ShapeDtypeStruct((early, cols, SPAN), jnp.float32),
        ]
        scratch += [
            pltpu.VMEM((early, SPAN, norb), bf),
            pltpu.VMEM((early, npoints, SPAN), bf),
            pltpu.SemaphoreType.DMA(()),
            pltpu.SemaphoreType.DMA((chunks,)),
        ]

    def body(*refs):
        share_kernel(chunks, early, refs)

    outs = pl.pallas_call(
        body,
        out_shape=out_shape,
        in_specs=in_specs,
        out_specs=out_specs,
        scratch_shapes=scratch,
        compiler_params=pltpu.CompilerParams(
            collective_id=4, has_side_effects=True, vmem_limit_bytes=46 << 20
        ),
        name="share_rows",
    )(*args)
    rows = outs[0].reshape(npoints, norb)
    return (rows, outs[1], outs[2]) if early else rows


OCTET = 8


def pick_kernel(points_ref, flags_ref, offset_ref, orb_ref, o_ref, found, where, spare, sheet, sem):
    octets, _, norb = orb_ref.shape
    limit = octets * OCTET
    npoints = o_ref.shape[0]
    offset = offset_ref[0]
    sheet[...] = jnp.zeros_like(sheet)

    def fetch(slot, octet):
        return pltpu.make_async_copy(orb_ref.at[octet], found.at[slot], sem)

    def look(i, held):
        position = points_ref[i] - offset
        inside = (position >= 0) & (position < limit)

        @pl.when(inside)
        def _():
            fetch(held, position // OCTET).start()
            where[held] = i
            spare[held] = lax.rem(position, OCTET)

        return held + inside.astype(jnp.int32)

    def scan(group, held):
        return lax.cond(
            flags_ref[group] > 0,
            lambda h: lax.fori_loop(
                0, OCTET, lambda k, n: look(group * OCTET + k, n), h, unroll=True
            ),
            lambda h: h,
            held,
        )

    held = lax.fori_loop(0, npoints // OCTET, scan, 0)

    def settle(slot, carry):
        fetch(slot, 0).wait()
        return carry

    lax.fori_loop(0, held, settle, 0)
    line = lax.broadcasted_iota(jnp.int32, (OCTET, norb), 0)

    def place(slot, carry):
        octet = found[slot].astype(jnp.float32)
        row = jnp.sum(jnp.where(line == spare[slot], octet, 0.0), axis=0, keepdims=True)
        sheet[pl.ds(where[slot], 1), :] = row
        return carry

    lax.fori_loop(0, held, place, 0)
    o_ref[...] = sheet[...].astype(o_ref.dtype)


def pick_rows(orbitals, points, offset):
    rows, norb = orbitals.shape
    npoints = points.shape[0]
    position = points - offset
    if rows % OCTET != 0 or npoints % OCTET != 0:
        inside = (position >= 0) & (position < rows)
        picked = jnp.take(orbitals, jnp.clip(position, 0, rows - 1), axis=0)
        return jnp.where(inside[:, None], picked, jnp.zeros_like(picked))
    inside = (position >= 0) & (position < rows)
    flags = jnp.max(inside.reshape(-1, OCTET).astype(jnp.int32), axis=1)
    return pl.pallas_call(
        pick_kernel,
        out_shape=jax.ShapeDtypeStruct((npoints, norb), orbitals.dtype),
        in_specs=[
            pl.BlockSpec(memory_space=pltpu.SMEM),
            pl.BlockSpec(memory_space=pltpu.SMEM),
            pl.BlockSpec(memory_space=pltpu.SMEM),
            pl.BlockSpec(memory_space=pl.ANY),
        ],
        out_specs=pl.BlockSpec(memory_space=pltpu.VMEM),
        scratch_shapes=[
            pltpu.VMEM((npoints, OCTET, norb), orbitals.dtype),
            pltpu.SMEM((npoints,), jnp.int32),
            pltpu.SMEM((npoints,), jnp.int32),
            pltpu.VMEM((npoints, norb), jnp.float32),
            pltpu.SemaphoreType.DMA(()),
        ],
        compiler_params=pltpu.CompilerParams(vmem_limit_bytes=28 << 20),
        name="pick_rows",
    )(points, flags, offset[None].astype(jnp.int32), orbitals.reshape(rows // OCTET, OCTET, norb))


def project(pair, pot_rows):
    scale = 1.0 / math.sqrt(float(NG**3))
    term = lax.dot_general(
        pair, pot_rows, (((0,), (1,)), ((), ())), preferred_element_type=jnp.float32
    )
    term = term * jnp.float32(scale)
    npoints, cols = term.shape
    count = lax.axis_size("grid") * lax.axis_size("vec")
    share = npoints // count
    if share * cols % LANES == 0:
        blocks = term.reshape(count, share * cols // LANES, LANES)
        return exchange(blocks, 3, True).reshape(share, cols)
    partial_block = lax.psum_scatter(term, "grid", scatter_dimension=0, tiled=True)
    return lax.psum_scatter(partial_block, "vec", scatter_dimension=0, tiled=True)


def peers_of():
    vec_count = lax.axis_size("vec")
    count = lax.axis_size("grid") * vec_count
    me = lax.axis_index("grid") * vec_count + lax.axis_index("vec")

    def place(index):
        return (index // vec_count, lax.rem(index, vec_count))

    return count, me, place


def greet_all(count, me, place):
    barrier = pltpu.get_barrier_semaphore()

    def greet(step, carry):
        pl.semaphore_signal(
            barrier,
            inc=1,
            device_id=place(lax.rem(me + step, count)),
            device_id_type=pl.DeviceIdType.MESH,
        )
        return carry

    lax.fori_loop(1, count, greet, 0)


def wait_greeted(count):
    pl.semaphore_wait(pltpu.get_barrier_semaphore(), count - 1)


NT = (((1,), (1,)), ((), ()))
NN = (((1,), (0,)), ((), ()))
LINES = 16
SPAN = LINES * NG
TAKE = 512
JOIN = NG // LINES
TAIL = (3, 5)
EARLY = 4


def pair_fit_kernel(
    orb_ref, rows_ref, panel_ref, early_ref, pair_ref, field_ref, fit_buf, fit_rows, out_buf,
    send_sem, recv_sem, own_sem,
):
    bf = jnp.bfloat16
    block = pl.program_id(0) + EARLY
    blocks = pl.num_programs(0) + EARLY
    count, me, place = peers_of()
    npoints = rows_ref.shape[0]
    cols = panel_ref.shape[0]
    per_plane = NG // LINES
    groups = blocks // JOIN
    tall = JOIN * LINES

    def send(group, begin, lines):
        slot = lax.rem(group, 2)
        start = pl.multiple_of(lax.rem(group * JOIN, per_plane) * LINES + begin, LINES)
        target = field_ref.at[me, group * JOIN // per_plane, pl.ds(start, lines)]

        def body(step, carry):
            peer = lax.rem(me + step, count)
            pltpu.make_async_remote_copy(
                src_ref=out_buf.at[slot, peer, pl.ds(begin, lines)],
                dst_ref=target,
                send_sem=send_sem.at[slot],
                recv_sem=recv_sem.at[me],
                device_id=place(peer),
                device_id_type=pl.DeviceIdType.MESH,
            ).start()
            return carry

        pltpu.make_async_copy(
            out_buf.at[slot, me, pl.ds(begin, lines)], target, own_sem.at[slot]
        ).start()
        lax.fori_loop(1, count, body, 0, unroll=True)

    def drain(group):
        slot = lax.rem(group, 2)
        sent = out_buf.at[slot, pl.ds(0, count - 1)]
        mine = out_buf.at[slot, me]
        pltpu.make_async_copy(mine, mine, own_sem.at[slot]).wait()
        pltpu.make_async_copy(sent, sent, send_sem.at[slot]).wait()

    @pl.when(block == EARLY)
    def _():
        greet_all(count, me, place)

    before = block - 1

    @pl.when((block > 2 * JOIN) & (lax.rem(before, JOIN) == 0))
    def _():
        drain(before // JOIN - 2)

    def multiply(first):
        part = lax.dot_general(
            rows_ref[first : first + TAKE, :], orb_ref[...], NT, preferred_element_type=jnp.float32
        )
        pair_ref[0, first : first + TAKE, :] = (part * part).astype(bf)

    def arrange(index):
        for line in range(LINES):
            begin = line * NG
            low = begin // LANES * LANES
            turn = begin - low
            wide = fit_buf[:, low : min(low + 2 * LANES, SPAN)]
            if wide.shape[1] == LANES:
                wide = jnp.concatenate([wide, wide], axis=1)
            if turn:
                wide = pltpu.roll(wide, 2 * LANES - turn, 1)
            fit_rows[pl.ds(line, cols, stride=LINES), :] = wide[:, :LANES]
        slot = index // JOIN % 2
        begin = index % JOIN * LINES
        if not isinstance(index, int):
            begin = pl.multiple_of(begin, LINES)
        out_buf[slot, :, pl.ds(begin, LINES), :] = (
            fit_rows[...].astype(bf).reshape(cols, LINES, LANES)
        )

    @pl.when(block == EARLY)
    def _():
        for index in range(EARLY - 1):
            fit_buf[...] = early_ref[index]
            arrange(index)
        fit_buf[...] = early_ref[EARLY - 1]

    multiply(0)
    arrange(before)
    for first in range(TAKE, npoints // 2, TAKE):
        multiply(first)

    @pl.when(block == EARLY + 1)
    def _():
        wait_greeted(count)

    @pl.when((block > EARLY) & (lax.rem(block, JOIN) == 0))
    def _():
        send(block // JOIN - 1, 0, tall)

    for start, stop in zip((0,) + TAIL, TAIL):

        @pl.when(block == blocks - JOIN + stop)
        def _(start=start, stop=stop):
            send(groups - 1, start * LINES, (stop - start) * LINES)

    for first in range(npoints // 2, npoints, TAKE):
        multiply(first)
    fit_buf[...] = lax.dot_general(
        panel_ref[...], pair_ref[0], NN, preferred_element_type=jnp.float32
    )

    @pl.when(block == blocks - 1)
    def _():
        arrange(block)
        send(groups - 1, TAIL[-1] * LINES, (JOIN - TAIL[-1]) * LINES)

        def receive(step, carry):
            source = lax.rem(me + count - step, count)
            land = field_ref.at[source]
            pltpu.make_async_copy(land, land, recv_sem.at[source]).wait()
            return carry

        lax.fori_loop(1, count, receive, 0)
        drain(groups - 2)
        drain(groups - 1)


def pair_and_fit(orbitals, point_rows, panel, early_fit):
    bf = jnp.bfloat16
    rows, norb = orbitals.shape
    npoints = point_rows.shape[0]
    cols = panel.shape[0]
    blocks = rows // SPAN - EARLY
    planes = rows // (NG * NG)
    count = lax.axis_size("grid") * lax.axis_size("vec")
    return pl.pallas_call(
        pair_fit_kernel,
        grid=(blocks,),
        in_specs=[
            pl.BlockSpec((SPAN, norb), lambda i: (i + EARLY, 0)),
            pl.BlockSpec((npoints, norb), lambda i: (0, 0)),
            pl.BlockSpec((cols, npoints), lambda i: (0, 0)),
            pl.BlockSpec((EARLY, cols, SPAN), lambda i: (0, 0, 0)),
        ],
        out_specs=[
            pl.BlockSpec((1, npoints, SPAN), lambda i: (i, 0, 0)),
            pl.BlockSpec(memory_space=pl.ANY),
        ],
        out_shape=[
            jax.ShapeDtypeStruct((blocks, npoints, SPAN), bf),
            jax.ShapeDtypeStruct((count, planes, NG, LANES), bf),
        ],
        scratch_shapes=[
            pltpu.VMEM((cols, SPAN), jnp.float32),
            pltpu.VMEM((cols * LINES, LANES), jnp.float32),
            pltpu.VMEM((2, cols, JOIN * LINES, LANES), bf),
            pltpu.SemaphoreType.DMA((2,)),
            pltpu.SemaphoreType.DMA((count,)),
            pltpu.SemaphoreType.DMA((2,)),
        ],
        compiler_params=pltpu.CompilerParams(
            collective_id=1, has_side_effects=True, vmem_limit_bytes=36 << 20
        ),
        name="pair_fit_send",
    )(orbitals, point_rows, panel, early_fit)


GROUP = 24
HALF = 64
THIRDS = 3
PIECE = NG * NG // LANES // THIRDS
RING = EARLY


def solve_project_kernel(
    field_ref, tz_ref, ty_ref, tyi_ref, tzi_ref, early_ref, pair_ref, o_ref,
    field, by_y, by_x, flat, dense, pot, ring, land, wide, total, parts, held,
    field_sem, send_sem, recv_sem, own_sem, pair_sem, part_send, part_recv,
):
    bf = jnp.bfloat16
    f32 = jnp.float32
    count, me, place = peers_of()
    rest, npoints, _ = pair_ref.shape
    blocks = rest + EARLY
    pieces = pot.shape[0]
    cols = count
    share = npoints // count
    planes = NG // count
    per_piece = blocks // pieces
    strips = SPAN // LANES

    def load(step):
        part = pl.ds(step * GROUP, GROUP)
        return pltpu.make_async_copy(field_ref.at[part], field.at[part], field_sem.at[step])

    def fetch(ref, block):
        slot = lax.rem(block, RING)
        return pltpu.make_async_copy(ref.at[block], ring.at[slot], pair_sem.at[slot])

    for step in range(NG // GROUP):
        load(step).start()
    greet_all(count, me, place)

    lane = lax.broadcasted_iota(jnp.int32, (NG, LANES), 1)
    row = lax.broadcasted_iota(jnp.int32, (NG, LANES), 0)
    sign = jnp.where(lane < HALF, 1.0, -1.0).astype(f32)
    wave_z = lax.rem(lane, HALF).astype(f32)
    wave_x = jnp.where(row < NG // 2, row, row - NG).astype(f32)
    plane_sq = wave_x * wave_x + wave_z * wave_z
    factor = NG / (2.0 * math.pi) * (NG / (2.0 * math.pi))

    def both(shapes):
        top = jnp.concatenate([part.astype(bf) for part in shapes], axis=1)
        turned = [(pltpu.roll(part, HALF, 1) * sign).astype(bf) for part in shapes]
        return jnp.concatenate([top, jnp.concatenate(turned, axis=1)], axis=0)

    def cut(sheet, k):
        return sheet[:, k * LANES : (k + 1) * LANES]

    def forward(step, carry):
        first = step * GROUP
        load(step).wait()
        data = field[pl.ds(first, GROUP)].reshape(GROUP * NG, LANES)
        a = lax.dot_general(data, tz_ref[...], NN, preferred_element_type=f32).astype(bf)
        top = [a[k * NG : (k + 1) * NG, :LANES] for k in range(GROUP)]
        low = [a[k * NG : (k + 1) * NG, LANES:] for k in range(GROUP)]
        stack = jnp.concatenate(
            [jnp.concatenate(top, axis=1), jnp.concatenate(low, axis=1)], axis=0
        )
        b = lax.dot_general(ty_ref[...], stack, NN, preferred_element_type=f32)
        for k in range(GROUP):
            by_y[pl.ds(first + k, NG, stride=NG), :] = cut(b, k)
        return carry

    lax.fori_loop(0, NG // GROUP, forward, 0)

    def prime(block, carry):
        fetch(early_ref, block).start()
        return carry

    lax.fori_loop(0, EARLY, prime, 0)

    def middle(step, carry):
        first = step * GROUP
        rows = [by_y[pl.ds((first + k) * NG, NG), :] for k in range(GROUP)]
        h = lax.dot_general(ty_ref[...], both(rows), NN, preferred_element_type=f32)
        scaled = []
        for k in range(GROUP):
            index = first + k
            wave_y = jnp.where(index < NG // 2, index, index - NG).astype(f32)
            squared = plane_sq + wave_y * wave_y
            kernel = jnp.where(squared > 0.5, factor / (squared + SCREEN), 0.0)
            scaled.append(cut(h, k) * kernel)
        g = lax.dot_general(tyi_ref[...], both(scaled), NN, preferred_element_type=f32)
        for k in range(GROUP):
            by_x[pl.ds(first + k, NG, stride=NG), :] = cut(g, k)
        return carry

    lax.fori_loop(0, NG // GROUP, middle, 0)
    wait_greeted(count)

    whole = (planes - 1) * THIRDS

    def own(part, piece):
        return pltpu.make_async_copy(pot.at[part, me], land.at[part, me], own_sem.at[piece])

    def send_pieces(part, piece):
        def body(step, carry):
            peer = lax.rem(me + step, count)
            pltpu.make_async_remote_copy(
                src_ref=pot.at[part, peer],
                dst_ref=land.at[part, me],
                send_sem=send_sem.at[piece],
                recv_sem=recv_sem.at[piece],
                device_id=place(peer),
                device_id_type=pl.DeviceIdType.MESH,
            ).start()
            return carry

        own(part, piece).start()
        lax.fori_loop(1, count, body, 0, unroll=True)

    def arrive(part, piece):
        own(part, piece).wait()
        others = land.at[part, pl.ds(0, count - 1)]
        pltpu.make_async_copy(others, others, recv_sem.at[piece]).wait()

    def leave(part, piece):
        sent = pot.at[part, pl.ds(0, count - 1)]
        pltpu.make_async_copy(sent, sent, send_sem.at[piece]).wait()

    quarter = NG // 4
    spot = lane[:quarter]

    def backward(local, carry):
        rows = [by_x[pl.ds((local + planes * k) * NG, NG), :] for k in range(count)]
        p = lax.dot_general(tyi_ref[...], both(rows), NN, preferred_element_type=f32).astype(bf)
        tall = jnp.concatenate([cut(p, k) for k in range(count)], axis=0)
        final = lax.dot_general(tall, tzi_ref[...], NN, preferred_element_type=f32)
        flat[...] = final * f32(1.0 / float(NG**3))
        for k in range(count):
            y0, y1, y2, y3 = [flat[pl.ds(k * NG + j, quarter, stride=4), :] for j in range(4)]
            y1, y2, y3 = pltpu.roll(y1, 96, 1), pltpu.roll(y2, 64, 1), pltpu.roll(y3, 32, 1)
            base = k % 4 * 3 * PIECE
            dense[pl.ds(base, quarter, stride=3), :] = jnp.where(spot < 96, y0, y1)
            dense[pl.ds(base + 1, quarter, stride=3), :] = jnp.where(spot < 64, y1, y2)
            dense[pl.ds(base + 2, quarter, stride=3), :] = jnp.where(spot < 32, y2, y3)
            for m in range(3):
                pot[local * 3 + m, k] = dense[base + m * PIECE : base + (m + 1) * PIECE, :].astype(bf)

        @pl.when(local < planes - 1)
        def _():
            send_pieces(pl.ds(local * THIRDS, THIRDS), local * THIRDS)

        @pl.when(local == planes - 1)
        def _():
            for m in range(THIRDS):
                send_pieces(pl.ds(whole + m, 1), whole + m)

        return carry

    lax.fori_loop(0, planes, backward, 0)
    total[...] = jnp.zeros_like(total)

    def work(piece, carry):
        @pl.when((piece < whole) & (lax.rem(piece, THIRDS) == 0))
        def _():
            arrive(pl.ds(piece, THIRDS), piece)

        @pl.when(piece >= whole)
        def _():
            arrive(pl.ds(piece, 1), piece)

        wide[...] = land[piece].astype(f32).reshape(cols * PIECE, LANES)
        for half in range(per_piece):
            block = piece * per_piece + half
            slot = lax.rem(block, RING)
            pltpu.make_async_copy(ring.at[slot], ring.at[slot], pair_sem.at[slot]).wait()
            lines = [
                wide[pl.ds(half * strips + j, cols, stride=PIECE), :].astype(bf)
                for j in range(strips)
            ]
            total[...] += lax.dot_general(
                jnp.concatenate(lines, axis=1), ring[slot], NT, preferred_element_type=f32
            )

            @pl.when(block < rest)
            def _():
                fetch(pair_ref, block).start()

        return carry

    lax.fori_loop(0, pieces, work, 0)

    scale = f32(1.0 / math.sqrt(float(NG**3)))
    low_lane = lax.broadcasted_iota(jnp.int32, (cols // 2, LANES), 1) < share
    for k in range(npoints // LANES):
        tile = total[:, k * LANES : (k + 1) * LANES] * scale
        top, low = tile[: cols // 2], tile[cols // 2 :]
        parts[2 * k] = jnp.where(low_lane, top, pltpu.roll(low, share, 1))
        parts[2 * k + 1] = jnp.where(low_lane, pltpu.roll(top, share, 1), low)

    def part_copy(step, source, slot):
        peer = lax.rem(me + step, count)
        return pltpu.make_async_remote_copy(
            src_ref=parts.at[source],
            dst_ref=held.at[slot],
            send_sem=part_send.at[step],
            recv_sem=part_recv.at[step],
            device_id=place(peer),
            device_id_type=pl.DeviceIdType.MESH,
        )

    def part_start(step, carry):
        part_copy(step, lax.rem(me + step, count), me).start()
        return carry

    lax.fori_loop(1, count, part_start, 0)
    held[me] = parts[me]

    for local in range(planes - 1):
        leave(pl.ds(local * THIRDS, THIRDS), local * THIRDS)
    for m in range(THIRDS):
        leave(pl.ds(whole + m, 1), whole + m)

    def part_receive(step, carry):
        source = lax.rem(me + count - step, count)
        part_copy(step, source, source).wait_recv()
        return carry

    lax.fori_loop(1, count, part_receive, 0)
    summed = jnp.sum(held[...], axis=0)
    pile = jnp.concatenate([summed, pltpu.roll(summed, share, 1)], axis=0)
    o_ref[...] = pile.T[:share, :]

    def part_drain(step, carry):
        part_copy(step, lax.rem(me + step, count), me).wait_send()
        return carry

    lax.fori_loop(1, count, part_drain, 0)


def solve_and_project(field, early, pair, count):
    bf = jnp.bfloat16
    f32 = jnp.float32
    cos_tab, sin_tab = literal_tables(NG)
    keep = NG // 2 + 1

    def padded(table):
        return np.pad(table[:, :keep], ((0, LANES - NG), (0, HALF - keep)))

    cz, sz = padded(cos_tab), padded(sin_tab)
    tz = np.concatenate([cz, -sz, -sz, -cz], axis=1)
    ty = np.concatenate([cos_tab, sin_tab], axis=1)
    tyi = np.concatenate([cos_tab, -sin_tab], axis=1)
    spot = np.arange(HALF)[:, None]
    weight = np.where((spot == 0) | (spot == NG // 2), 1.0, 2.0).astype(bf)
    tzi = np.concatenate([cz.T * weight, -(sz.T * weight)], axis=0)
    tz, ty, tyi, tzi = [jnp.asarray(table, bf) for table in (tz, ty, tyi, tzi)]
    pieces = NG // count * 3
    blocks, npoints, span = pair.shape
    cols = count
    any_spec = pl.BlockSpec(memory_space=pl.ANY)
    vmem_spec = pl.BlockSpec(memory_space=pltpu.VMEM)
    return pl.pallas_call(
        solve_project_kernel,
        out_shape=jax.ShapeDtypeStruct((npoints // count, cols), f32),
        in_specs=[any_spec] + [vmem_spec] * 4 + [any_spec] * 2,
        out_specs=vmem_spec,
        scratch_shapes=[
            pltpu.VMEM((NG, NG, LANES), bf),
            pltpu.VMEM((NG * NG, LANES), f32),
            pltpu.VMEM((NG * NG, LANES), f32),
            pltpu.VMEM((count * NG, LANES), f32),
            pltpu.VMEM((4 * 3 * PIECE, LANES), f32),
            pltpu.VMEM((pieces, count, PIECE, LANES), bf),
            pltpu.VMEM((RING, npoints, span), bf),
            pltpu.VMEM((pieces, count, PIECE, LANES), bf),
            pltpu.VMEM((cols * PIECE, LANES), f32),
            pltpu.VMEM((cols, npoints), f32),
            pltpu.VMEM((count, cols // 2, LANES), f32),
            pltpu.VMEM((count, cols // 2, LANES), f32),
            pltpu.SemaphoreType.DMA((NG // GROUP,)),
            pltpu.SemaphoreType.DMA((pieces,)),
            pltpu.SemaphoreType.DMA((pieces,)),
            pltpu.SemaphoreType.DMA((pieces,)),
            pltpu.SemaphoreType.DMA((RING,)),
            pltpu.SemaphoreType.DMA((count,)),
            pltpu.SemaphoreType.DMA((count,)),
        ],
        compiler_params=pltpu.CompilerParams(
            collective_id=2, has_side_effects=True, vmem_limit_bytes=54 << 20
        ),
        name="solve_project",
    )(field.reshape(NG, NG, LANES), tz, ty, tyi, tzi, early, pair)


def fits_planes(rows, npoints, cols, count):
    blocks = rows // SPAN
    return (
        cols == count
        and rows % (NG * NG) == 0
        and NG % (rows // (NG * NG)) == 0
        and blocks >= 3 * JOIN
        and EARLY + 1 < JOIN
        and npoints % (count * ROWS) == 0
        and NG // LINES % JOIN == 0
        and npoints % TAKE == 0
        and 2 * npoints == count * LANES
    )


def shards(orbitals, inverse_panel, points):
    bf = jnp.bfloat16
    row_count = orbitals.shape[0]
    grid_count = lax.axis_size("grid")
    vec_count = lax.axis_size("vec")
    npoints = points.shape[0]
    offset = (lax.axis_index("grid") * vec_count + lax.axis_index("vec")) * row_count
    picked = pick_rows(orbitals, points, offset)
    cols = inverse_panel.shape[1]
    if fits_planes(row_count, npoints, cols, grid_count * vec_count):
        panel = inverse_panel.T
        point_rows, early, early_fit = share_rows(picked, grid_count, vec_count, panel, orbitals)
        pair, field = pair_and_fit(orbitals, point_rows, panel, early_fit)
        return solve_and_project(field, early, pair, grid_count * vec_count)
    point_rows = share_rows(picked, grid_count, vec_count)

    def pair_block(block):
        correlation = lax.dot_general(
            block, point_rows, (((1,), (1,)), ((), ())), preferred_element_type=jnp.float32
        )
        return (correlation * correlation).astype(bf)

    pair = lax.map(pair_block, orbitals.reshape(4, row_count // 4, orbitals.shape[1])).reshape(
        row_count, npoints
    )
    fit_cols = lax.dot_general(
        inverse_panel, pair, (((0,), (1,)), ((), ())), preferred_element_type=jnp.float32
    ).astype(bf)
    slab = lax.all_to_all(fit_cols, "vec", split_axis=0, concat_axis=1, tiled=True)
    col_local = slab.shape[0]
    planes = NG // grid_count
    field = slab.reshape(col_local, planes, NG, NG)
    cos_tab, sin_tab = wave_tables(NG)
    z_re = mult(field, cos_tab, "vxyz,zk->vxyk").astype(bf)
    z_im = (-mult(field, sin_tab, "vxyz,zk->vxyk")).astype(bf)
    y_re = (mult(z_re, cos_tab, "vxyz,yk->vxkz") + mult(z_im, sin_tab, "vxyz,yk->vxkz")).astype(bf)
    y_im = (mult(z_im, cos_tab, "vxyz,yk->vxkz") - mult(z_re, sin_tab, "vxyz,yk->vxkz")).astype(bf)
    stacked = jnp.stack([y_re, y_im])
    waves = wavenumber(lax.iota(jnp.int32, NG), NG)
    y_waves = wavenumber(lax.axis_index("grid") * planes + lax.iota(jnp.int32, planes), NG)
    kernel = screened(waves, y_waves, waves)[None]
    piece = lax.all_to_all(stacked, "grid", split_axis=3, concat_axis=2, tiled=True)
    p_re = piece[0]
    p_im = piece[1]
    x_re = mult(p_re, cos_tab, "vxyz,xk->vkyz") + mult(p_im, sin_tab, "vxyz,xk->vkyz")
    x_im = mult(p_im, cos_tab, "vxyz,xk->vkyz") - mult(p_re, sin_tab, "vxyz,xk->vkyz")
    q_re = (x_re * kernel).astype(bf)
    q_im = (x_im * kernel).astype(bf)
    i_re = (mult(q_re, cos_tab, "vxyz,xk->vkyz") - mult(q_im, sin_tab, "vxyz,xk->vkyz")).astype(bf)
    i_im = (mult(q_im, cos_tab, "vxyz,xk->vkyz") + mult(q_re, sin_tab, "vxyz,xk->vkyz")).astype(bf)
    spectrum = lax.all_to_all(
        jnp.stack([i_re, i_im]), "grid", split_axis=2, concat_axis=3, tiled=True
    )
    s_re = spectrum[0]
    s_im = spectrum[1]
    h_re = (mult(s_re, cos_tab, "vxyz,yk->vxkz") - mult(s_im, sin_tab, "vxyz,yk->vxkz")).astype(bf)
    h_im = (mult(s_im, cos_tab, "vxyz,yk->vxkz") + mult(s_re, sin_tab, "vxyz,yk->vxkz")).astype(bf)
    final = mult(h_re, cos_tab, "vxyz,zk->vxyk") - mult(h_im, sin_tab, "vxyz,zk->vxyk")
    potential = (final / float(NG**3)).astype(bf).reshape(col_local, planes * NG * NG)
    pot_rows = lax.all_to_all(potential, "vec", split_axis=1, concat_axis=0, tiled=True)
    return project(pair, pot_rows)


def solution(mesh):
    in_specs = (P(("grid", "vec"), None), P(), P())
    out_specs = P(("grid", "vec"), None)
    return jax.shard_map(shards, mesh=mesh, in_specs=in_specs, out_specs=out_specs, check_vma=False)
```

```python
import math

import jax
import jax.numpy as jnp
import numpy as np
from jax import lax
from jax.experimental import pallas as pl
from jax.experimental.pallas import tpu as pltpu
from jax.sharding import PartitionSpec as P

NG = 96


SCREEN = 2.25


def wave_tables(count):
    index = lax.iota(jnp.int32, count)
    phase = index[:, None] * index[None, :] % count
    angle = phase.astype(jnp.float32) * (2.0 * math.pi / count)
    return (jnp.cos(angle).astype(jnp.bfloat16), jnp.sin(angle).astype(jnp.bfloat16))


def literal_tables(count):
    index = np.arange(count)
    phase = index[:, None] * index[None, :] % count
    angle = phase.astype(np.float32) * np.float32(2.0 * math.pi / count)
    return np.cos(angle).astype(jnp.bfloat16), np.sin(angle).astype(jnp.bfloat16)


def wavenumber(index, count):
    return jnp.where(index < count // 2, index, index - count).astype(jnp.float32)


def screened(wave_x, wave_y, wave_z):
    squared = (
        wave_x[:, None, None] * wave_x[:, None, None]
        + wave_y[None, :, None] * wave_y[None, :, None]
        + wave_z[None, None, :] * wave_z[None, None, :]
    )
    factor = NG / (2.0 * math.pi) * (NG / (2.0 * math.pi))
    return jnp.where(squared > 0.5, factor / (squared + SCREEN), jnp.float32(0.0))


def mult(data, table, form):
    return jnp.einsum(form, data, table, preferred_element_type=jnp.float32)


LANES = 128


def exchange_kernel(axes, total, gather, x_ref, o_ref, held, send_sem, recv_sem, own_sem):
    if len(axes) == 2:
        vec_count = lax.axis_size("vec")
        count = lax.axis_size("grid") * vec_count
        me = lax.axis_index("grid") * vec_count + lax.axis_index("vec")
    else:
        count = lax.axis_size(axes[0])
        me = lax.axis_index(axes[0])
    land = held if total else o_ref

    def place(index):
        if len(axes) == 2:
            return (index // vec_count, lax.rem(index, vec_count))
        if axes[0] == "grid":
            return (index, lax.axis_index("vec"))
        return (lax.axis_index("grid"), index)

    def part(index):
        return x_ref if gather else x_ref.at[index]

    barrier = pltpu.get_barrier_semaphore()

    def greet(step, carry):
        pl.semaphore_signal(
            barrier,
            inc=1,
            device_id=place(lax.rem(me + step, count)),
            device_id_type=pl.DeviceIdType.MESH,
        )
        return carry

    lax.fori_loop(1, count, greet, 0)
    own = pltpu.make_async_copy(part(me), land.at[me], own_sem)
    own.start()
    pl.semaphore_wait(barrier, count - 1)

    def copy(step, source, slot):
        peer = lax.rem(me + step, count)
        return pltpu.make_async_remote_copy(
            src_ref=part(source),
            dst_ref=land.at[slot],
            send_sem=send_sem.at[step],
            recv_sem=recv_sem.at[step],
            device_id=place(peer),
            device_id_type=pl.DeviceIdType.MESH,
        )

    def send(step, carry):
        copy(step, lax.rem(me + step, count), me).start()
        return carry

    lax.fori_loop(1, count, send, 0)
    own.wait()

    def receive(step, carry):
        source = lax.rem(me + count - step, count)
        copy(step, source, source).wait_recv()
        return carry

    lax.fori_loop(1, count, receive, 0)
    if total:
        o_ref[...] = jnp.sum(held[...].astype(jnp.float32), axis=0).astype(o_ref.dtype)

    def drain(step, carry):
        copy(step, lax.rem(me + step, count), me).wait_send()
        return carry

    lax.fori_loop(1, count, drain, 0)


def exchange(blocks, ident, total=False, axes=("grid", "vec"), gather=False):
    rows, lanes = blocks.shape[-2:]
    count = 1
    for axis in axes:
        count *= lax.axis_size(axis)
    shape = (rows, lanes) if total else (count, rows, lanes)
    held_shape = blocks.shape if total else (1, 8, LANES)

    def body(*refs):
        exchange_kernel(axes, total, gather, *refs)

    return pl.pallas_call(
        body,
        out_shape=jax.ShapeDtypeStruct(shape, blocks.dtype),
        in_specs=[pl.BlockSpec(memory_space=pltpu.VMEM)],
        out_specs=pl.BlockSpec(memory_space=pltpu.VMEM),
        scratch_shapes=[
            pltpu.VMEM(held_shape, blocks.dtype),
            pltpu.SemaphoreType.DMA((count,)),
            pltpu.SemaphoreType.DMA((count,)),
            pltpu.SemaphoreType.DMA(()),
        ],
        compiler_params=pltpu.CompilerParams(
            collective_id=ident, has_side_effects=True, vmem_limit_bytes=32 << 20
        ),
        name="exchange_total" if total else "exchange_gather" if gather else "exchange_blocks",
    )(blocks)


def share_kernel(chunks, early, refs):
    if early:
        x_ref, panel_ref, orb_ref, o_ref, early_ref, fit_ref = refs[:6]
        orbs, pairs, orb_sem, pair_sem = refs[-4:]
        near, wide, far, sum1, sum2, sum3, sends, recvs, own_sem = refs[6:-4]
    else:
        x_ref, o_ref, near, wide, far, sum1, sum2, sum3, sends, recvs, own_sem = refs
    bf = jnp.bfloat16
    f32 = jnp.float32
    vec_count = lax.axis_size("vec")
    deep = lax.axis_size("grid") // 2
    grid_at, mine = lax.axis_index("grid"), lax.axis_index("vec")
    level, core = grid_at // 2, lax.rem(grid_at, 2)
    other = 1 - core
    across = vec_count - 1

    def partner(step):
        return (level * 2 + other, mine)

    def beside(step):
        return (grid_at, lax.rem(mine + step, vec_count))

    def above(step):
        return (lax.rem(level + step, deep) * 2 + core, mine)

    peers = [partner(1)]
    peers += [beside(step) for step in range(1, vec_count)]
    peers += [above(step) for step in range(1, deep)]
    barrier = pltpu.get_barrier_semaphore()
    for peer in peers:
        pl.semaphore_signal(barrier, inc=1, device_id=peer, device_id_type=pl.DeviceIdType.MESH)
    pl.semaphore_wait(barrier, len(peers))

    def send(source, target, slot, peer):
        return pltpu.make_async_remote_copy(
            src_ref=source,
            dst_ref=target,
            send_sem=sends.at[slot],
            recv_sem=recvs.at[slot],
            device_id=peer,
            device_id_type=pl.DeviceIdType.MESH,
        )

    per_chunk = 2 + 2 * across + 2 * (deep - 1)

    def copies(stage, c):
        base = c * per_chunk
        if stage == 0:
            return [send(x_ref.at[c, other], near.at[c], base, partner(1))]
        if stage == 1:
            return [
                send(
                    sum1.at[c, lax.rem(mine + step, vec_count)],
                    wide.at[c, step - 1],
                    base + step,
                    beside(step),
                )
                for step in range(1, vec_count)
            ]
        if stage == 2:
            return [
                send(
                    sum2.at[c, lax.rem(level + step, deep)],
                    far.at[c, step - 1],
                    base + across + step,
                    above(step),
                )
                for step in range(1, deep)
            ]
        base += across + deep
        if stage == 3:
            spot = o_ref.at[c, core, mine, level]
            return [send(sum3.at[c], spot, base + step - 1, above(step)) for step in range(1, deep)]
        base += deep - 1
        if stage == 4:
            spot = o_ref.at[c, core, mine]
            return [send(spot, spot, base + step - 1, beside(step)) for step in range(1, vec_count)]
        spot = o_ref.at[c, core]
        return [send(spot, spot, base + across, partner(1))]

    def own(c):
        return pltpu.make_async_copy(sum3.at[c], o_ref.at[c, core, mine, level], own_sem.at[c])

    def prepare(stage, c):
        for move in copies(stage - 1, c):
            move.wait_recv()
        if stage == 1:
            sum1[c] = (x_ref[c, core].astype(f32) + near[c].astype(f32)).astype(bf)
        if stage == 2:
            total = sum1[c, mine].astype(f32)
            for step in range(across):
                total += wide[c, step].astype(f32)
            sum2[c] = total.astype(bf)
        if stage == 3:
            total = sum2[c, level].astype(f32)
            for step in range(deep - 1):
                total += far[c, step].astype(f32)
            sum3[c] = total.astype(bf)
            own(c).start()
        if stage == 4:
            own(c).wait()

    def fetch():
        return pltpu.make_async_copy(orb_ref.at[pl.ds(0, early)], orbs, orb_sem)

    def keep(c):
        height = pairs.shape[1] // chunks
        part = pl.ds(c * height, height)
        return pltpu.make_async_copy(
            pairs.at[:, part], early_ref.at[:, part], pair_sem.at[c]
        )

    def multiply(c):
        height = pairs.shape[1] // chunks
        rows = o_ref[c].reshape(height, o_ref.shape[-1])

        def body(e, carry):
            part = lax.dot_general(rows, orbs[e], NT, preferred_element_type=f32)
            pairs[e, c * height : (c + 1) * height, :] = (part * part).astype(bf)
            return carry

        lax.fori_loop(0, early, body, 0)

    if early:
        fetch().start()
    for tick in range(chunks + 6):
        for stage in range(6, -1, -1):
            c = tick - stage
            if 0 <= c < chunks:
                if stage > 0:
                    prepare(stage, c)
                if stage < 6:
                    for move in copies(stage, c):
                        move.start()
        if early and tick >= 6:
            if tick == 6:
                fetch().wait()
            multiply(tick - 6)
            keep(tick - 6).start()
    if early:

        def fit(e, carry):
            fit_ref[e] = lax.dot_general(
                panel_ref[...], pairs[e], NN, preferred_element_type=f32
            )
            return carry

        lax.fori_loop(0, early, fit, 0)
        for c in range(chunks):
            keep(c).wait()
    for c in range(chunks):
        for stage in range(6):
            for move in copies(stage, c):
                move.wait_send()


ROWS = 16


def share_rows(picked, grid_count, vec_count, panel=None, orbitals=None):
    bf = jnp.bfloat16
    npoints, norb = picked.shape
    count = grid_count * vec_count
    if npoints % (count * ROWS) != 0 or grid_count % 2 != 0:
        return lax.psum(picked.astype(jnp.float32), ("grid", "vec")).astype(picked.dtype)
    early = 0 if panel is None else EARLY
    chunks = npoints // (count * ROWS)
    deep = grid_count // 2
    shape = (chunks, 2, vec_count, deep, ROWS, norb)
    slots = chunks * (2 + 2 * (vec_count - 1) + 2 * (deep - 1))
    vmem_spec = pl.BlockSpec(memory_space=pltpu.VMEM)
    any_spec = pl.BlockSpec(memory_space=pl.ANY)
    args = [picked.reshape(shape)]
    in_specs, out_specs = [vmem_spec], [vmem_spec]
    out_shape = [jax.ShapeDtypeStruct(shape, bf)]
    scratch = [
        pltpu.VMEM((chunks, vec_count, deep, ROWS, norb), bf),
        pltpu.VMEM((chunks, vec_count - 1, deep, ROWS, norb), bf),
        pltpu.VMEM((chunks, deep - 1, ROWS, norb), bf),
        pltpu.VMEM((chunks, vec_count, deep, ROWS, norb), bf),
        pltpu.VMEM((chunks, deep, ROWS, norb), bf),
        pltpu.VMEM((chunks, ROWS, norb), bf),
        pltpu.SemaphoreType.DMA((slots,)),
        pltpu.SemaphoreType.DMA((slots,)),
        pltpu.SemaphoreType.DMA((chunks,)),
    ]
    if early:
        cols = panel.shape[0]
        args += [panel, orbitals.reshape(-1, SPAN, norb)]
        in_specs += [vmem_spec, any_spec]
        out_specs += [any_spec, vmem_spec]
        out_shape += [
            jax.ShapeDtypeStruct((early, npoints, SPAN), bf),
            jax.ShapeDtypeStruct((early, cols, SPAN), jnp.float32),
        ]
        scratch += [
            pltpu.VMEM((early, SPAN, norb), bf),
            pltpu.VMEM((early, npoints, SPAN), bf),
            pltpu.SemaphoreType.DMA(()),
            pltpu.SemaphoreType.DMA((chunks,)),
        ]

    def body(*refs):
        share_kernel(chunks, early, refs)

    outs = pl.pallas_call(
        body,
        out_shape=out_shape,
        in_specs=in_specs,
        out_specs=out_specs,
        scratch_shapes=scratch,
        compiler_params=pltpu.CompilerParams(
            collective_id=4, has_side_effects=True, vmem_limit_bytes=46 << 20
        ),
        name="share_rows",
    )(*args)
    rows = outs[0].reshape(npoints, norb)
    return (rows, outs[1], outs[2]) if early else rows


OCTET = 8


def pick_kernel(points_ref, flags_ref, offset_ref, orb_ref, o_ref, found, where, spare, sheet, sem):
    octets, _, norb = orb_ref.shape
    limit = octets * OCTET
    npoints = o_ref.shape[0]
    offset = offset_ref[0]
    sheet[...] = jnp.zeros_like(sheet)

    def fetch(slot, octet):
        return pltpu.make_async_copy(orb_ref.at[octet], found.at[slot], sem)

    def look(i, held):
        position = points_ref[i] - offset
        inside = (position >= 0) & (position < limit)

        @pl.when(inside)
        def _():
            fetch(held, position // OCTET).start()
            where[held] = i
            spare[held] = lax.rem(position, OCTET)

        return held + inside.astype(jnp.int32)

    def scan(group, held):
        return lax.cond(
            flags_ref[group] > 0,
            lambda h: lax.fori_loop(
                0, OCTET, lambda k, n: look(group * OCTET + k, n), h, unroll=True
            ),
            lambda h: h,
            held,
        )

    held = lax.fori_loop(0, npoints // OCTET, scan, 0)

    def settle(slot, carry):
        fetch(slot, 0).wait()
        return carry

    lax.fori_loop(0, held, settle, 0)
    line = lax.broadcasted_iota(jnp.int32, (OCTET, norb), 0)

    def place(slot, carry):
        octet = found[slot].astype(jnp.float32)
        row = jnp.sum(jnp.where(line == spare[slot], octet, 0.0), axis=0, keepdims=True)
        sheet[pl.ds(where[slot], 1), :] = row
        return carry

    lax.fori_loop(0, held, place, 0)
    o_ref[...] = sheet[...].astype(o_ref.dtype)


def pick_rows(orbitals, points, offset):
    rows, norb = orbitals.shape
    npoints = points.shape[0]
    position = points - offset
    if rows % OCTET != 0 or npoints % OCTET != 0:
        inside = (position >= 0) & (position < rows)
        picked = jnp.take(orbitals, jnp.clip(position, 0, rows - 1), axis=0)
        return jnp.where(inside[:, None], picked, jnp.zeros_like(picked))
    inside = (position >= 0) & (position < rows)
    flags = jnp.max(inside.reshape(-1, OCTET).astype(jnp.int32), axis=1)
    return pl.pallas_call(
        pick_kernel,
        out_shape=jax.ShapeDtypeStruct((npoints, norb), orbitals.dtype),
        in_specs=[
            pl.BlockSpec(memory_space=pltpu.SMEM),
            pl.BlockSpec(memory_space=pltpu.SMEM),
            pl.BlockSpec(memory_space=pltpu.SMEM),
            pl.BlockSpec(memory_space=pl.ANY),
        ],
        out_specs=pl.BlockSpec(memory_space=pltpu.VMEM),
        scratch_shapes=[
            pltpu.VMEM((npoints, OCTET, norb), orbitals.dtype),
            pltpu.SMEM((npoints,), jnp.int32),
            pltpu.SMEM((npoints,), jnp.int32),
            pltpu.VMEM((npoints, norb), jnp.float32),
            pltpu.SemaphoreType.DMA(()),
        ],
        compiler_params=pltpu.CompilerParams(vmem_limit_bytes=28 << 20),
        name="pick_rows",
    )(points, flags, offset[None].astype(jnp.int32), orbitals.reshape(rows // OCTET, OCTET, norb))


def project(pair, pot_rows):
    scale = 1.0 / math.sqrt(float(NG**3))
    term = lax.dot_general(
        pair, pot_rows, (((0,), (1,)), ((), ())), preferred_element_type=jnp.float32
    )
    term = term * jnp.float32(scale)
    npoints, cols = term.shape
    count = lax.axis_size("grid") * lax.axis_size("vec")
    share = npoints // count
    if share * cols % LANES == 0:
        blocks = term.reshape(count, share * cols // LANES, LANES)
        return exchange(blocks, 3, True).reshape(share, cols)
    partial_block = lax.psum_scatter(term, "grid", scatter_dimension=0, tiled=True)
    return lax.psum_scatter(partial_block, "vec", scatter_dimension=0, tiled=True)


def peers_of():
    vec_count = lax.axis_size("vec")
    count = lax.axis_size("grid") * vec_count
    me = lax.axis_index("grid") * vec_count + lax.axis_index("vec")

    def place(index):
        return (index // vec_count, lax.rem(index, vec_count))

    return count, me, place


def shift_of(step, count):
    return lax.rem(step, 2) * (count // 2) + step // 2


def greet_all(count, me, place):
    barrier = pltpu.get_barrier_semaphore()

    def greet(step, carry):
        pl.semaphore_signal(
            barrier,
            inc=1,
            device_id=place(lax.rem(me + step, count)),
            device_id_type=pl.DeviceIdType.MESH,
        )
        return carry

    lax.fori_loop(1, count, greet, 0)


def wait_greeted(count):
    pl.semaphore_wait(pltpu.get_barrier_semaphore(), count - 1)


NT = (((1,), (1,)), ((), ()))
NN = (((1,), (0,)), ((), ()))
LINES = 16
SPAN = LINES * NG
TAKE = 512
JOIN = 3
EARLY = 4


def pair_fit_kernel(
    orb_ref, rows_ref, panel_ref, early_ref, pair_ref, field_ref, fit_buf, fit_rows, out_buf,
    send_sem, recv_sem, own_sem,
):
    bf = jnp.bfloat16
    block = pl.program_id(0) + EARLY
    blocks = pl.num_programs(0) + EARLY
    count, me, place = peers_of()
    npoints = rows_ref.shape[0]
    cols = panel_ref.shape[0]
    per_plane = NG // LINES
    groups = blocks // JOIN
    tall = JOIN * LINES

    def send(group, begin, lines):
        slot = lax.rem(group, 2)
        start = pl.multiple_of(lax.rem(group * JOIN, per_plane) * LINES + begin, LINES)
        target = field_ref.at[me, group * JOIN // per_plane, pl.ds(start, lines)]

        def body(step, carry):
            peer = lax.rem(me + shift_of(step, count), count)
            pltpu.make_async_remote_copy(
                src_ref=out_buf.at[slot, peer, pl.ds(begin, lines)],
                dst_ref=target,
                send_sem=send_sem.at[slot],
                recv_sem=recv_sem.at[me],
                device_id=place(peer),
                device_id_type=pl.DeviceIdType.MESH,
            ).start()
            return carry

        pltpu.make_async_copy(
            out_buf.at[slot, me, pl.ds(begin, lines)], target, own_sem.at[slot]
        ).start()
        lax.fori_loop(1, count, body, 0, unroll=True)

    def drain(group):
        slot = lax.rem(group, 2)
        sent = out_buf.at[slot, pl.ds(0, count - 1)]
        mine = out_buf.at[slot, me]
        pltpu.make_async_copy(mine, mine, own_sem.at[slot]).wait()
        pltpu.make_async_copy(sent, sent, send_sem.at[slot]).wait()

    @pl.when(block == EARLY)
    def _():
        greet_all(count, me, place)

    before = block - 1

    @pl.when((block > 2 * JOIN) & (lax.rem(before, JOIN) == 0))
    def _():
        drain(before // JOIN - 2)

    def multiply(first):
        part = lax.dot_general(
            rows_ref[first : first + TAKE, :], orb_ref[...], NT, preferred_element_type=jnp.float32
        )
        pair_ref[0, first : first + TAKE, :] = (part * part).astype(bf)

    def arrange(index):
        for line in range(LINES):
            begin = line * NG
            low = begin // LANES * LANES
            turn = begin - low
            wide = fit_buf[:, low : min(low + 2 * LANES, SPAN)]
            if wide.shape[1] == LANES:
                wide = jnp.concatenate([wide, wide], axis=1)
            if turn:
                wide = pltpu.roll(wide, 2 * LANES - turn, 1)
            fit_rows[pl.ds(line, cols, stride=LINES), :] = wide[:, :LANES]
        slot = index // JOIN % 2
        begin = index % JOIN * LINES
        if not isinstance(index, int):
            begin = pl.multiple_of(begin, LINES)
        out_buf[slot, :, pl.ds(begin, LINES), :] = (
            fit_rows[...].astype(bf).reshape(cols, LINES, LANES)
        )

    @pl.when(block == EARLY)
    def _():
        for index in range(EARLY - 1):
            fit_buf[...] = early_ref[index]
            arrange(index)
        fit_buf[...] = early_ref[EARLY - 1]

    multiply(0)
    arrange(before)
    for first in range(TAKE, npoints // 2, TAKE):
        multiply(first)

    @pl.when(block == EARLY)
    def _():
        wait_greeted(count)
        send(0, 0, tall)

    @pl.when((block > EARLY) & (lax.rem(block, JOIN) == 0))
    def _():
        send(block // JOIN - 1, 0, tall)

    for late in range(JOIN - 1):

        @pl.when(block == blocks - JOIN + 1 + late)
        def _(late=late):
            send(groups - 1, late * LINES, LINES)

    for first in range(npoints // 2, npoints, TAKE):
        multiply(first)
    fit_buf[...] = lax.dot_general(
        panel_ref[...], pair_ref[0], NN, preferred_element_type=jnp.float32
    )

    @pl.when(block == blocks - 1)
    def _():
        arrange(block)
        send(groups - 1, (JOIN - 1) * LINES, LINES)

        def receive(step, carry):
            source = lax.rem(me + count - step, count)
            land = field_ref.at[source]
            pltpu.make_async_copy(land, land, recv_sem.at[source]).wait()
            return carry

        lax.fori_loop(1, count, receive, 0)
        drain(groups - 2)
        drain(groups - 1)


def pair_and_fit(orbitals, point_rows, panel, early_fit):
    bf = jnp.bfloat16
    rows, norb = orbitals.shape
    npoints = point_rows.shape[0]
    cols = panel.shape[0]
    blocks = rows // SPAN - EARLY
    planes = rows // (NG * NG)
    count = lax.axis_size("grid") * lax.axis_size("vec")
    return pl.pallas_call(
        pair_fit_kernel,
        grid=(blocks,),
        in_specs=[
            pl.BlockSpec((SPAN, norb), lambda i: (i + EARLY, 0)),
            pl.BlockSpec((npoints, norb), lambda i: (0, 0)),
            pl.BlockSpec((cols, npoints), lambda i: (0, 0)),
            pl.BlockSpec((EARLY, cols, SPAN), lambda i: (0, 0, 0)),
        ],
        out_specs=[
            pl.BlockSpec((1, npoints, SPAN), lambda i: (i, 0, 0)),
            pl.BlockSpec(memory_space=pl.ANY),
        ],
        out_shape=[
            jax.ShapeDtypeStruct((blocks, npoints, SPAN), bf),
            jax.ShapeDtypeStruct((count, planes, NG, LANES), bf),
        ],
        scratch_shapes=[
            pltpu.VMEM((cols, SPAN), jnp.float32),
            pltpu.VMEM((cols * LINES, LANES), jnp.float32),
            pltpu.VMEM((2, cols, JOIN * LINES, LANES), bf),
            pltpu.SemaphoreType.DMA((2,)),
            pltpu.SemaphoreType.DMA((count,)),
            pltpu.SemaphoreType.DMA((2,)),
        ],
        compiler_params=pltpu.CompilerParams(
            collective_id=1, has_side_effects=True, vmem_limit_bytes=36 << 20
        ),
        name="pair_fit_send",
    )(orbitals, point_rows, panel, early_fit)


GROUP = 24
HALF = 64
PIECE = NG * NG // LANES // 3
RING = EARLY


def solve_project_kernel(
    field_ref, tz_ref, ty_ref, tyi_ref, tzi_ref, early_ref, pair_ref, o_ref,
    field, by_y, by_x, flat, dense, pot, ring, land, wide, total, parts, held,
    field_sem, send_sem, recv_sem, own_sem, pair_sem, part_send, part_recv,
):
    bf = jnp.bfloat16
    f32 = jnp.float32
    count, me, place = peers_of()
    rest, npoints, _ = pair_ref.shape
    blocks = rest + EARLY
    pieces = pot.shape[0]
    cols = count
    share = npoints // count
    planes = NG // count
    per_piece = blocks // pieces
    strips = SPAN // LANES

    def load(step):
        part = pl.ds(step * GROUP, GROUP)
        return pltpu.make_async_copy(field_ref.at[part], field.at[part], field_sem.at[step])

    def fetch(ref, block):
        slot = lax.rem(block, RING)
        return pltpu.make_async_copy(ref.at[block], ring.at[slot], pair_sem.at[slot])

    for step in range(NG // GROUP):
        load(step).start()
    greet_all(count, me, place)

    lane = lax.broadcasted_iota(jnp.int32, (NG, LANES), 1)
    row = lax.broadcasted_iota(jnp.int32, (NG, LANES), 0)
    sign = jnp.where(lane < HALF, 1.0, -1.0).astype(f32)
    wave_z = lax.rem(lane, HALF).astype(f32)
    wave_x = jnp.where(row < NG // 2, row, row - NG).astype(f32)
    plane_sq = wave_x * wave_x + wave_z * wave_z
    factor = NG / (2.0 * math.pi) * (NG / (2.0 * math.pi))

    def both(shapes):
        top = jnp.concatenate([part.astype(bf) for part in shapes], axis=1)
        turned = [(pltpu.roll(part, HALF, 1) * sign).astype(bf) for part in shapes]
        return jnp.concatenate([top, jnp.concatenate(turned, axis=1)], axis=0)

    def cut(sheet, k):
        return sheet[:, k * LANES : (k + 1) * LANES]

    def forward(step, carry):
        first = step * GROUP
        load(step).wait()
        data = field[pl.ds(first, GROUP)].reshape(GROUP * NG, LANES)
        a = lax.dot_general(data, tz_ref[...], NN, preferred_element_type=f32).astype(bf)
        top = [a[k * NG : (k + 1) * NG, :LANES] for k in range(GROUP)]
        low = [a[k * NG : (k + 1) * NG, LANES:] for k in range(GROUP)]
        stack = jnp.concatenate(
            [jnp.concatenate(top, axis=1), jnp.concatenate(low, axis=1)], axis=0
        )
        b = lax.dot_general(ty_ref[...], stack, NN, preferred_element_type=f32)
        for k in range(GROUP):
            by_y[pl.ds(first + k, NG, stride=NG), :] = cut(b, k)
        return carry

    lax.fori_loop(0, NG // GROUP, forward, 0)

    def prime(block, carry):
        fetch(early_ref, block).start()
        return carry

    lax.fori_loop(0, EARLY, prime, 0)

    def middle(step, carry):
        first = step * GROUP
        rows = [by_y[pl.ds((first + k) * NG, NG), :] for k in range(GROUP)]
        h = lax.dot_general(ty_ref[...], both(rows), NN, preferred_element_type=f32)
        scaled = []
        for k in range(GROUP):
            index = first + k
            wave_y = jnp.where(index < NG // 2, index, index - NG).astype(f32)
            squared = plane_sq + wave_y * wave_y
            kernel = jnp.where(squared > 0.5, factor / (squared + SCREEN), 0.0)
            scaled.append(cut(h, k) * kernel)
        g = lax.dot_general(tyi_ref[...], both(scaled), NN, preferred_element_type=f32)
        for k in range(GROUP):
            by_x[pl.ds(first + k, NG, stride=NG), :] = cut(g, k)
        return carry

    lax.fori_loop(0, NG // GROUP, middle, 0)
    wait_greeted(count)

    def own(piece):
        return pltpu.make_async_copy(pot.at[piece, me], land.at[piece, me], own_sem.at[piece])

    def send_piece(piece):
        def body(step, carry):
            peer = lax.rem(me + shift_of(step, count), count)
            pltpu.make_async_remote_copy(
                src_ref=pot.at[piece, peer],
                dst_ref=land.at[piece, me],
                send_sem=send_sem.at[piece],
                recv_sem=recv_sem.at[piece],
                device_id=place(peer),
                device_id_type=pl.DeviceIdType.MESH,
            ).start()
            return carry

        own(piece).start()
        lax.fori_loop(1, count, body, 0)

    quarter = NG // 4
    spot = lane[:quarter]

    def backward(local, carry):
        rows = [by_x[pl.ds((local + planes * k) * NG, NG), :] for k in range(count)]
        p = lax.dot_general(tyi_ref[...], both(rows), NN, preferred_element_type=f32).astype(bf)
        tall = jnp.concatenate([cut(p, k) for k in range(count)], axis=0)
        final = lax.dot_general(tall, tzi_ref[...], NN, preferred_element_type=f32)
        flat[...] = final * f32(1.0 / float(NG**3))
        for k in range(count):
            y0, y1, y2, y3 = [flat[pl.ds(k * NG + j, quarter, stride=4), :] for j in range(4)]
            y1, y2, y3 = pltpu.roll(y1, 96, 1), pltpu.roll(y2, 64, 1), pltpu.roll(y3, 32, 1)
            base = k % 4 * 3 * PIECE
            dense[pl.ds(base, quarter, stride=3), :] = jnp.where(spot < 96, y0, y1)
            dense[pl.ds(base + 1, quarter, stride=3), :] = jnp.where(spot < 64, y1, y2)
            dense[pl.ds(base + 2, quarter, stride=3), :] = jnp.where(spot < 32, y2, y3)
            for m in range(3):
                pot[local * 3 + m, k] = dense[base + m * PIECE : base + (m + 1) * PIECE, :].astype(bf)
        for m in range(3):
            send_piece(local * 3 + m)
        return carry

    lax.fori_loop(0, planes, backward, 0)
    total[...] = jnp.zeros_like(total)

    def work(piece, carry):
        own(piece).wait()
        others = land.at[piece, pl.ds(0, count - 1)]
        pltpu.make_async_copy(others, others, recv_sem.at[piece]).wait()
        wide[...] = land[piece].astype(f32).reshape(cols * PIECE, LANES)
        for half in range(per_piece):
            block = piece * per_piece + half
            slot = lax.rem(block, RING)
            pltpu.make_async_copy(ring.at[slot], ring.at[slot], pair_sem.at[slot]).wait()
            lines = [
                wide[pl.ds(half * strips + j, cols, stride=PIECE), :].astype(bf)
                for j in range(strips)
            ]
            total[...] += lax.dot_general(
                jnp.concatenate(lines, axis=1), ring[slot], NT, preferred_element_type=f32
            )

            @pl.when(block < rest)
            def _():
                fetch(pair_ref, block).start()

        return carry

    lax.fori_loop(0, pieces, work, 0)

    scale = f32(1.0 / math.sqrt(float(NG**3)))
    low_lane = lax.broadcasted_iota(jnp.int32, (cols // 2, LANES), 1) < share
    for k in range(npoints // LANES):
        tile = total[:, k * LANES : (k + 1) * LANES] * scale
        top, low = tile[: cols // 2], tile[cols // 2 :]
        parts[2 * k] = jnp.where(low_lane, top, pltpu.roll(low, share, 1))
        parts[2 * k + 1] = jnp.where(low_lane, pltpu.roll(top, share, 1), low)

    def part_copy(step, source, slot):
        peer = lax.rem(me + step, count)
        return pltpu.make_async_remote_copy(
            src_ref=parts.at[source],
            dst_ref=held.at[slot],
            send_sem=part_send.at[step],
            recv_sem=part_recv.at[step],
            device_id=place(peer),
            device_id_type=pl.DeviceIdType.MESH,
        )

    def part_start(step, carry):
        shift = shift_of(step, count)
        part_copy(shift, lax.rem(me + shift, count), me).start()
        return carry

    lax.fori_loop(1, count, part_start, 0)
    held[me] = parts[me]

    def drain_piece(piece, carry):
        sent = pot.at[piece, pl.ds(0, count - 1)]
        pltpu.make_async_copy(sent, sent, send_sem.at[piece]).wait()
        return carry

    lax.fori_loop(0, pieces, drain_piece, 0)

    def part_receive(step, carry):
        source = lax.rem(me + count - step, count)
        part_copy(step, source, source).wait_recv()
        return carry

    lax.fori_loop(1, count, part_receive, 0)
    summed = jnp.sum(held[...], axis=0)
    pile = jnp.concatenate([summed, pltpu.roll(summed, share, 1)], axis=0)
    o_ref[...] = pile.T[:share, :]

    def part_drain(step, carry):
        part_copy(step, lax.rem(me + step, count), me).wait_send()
        return carry

    lax.fori_loop(1, count, part_drain, 0)


def solve_and_project(field, early, pair, count):
    bf = jnp.bfloat16
    f32 = jnp.float32
    cos_tab, sin_tab = literal_tables(NG)
    keep = NG // 2 + 1

    def padded(table):
        return np.pad(table[:, :keep], ((0, LANES - NG), (0, HALF - keep)))

    cz, sz = padded(cos_tab), padded(sin_tab)
    tz = np.concatenate([cz, -sz, -sz, -cz], axis=1)
    ty = np.concatenate([cos_tab, sin_tab], axis=1)
    tyi = np.concatenate([cos_tab, -sin_tab], axis=1)
    spot = np.arange(HALF)[:, None]
    weight = np.where((spot == 0) | (spot == NG // 2), 1.0, 2.0).astype(bf)
    tzi = np.concatenate([cz.T * weight, -(sz.T * weight)], axis=0)
    tz, ty, tyi, tzi = [jnp.asarray(table, bf) for table in (tz, ty, tyi, tzi)]
    pieces = NG // count * 3
    blocks, npoints, span = pair.shape
    cols = count
    any_spec = pl.BlockSpec(memory_space=pl.ANY)
    vmem_spec = pl.BlockSpec(memory_space=pltpu.VMEM)
    return pl.pallas_call(
        solve_project_kernel,
        out_shape=jax.ShapeDtypeStruct((npoints // count, cols), f32),
        in_specs=[any_spec] + [vmem_spec] * 4 + [any_spec] * 2,
        out_specs=vmem_spec,
        scratch_shapes=[
            pltpu.VMEM((NG, NG, LANES), bf),
            pltpu.VMEM((NG * NG, LANES), f32),
            pltpu.VMEM((NG * NG, LANES), f32),
            pltpu.VMEM((count * NG, LANES), f32),
            pltpu.VMEM((4 * 3 * PIECE, LANES), f32),
            pltpu.VMEM((pieces, count, PIECE, LANES), bf),
            pltpu.VMEM((RING, npoints, span), bf),
            pltpu.VMEM((pieces, count, PIECE, LANES), bf),
            pltpu.VMEM((cols * PIECE, LANES), f32),
            pltpu.VMEM((cols, npoints), f32),
            pltpu.VMEM((count, cols // 2, LANES), f32),
            pltpu.VMEM((count, cols // 2, LANES), f32),
            pltpu.SemaphoreType.DMA((NG // GROUP,)),
            pltpu.SemaphoreType.DMA((pieces,)),
            pltpu.SemaphoreType.DMA((pieces,)),
            pltpu.SemaphoreType.DMA((pieces,)),
            pltpu.SemaphoreType.DMA((RING,)),
            pltpu.SemaphoreType.DMA((count,)),
            pltpu.SemaphoreType.DMA((count,)),
        ],
        compiler_params=pltpu.CompilerParams(
            collective_id=2, has_side_effects=True, vmem_limit_bytes=54 << 20
        ),
        name="solve_project",
    )(field.reshape(NG, NG, LANES), tz, ty, tyi, tzi, early, pair)


def fits_planes(rows, npoints, cols, count):
    blocks = rows // SPAN
    return (
        cols == count
        and count % 2 == 0
        and rows % (NG * NG) == 0
        and NG % (rows // (NG * NG)) == 0
        and blocks >= EARLY + 2 * JOIN
        and EARLY > JOIN
        and npoints % (count * ROWS) == 0
        and NG // LINES % JOIN == 0
        and npoints % TAKE == 0
        and 2 * npoints == count * LANES
    )


def shards(orbitals, inverse_panel, points):
    bf = jnp.bfloat16
    row_count = orbitals.shape[0]
    grid_count = lax.axis_size("grid")
    vec_count = lax.axis_size("vec")
    npoints = points.shape[0]
    offset = (lax.axis_index("grid") * vec_count + lax.axis_index("vec")) * row_count
    picked = pick_rows(orbitals, points, offset)
    cols = inverse_panel.shape[1]
    if fits_planes(row_count, npoints, cols, grid_count * vec_count):
        panel = inverse_panel.T
        point_rows, early, early_fit = share_rows(picked, grid_count, vec_count, panel, orbitals)
        pair, field = pair_and_fit(orbitals, point_rows, panel, early_fit)
        return solve_and_project(field, early, pair, grid_count * vec_count)
    point_rows = share_rows(picked, grid_count, vec_count)

    def pair_block(block):
        correlation = lax.dot_general(
            block, point_rows, (((1,), (1,)), ((), ())), preferred_element_type=jnp.float32
        )
        return (correlation * correlation).astype(bf)

    pair = lax.map(pair_block, orbitals.reshape(4, row_count // 4, orbitals.shape[1])).reshape(
        row_count, npoints
    )
    fit_cols = lax.dot_general(
        inverse_panel, pair, (((0,), (1,)), ((), ())), preferred_element_type=jnp.float32
    ).astype(bf)
    slab = lax.all_to_all(fit_cols, "vec", split_axis=0, concat_axis=1, tiled=True)
    col_local = slab.shape[0]
    planes = NG // grid_count
    field = slab.reshape(col_local, planes, NG, NG)
    cos_tab, sin_tab = wave_tables(NG)
    z_re = mult(field, cos_tab, "vxyz,zk->vxyk").astype(bf)
    z_im = (-mult(field, sin_tab, "vxyz,zk->vxyk")).astype(bf)
    y_re = (mult(z_re, cos_tab, "vxyz,yk->vxkz") + mult(z_im, sin_tab, "vxyz,yk->vxkz")).astype(bf)
    y_im = (mult(z_im, cos_tab, "vxyz,yk->vxkz") - mult(z_re, sin_tab, "vxyz,yk->vxkz")).astype(bf)
    stacked = jnp.stack([y_re, y_im])
    waves = wavenumber(lax.iota(jnp.int32, NG), NG)
    y_waves = wavenumber(lax.axis_index("grid") * planes + lax.iota(jnp.int32, planes), NG)
    kernel = screened(waves, y_waves, waves)[None]
    piece = lax.all_to_all(stacked, "grid", split_axis=3, concat_axis=2, tiled=True)
    p_re = piece[0]
    p_im = piece[1]
    x_re = mult(p_re, cos_tab, "vxyz,xk->vkyz") + mult(p_im, sin_tab, "vxyz,xk->vkyz")
    x_im = mult(p_im, cos_tab, "vxyz,xk->vkyz") - mult(p_re, sin_tab, "vxyz,xk->vkyz")
    q_re = (x_re * kernel).astype(bf)
    q_im = (x_im * kernel).astype(bf)
    i_re = (mult(q_re, cos_tab, "vxyz,xk->vkyz") - mult(q_im, sin_tab, "vxyz,xk->vkyz")).astype(bf)
    i_im = (mult(q_im, cos_tab, "vxyz,xk->vkyz") + mult(q_re, sin_tab, "vxyz,xk->vkyz")).astype(bf)
    spectrum = lax.all_to_all(
        jnp.stack([i_re, i_im]), "grid", split_axis=2, concat_axis=3, tiled=True
    )
    s_re = spectrum[0]
    s_im = spectrum[1]
    h_re = (mult(s_re, cos_tab, "vxyz,yk->vxkz") - mult(s_im, sin_tab, "vxyz,yk->vxkz")).astype(bf)
    h_im = (mult(s_im, cos_tab, "vxyz,yk->vxkz") + mult(s_re, sin_tab, "vxyz,yk->vxkz")).astype(bf)
    final = mult(h_re, cos_tab, "vxyz,zk->vxyk") - mult(h_im, sin_tab, "vxyz,zk->vxyk")
    potential = (final / float(NG**3)).astype(bf).reshape(col_local, planes * NG * NG)
    pot_rows = lax.all_to_all(potential, "vec", split_axis=1, concat_axis=0, tiled=True)
    return project(pair, pot_rows)


def solution(mesh):
    in_specs = (P(("grid", "vec"), None), P(), P())
    out_specs = P(("grid", "vec"), None)
    return jax.shard_map(shards, mesh=mesh, in_specs=in_specs, out_specs=out_specs, check_vma=False)
```

```python
import math

import jax
import jax.numpy as jnp
import numpy as np
from jax import lax
from jax.experimental import pallas as pl
from jax.experimental.pallas import tpu as pltpu
from jax.sharding import PartitionSpec as P

NG = 96


SCREEN = 2.25


def wave_tables(count):
    index = lax.iota(jnp.int32, count)
    phase = index[:, None] * index[None, :] % count
    angle = phase.astype(jnp.float32) * (2.0 * math.pi / count)
    return (jnp.cos(angle).astype(jnp.bfloat16), jnp.sin(angle).astype(jnp.bfloat16))


def literal_tables(count):
    index = np.arange(count)
    phase = index[:, None] * index[None, :] % count
    angle = phase.astype(np.float32) * np.float32(2.0 * math.pi / count)
    return np.cos(angle).astype(jnp.bfloat16), np.sin(angle).astype(jnp.bfloat16)


def wavenumber(index, count):
    return jnp.where(index < count // 2, index, index - count).astype(jnp.float32)


def screened(wave_x, wave_y, wave_z):
    squared = (
        wave_x[:, None, None] * wave_x[:, None, None]
        + wave_y[None, :, None] * wave_y[None, :, None]
        + wave_z[None, None, :] * wave_z[None, None, :]
    )
    factor = NG / (2.0 * math.pi) * (NG / (2.0 * math.pi))
    return jnp.where(squared > 0.5, factor / (squared + SCREEN), jnp.float32(0.0))


def mult(data, table, form):
    return jnp.einsum(form, data, table, preferred_element_type=jnp.float32)


LANES = 128


def exchange_kernel(axes, total, gather, x_ref, o_ref, held, send_sem, recv_sem, own_sem):
    if len(axes) == 2:
        vec_count = lax.axis_size("vec")
        count = lax.axis_size("grid") * vec_count
        me = lax.axis_index("grid") * vec_count + lax.axis_index("vec")
    else:
        count = lax.axis_size(axes[0])
        me = lax.axis_index(axes[0])
    land = held if total else o_ref

    def place(index):
        if len(axes) == 2:
            return (index // vec_count, lax.rem(index, vec_count))
        if axes[0] == "grid":
            return (index, lax.axis_index("vec"))
        return (lax.axis_index("grid"), index)

    def part(index):
        return x_ref if gather else x_ref.at[index]

    barrier = pltpu.get_barrier_semaphore()

    def greet(step, carry):
        pl.semaphore_signal(
            barrier,
            inc=1,
            device_id=place(lax.rem(me + step, count)),
            device_id_type=pl.DeviceIdType.MESH,
        )
        return carry

    lax.fori_loop(1, count, greet, 0)
    own = pltpu.make_async_copy(part(me), land.at[me], own_sem)
    own.start()
    pl.semaphore_wait(barrier, count - 1)

    def copy(step, source, slot):
        peer = lax.rem(me + step, count)
        return pltpu.make_async_remote_copy(
            src_ref=part(source),
            dst_ref=land.at[slot],
            send_sem=send_sem.at[step],
            recv_sem=recv_sem.at[step],
            device_id=place(peer),
            device_id_type=pl.DeviceIdType.MESH,
        )

    def send(step, carry):
        copy(step, lax.rem(me + step, count), me).start()
        return carry

    lax.fori_loop(1, count, send, 0)
    own.wait()

    def receive(step, carry):
        source = lax.rem(me + count - step, count)
        copy(step, source, source).wait_recv()
        return carry

    lax.fori_loop(1, count, receive, 0)
    if total:
        o_ref[...] = jnp.sum(held[...].astype(jnp.float32), axis=0).astype(o_ref.dtype)

    def drain(step, carry):
        copy(step, lax.rem(me + step, count), me).wait_send()
        return carry

    lax.fori_loop(1, count, drain, 0)


def exchange(blocks, ident, total=False, axes=("grid", "vec"), gather=False):
    rows, lanes = blocks.shape[-2:]
    count = 1
    for axis in axes:
        count *= lax.axis_size(axis)
    shape = (rows, lanes) if total else (count, rows, lanes)
    held_shape = blocks.shape if total else (1, 8, LANES)

    def body(*refs):
        exchange_kernel(axes, total, gather, *refs)

    return pl.pallas_call(
        body,
        out_shape=jax.ShapeDtypeStruct(shape, blocks.dtype),
        in_specs=[pl.BlockSpec(memory_space=pltpu.VMEM)],
        out_specs=pl.BlockSpec(memory_space=pltpu.VMEM),
        scratch_shapes=[
            pltpu.VMEM(held_shape, blocks.dtype),
            pltpu.SemaphoreType.DMA((count,)),
            pltpu.SemaphoreType.DMA((count,)),
            pltpu.SemaphoreType.DMA(()),
        ],
        compiler_params=pltpu.CompilerParams(
            collective_id=ident, has_side_effects=True, vmem_limit_bytes=32 << 20
        ),
        name="exchange_total" if total else "exchange_gather" if gather else "exchange_blocks",
    )(blocks)


def share_kernel(chunks, early, refs):
    if early:
        x_ref, panel_ref, orb_ref, o_ref, early_ref, lines_ref, fit_ref = refs[:7]
        orbs, pairs, fit_rows, orb_sem, pair_sem = refs[-5:]
        near, wide, far, sum1, sum2, sum3, sends, recvs, own_sem = refs[7:-5]
    else:
        x_ref, o_ref, near, wide, far, sum1, sum2, sum3, sends, recvs, own_sem = refs
    bf = jnp.bfloat16
    f32 = jnp.float32
    vec_count = lax.axis_size("vec")
    deep = lax.axis_size("grid") // 2
    grid_at, mine = lax.axis_index("grid"), lax.axis_index("vec")
    level, core = grid_at // 2, lax.rem(grid_at, 2)
    other = 1 - core
    across = vec_count - 1

    def partner(step):
        return (level * 2 + other, mine)

    def beside(step):
        return (grid_at, lax.rem(mine + step, vec_count))

    def above(step):
        return (lax.rem(level + step, deep) * 2 + core, mine)

    peers = [partner(1)]
    peers += [beside(step) for step in range(1, vec_count)]
    peers += [above(step) for step in range(1, deep)]
    barrier = pltpu.get_barrier_semaphore()
    for peer in peers:
        pl.semaphore_signal(barrier, inc=1, device_id=peer, device_id_type=pl.DeviceIdType.MESH)
    pl.semaphore_wait(barrier, len(peers))

    def send(source, target, slot, peer):
        return pltpu.make_async_remote_copy(
            src_ref=source,
            dst_ref=target,
            send_sem=sends.at[slot],
            recv_sem=recvs.at[slot],
            device_id=peer,
            device_id_type=pl.DeviceIdType.MESH,
        )

    per_chunk = 2 + 2 * across + 2 * (deep - 1)

    def copies(stage, c):
        base = c * per_chunk
        if stage == 0:
            return [send(x_ref.at[c, other], near.at[c], base, partner(1))]
        if stage == 1:
            return [
                send(
                    sum1.at[c, lax.rem(mine + step, vec_count)],
                    wide.at[c, step - 1],
                    base + step,
                    beside(step),
                )
                for step in range(1, vec_count)
            ]
        if stage == 2:
            return [
                send(
                    sum2.at[c, lax.rem(level + step, deep)],
                    far.at[c, step - 1],
                    base + across + step,
                    above(step),
                )
                for step in range(1, deep)
            ]
        base += across + deep
        if stage == 3:
            spot = o_ref.at[c, core, mine, level]
            return [send(sum3.at[c], spot, base + step - 1, above(step)) for step in range(1, deep)]
        base += deep - 1
        if stage == 4:
            spot = o_ref.at[c, core, mine]
            return [send(spot, spot, base + step - 1, beside(step)) for step in range(1, vec_count)]
        spot = o_ref.at[c, core]
        return [send(spot, spot, base + across, partner(1))]

    def own(c):
        return pltpu.make_async_copy(sum3.at[c], o_ref.at[c, core, mine, level], own_sem.at[c])

    def prepare(stage, c):
        for move in copies(stage - 1, c):
            move.wait_recv()
        if stage == 1:
            sum1[c] = (x_ref[c, core].astype(f32) + near[c].astype(f32)).astype(bf)
        if stage == 2:
            total = sum1[c, mine].astype(f32)
            for step in range(across):
                total += wide[c, step].astype(f32)
            sum2[c] = total.astype(bf)
        if stage == 3:
            total = sum2[c, level].astype(f32)
            for step in range(deep - 1):
                total += far[c, step].astype(f32)
            sum3[c] = total.astype(bf)
            own(c).start()
        if stage == 4:
            own(c).wait()

    def fetch():
        return pltpu.make_async_copy(orb_ref.at[pl.ds(0, early)], orbs, orb_sem)

    def keep(c):
        height = pairs.shape[1] // chunks
        part = pl.ds(c * height, height)
        return pltpu.make_async_copy(
            pairs.at[:, part], early_ref.at[:, part], pair_sem.at[c]
        )

    def multiply(c):
        height = pairs.shape[1] // chunks
        rows = o_ref[c].reshape(height, o_ref.shape[-1])

        def body(e, carry):
            part = lax.dot_general(rows, orbs[e], NT, preferred_element_type=f32)
            pairs[e, c * height : (c + 1) * height, :] = (part * part).astype(bf)
            return carry

        lax.fori_loop(0, early, body, 0)

    if early:
        fetch().start()
    for tick in range(chunks + 6):
        for stage in range(6, -1, -1):
            c = tick - stage
            if 0 <= c < chunks:
                if stage > 0:
                    prepare(stage, c)
                if stage < 6:
                    for move in copies(stage, c):
                        move.start()
        if early and tick >= 6:
            if tick == 6:
                fetch().wait()
            multiply(tick - 6)
            keep(tick - 6).start()
    if early:

        fit_ref[...] = jnp.zeros_like(fit_ref)

        def fit(e, carry):
            begin = pl.multiple_of(jnp.maximum(e - 1, 0) * LINES, LINES)
            lines_ref[:, pl.ds(begin, LINES), :] = split_lines(fit_ref, fit_rows)
            fit_ref[...] = lax.dot_general(
                panel_ref[...], pairs[e], NN, preferred_element_type=f32
            )
            return carry

        lax.fori_loop(0, early, fit, 0)
        for c in range(chunks):
            keep(c).wait()
    for c in range(chunks):
        for stage in range(6):
            for move in copies(stage, c):
                move.wait_send()


ROWS = 16


def share_rows(picked, grid_count, vec_count, panel=None, orbitals=None):
    bf = jnp.bfloat16
    npoints, norb = picked.shape
    count = grid_count * vec_count
    if npoints % (count * ROWS) != 0 or grid_count % 2 != 0:
        return lax.psum(picked.astype(jnp.float32), ("grid", "vec")).astype(picked.dtype)
    early = 0 if panel is None else EARLY
    chunks = npoints // (count * ROWS)
    deep = grid_count // 2
    shape = (chunks, 2, vec_count, deep, ROWS, norb)
    slots = chunks * (2 + 2 * (vec_count - 1) + 2 * (deep - 1))
    vmem_spec = pl.BlockSpec(memory_space=pltpu.VMEM)
    any_spec = pl.BlockSpec(memory_space=pl.ANY)
    args = [picked.reshape(shape)]
    in_specs, out_specs = [vmem_spec], [vmem_spec]
    out_shape = [jax.ShapeDtypeStruct(shape, bf)]
    scratch = [
        pltpu.VMEM((chunks, vec_count, deep, ROWS, norb), bf),
        pltpu.VMEM((chunks, vec_count - 1, deep, ROWS, norb), bf),
        pltpu.VMEM((chunks, deep - 1, ROWS, norb), bf),
        pltpu.VMEM((chunks, vec_count, deep, ROWS, norb), bf),
        pltpu.VMEM((chunks, deep, ROWS, norb), bf),
        pltpu.VMEM((chunks, ROWS, norb), bf),
        pltpu.SemaphoreType.DMA((slots,)),
        pltpu.SemaphoreType.DMA((slots,)),
        pltpu.SemaphoreType.DMA((chunks,)),
    ]
    if early:
        cols = panel.shape[0]
        args += [panel, orbitals.reshape(-1, SPAN, norb)]
        in_specs += [vmem_spec, any_spec]
        out_specs += [any_spec, vmem_spec, vmem_spec]
        out_shape += [
            jax.ShapeDtypeStruct((early, npoints, SPAN), bf),
            jax.ShapeDtypeStruct((cols, (early - 1) * LINES, LANES), bf),
            jax.ShapeDtypeStruct((cols, SPAN), jnp.float32),
        ]
        scratch += [
            pltpu.VMEM((early, SPAN, norb), bf),
            pltpu.VMEM((early, npoints, SPAN), bf),
            pltpu.VMEM((cols * LINES, LANES), jnp.float32),
            pltpu.SemaphoreType.DMA(()),
            pltpu.SemaphoreType.DMA((chunks,)),
        ]

    def body(*refs):
        share_kernel(chunks, early, refs)

    outs = pl.pallas_call(
        body,
        out_shape=out_shape,
        in_specs=in_specs,
        out_specs=out_specs,
        scratch_shapes=scratch,
        compiler_params=pltpu.CompilerParams(
            collective_id=4, has_side_effects=True, vmem_limit_bytes=46 << 20
        ),
        name="share_rows",
    )(*args)
    rows = outs[0].reshape(npoints, norb)
    return (rows, *outs[1:]) if early else rows


OCTET = 8


def pick_kernel(points_ref, flags_ref, offset_ref, orb_ref, o_ref, found, where, spare, sheet, sem):
    octets, _, norb = orb_ref.shape
    limit = octets * OCTET
    npoints = o_ref.shape[0]
    offset = offset_ref[0]
    sheet[...] = jnp.zeros_like(sheet)

    def fetch(slot, octet):
        return pltpu.make_async_copy(orb_ref.at[octet], found.at[slot], sem)

    def look(i, held):
        position = points_ref[i] - offset
        inside = (position >= 0) & (position < limit)

        @pl.when(inside)
        def _():
            fetch(held, position // OCTET).start()
            where[held] = i
            spare[held] = lax.rem(position, OCTET)

        return held + inside.astype(jnp.int32)

    def scan(group, held):
        return lax.cond(
            flags_ref[group] > 0,
            lambda h: lax.fori_loop(
                0, OCTET, lambda k, n: look(group * OCTET + k, n), h, unroll=True
            ),
            lambda h: h,
            held,
        )

    held = lax.fori_loop(0, npoints // OCTET, scan, 0)

    def settle(slot, carry):
        fetch(slot, 0).wait()
        return carry

    lax.fori_loop(0, held, settle, 0)
    line = lax.broadcasted_iota(jnp.int32, (OCTET, norb), 0)

    def place(slot, carry):
        octet = found[slot].astype(jnp.float32)
        row = jnp.sum(jnp.where(line == spare[slot], octet, 0.0), axis=0, keepdims=True)
        sheet[pl.ds(where[slot], 1), :] = row
        return carry

    lax.fori_loop(0, held, place, 0)
    o_ref[...] = sheet[...].astype(o_ref.dtype)


def pick_rows(orbitals, points, offset):
    rows, norb = orbitals.shape
    npoints = points.shape[0]
    position = points - offset
    if rows % OCTET != 0 or npoints % OCTET != 0:
        inside = (position >= 0) & (position < rows)
        picked = jnp.take(orbitals, jnp.clip(position, 0, rows - 1), axis=0)
        return jnp.where(inside[:, None], picked, jnp.zeros_like(picked))
    inside = (position >= 0) & (position < rows)
    flags = jnp.max(inside.reshape(-1, OCTET).astype(jnp.int32), axis=1)
    return pl.pallas_call(
        pick_kernel,
        out_shape=jax.ShapeDtypeStruct((npoints, norb), orbitals.dtype),
        in_specs=[
            pl.BlockSpec(memory_space=pltpu.SMEM),
            pl.BlockSpec(memory_space=pltpu.SMEM),
            pl.BlockSpec(memory_space=pltpu.SMEM),
            pl.BlockSpec(memory_space=pl.ANY),
        ],
        out_specs=pl.BlockSpec(memory_space=pltpu.VMEM),
        scratch_shapes=[
            pltpu.VMEM((npoints, OCTET, norb), orbitals.dtype),
            pltpu.SMEM((npoints,), jnp.int32),
            pltpu.SMEM((npoints,), jnp.int32),
            pltpu.VMEM((npoints, norb), jnp.float32),
            pltpu.SemaphoreType.DMA(()),
        ],
        compiler_params=pltpu.CompilerParams(vmem_limit_bytes=28 << 20),
        name="pick_rows",
    )(points, flags, offset[None].astype(jnp.int32), orbitals.reshape(rows // OCTET, OCTET, norb))


def project(pair, pot_rows):
    scale = 1.0 / math.sqrt(float(NG**3))
    term = lax.dot_general(
        pair, pot_rows, (((0,), (1,)), ((), ())), preferred_element_type=jnp.float32
    )
    term = term * jnp.float32(scale)
    npoints, cols = term.shape
    count = lax.axis_size("grid") * lax.axis_size("vec")
    share = npoints // count
    if share * cols % LANES == 0:
        blocks = term.reshape(count, share * cols // LANES, LANES)
        return exchange(blocks, 3, True).reshape(share, cols)
    partial_block = lax.psum_scatter(term, "grid", scatter_dimension=0, tiled=True)
    return lax.psum_scatter(partial_block, "vec", scatter_dimension=0, tiled=True)


def peers_of():
    vec_count = lax.axis_size("vec")
    count = lax.axis_size("grid") * vec_count
    me = lax.axis_index("grid") * vec_count + lax.axis_index("vec")

    def place(index):
        return (index // vec_count, lax.rem(index, vec_count))

    return count, me, place


def greet_all(count, me, place):
    barrier = pltpu.get_barrier_semaphore()

    def greet(step, carry):
        pl.semaphore_signal(
            barrier,
            inc=1,
            device_id=place(lax.rem(me + step, count)),
            device_id_type=pl.DeviceIdType.MESH,
        )
        return carry

    lax.fori_loop(1, count, greet, 0)


def wait_greeted(count):
    pl.semaphore_wait(pltpu.get_barrier_semaphore(), count - 1)


NT = (((1,), (1,)), ((), ()))
NN = (((1,), (0,)), ((), ()))
LINES = 16
SPAN = LINES * NG
TAKE = 512
JOIN = 3
EARLY = 4


def split_lines(fit_ref, fit_rows):
    cols = fit_ref.shape[0]
    for line in range(LINES):
        begin = line * NG
        low = begin // LANES * LANES
        turn = begin - low
        wide = fit_ref[:, low : min(low + 2 * LANES, SPAN)]
        if wide.shape[1] == LANES:
            wide = jnp.concatenate([wide, wide], axis=1)
        if turn:
            wide = pltpu.roll(wide, 2 * LANES - turn, 1)
        fit_rows[pl.ds(line, cols, stride=LINES), :] = wide[:, :LANES]
    return fit_rows[...].astype(jnp.bfloat16).reshape(cols, LINES, LANES)


def pair_fit_kernel(
    orb_ref, rows_ref, panel_ref, early_ref, last_ref, pair_ref, field_ref, fit_buf, fit_rows, out_buf,
    send_sem, recv_sem, own_sem,
):
    bf = jnp.bfloat16
    block = pl.program_id(0) + EARLY
    blocks = pl.num_programs(0) + EARLY
    count, me, place = peers_of()
    npoints = rows_ref.shape[0]
    cols = panel_ref.shape[0]
    per_plane = NG // LINES
    groups = blocks // JOIN
    tall = JOIN * LINES

    def send(group, begin, lines, source=None):
        slot = lax.rem(group, 2)
        source = out_buf.at[slot] if source is None else source
        start = pl.multiple_of(lax.rem(group * JOIN, per_plane) * LINES + begin, LINES)
        target = field_ref.at[me, group * JOIN // per_plane, pl.ds(start, lines)]

        def body(step, carry):
            peer = lax.rem(me + step, count)
            pltpu.make_async_remote_copy(
                src_ref=source.at[peer, pl.ds(begin, lines)],
                dst_ref=target,
                send_sem=send_sem.at[slot],
                recv_sem=recv_sem.at[me],
                device_id=place(peer),
                device_id_type=pl.DeviceIdType.MESH,
            ).start()
            return carry

        pltpu.make_async_copy(
            source.at[me, pl.ds(begin, lines)], target, own_sem.at[slot]
        ).start()
        lax.fori_loop(1, count, body, 0, unroll=True)

    def drain(group):
        slot = lax.rem(group, 2)
        sent = out_buf.at[slot, pl.ds(0, count - 1)]
        mine = out_buf.at[slot, me]
        pltpu.make_async_copy(mine, mine, own_sem.at[slot]).wait()
        pltpu.make_async_copy(sent, sent, send_sem.at[slot]).wait()

    @pl.when(block == EARLY)
    def _():
        greet_all(count, me, place)

    before = block - 1

    @pl.when((block > 2 * JOIN) & (lax.rem(before, JOIN) == 0))
    def _():
        drain(before // JOIN - 2)

    def multiply(first):
        part = lax.dot_general(
            rows_ref[first : first + TAKE, :], orb_ref[...], NT, preferred_element_type=jnp.float32
        )
        pair_ref[0, first : first + TAKE, :] = (part * part).astype(bf)

    def arrange(index):
        begin = pl.multiple_of(lax.rem(index, JOIN) * LINES, LINES)
        out_buf[lax.rem(index // JOIN, 2), :, pl.ds(begin, LINES), :] = split_lines(
            fit_buf, fit_rows
        )

    @pl.when(block == EARLY)
    def _():
        fit_buf[...] = last_ref[...]

    multiply(0)
    arrange(before)
    for first in range(TAKE, npoints // 2, TAKE):
        multiply(first)

    @pl.when(block == EARLY)
    def _():
        wait_greeted(count)
        send(0, 0, tall, early_ref)

    @pl.when((block > EARLY) & (lax.rem(block, JOIN) == 0))
    def _():
        send(block // JOIN - 1, 0, tall)

    for late in range(JOIN - 1):

        @pl.when(block == blocks - JOIN + 1 + late)
        def _(late=late):
            send(groups - 1, late * LINES, LINES)

    for first in range(npoints // 2, npoints, TAKE):
        multiply(first)
    fit_buf[...] = lax.dot_general(
        panel_ref[...], pair_ref[0], NN, preferred_element_type=jnp.float32
    )

    @pl.when(block == blocks - 1)
    def _():
        arrange(block)
        send(groups - 1, (JOIN - 1) * LINES, LINES)

        def receive(step, carry):
            source = lax.rem(me + count - step, count)
            land = field_ref.at[source]
            pltpu.make_async_copy(land, land, recv_sem.at[source]).wait()
            return carry

        lax.fori_loop(1, count, receive, 0)
        drain(groups - 2)
        drain(groups - 1)


def pair_and_fit(orbitals, point_rows, panel, early_fit, last_fit):
    bf = jnp.bfloat16
    rows, norb = orbitals.shape
    npoints = point_rows.shape[0]
    cols = panel.shape[0]
    blocks = rows // SPAN - EARLY
    planes = rows // (NG * NG)
    count = lax.axis_size("grid") * lax.axis_size("vec")
    return pl.pallas_call(
        pair_fit_kernel,
        grid=(blocks,),
        in_specs=[
            pl.BlockSpec((SPAN, norb), lambda i: (i + EARLY, 0)),
            pl.BlockSpec((npoints, norb), lambda i: (0, 0)),
            pl.BlockSpec((cols, npoints), lambda i: (0, 0)),
            pl.BlockSpec((cols, JOIN * LINES, LANES), lambda i: (0, 0, 0)),
            pl.BlockSpec((cols, SPAN), lambda i: (0, 0)),
        ],
        out_specs=[
            pl.BlockSpec((1, npoints, SPAN), lambda i: (i, 0, 0)),
            pl.BlockSpec(memory_space=pltpu.HBM),
        ],
        out_shape=[
            jax.ShapeDtypeStruct((blocks, npoints, SPAN), bf),
            jax.ShapeDtypeStruct((count, planes, NG, LANES), bf),
        ],
        scratch_shapes=[
            pltpu.VMEM((cols, SPAN), jnp.float32),
            pltpu.VMEM((cols * LINES, LANES), jnp.float32),
            pltpu.VMEM((2, cols, JOIN * LINES, LANES), bf),
            pltpu.SemaphoreType.DMA((2,)),
            pltpu.SemaphoreType.DMA((count,)),
            pltpu.SemaphoreType.DMA((2,)),
        ],
        compiler_params=pltpu.CompilerParams(
            collective_id=1, has_side_effects=True, vmem_limit_bytes=50 << 20
        ),
        name="pair_fit_send",
    )(orbitals, point_rows, panel, early_fit, last_fit)


GROUP = 24
HALF = 64
PIECE = NG * NG // LANES // 3
RING = EARLY


def solve_project_kernel(
    field_ref, tz_ref, ty_ref, tyi_ref, tzi_ref, early_ref, pair_ref, o_ref,
    field, by_y, by_x, flat, dense, pot, ring, land, wide, total, parts, held,
    field_sem, send_sem, recv_sem, own_sem, pair_sem, part_send, part_recv,
):
    bf = jnp.bfloat16
    f32 = jnp.float32
    count, me, place = peers_of()
    rest, npoints, _ = pair_ref.shape
    blocks = rest + EARLY
    pieces = pot.shape[0]
    cols = count
    share = npoints // count
    planes = NG // count
    per_piece = blocks // pieces
    strips = SPAN // LANES

    def load(step):
        part = pl.ds(step * GROUP, GROUP)
        return pltpu.make_async_copy(field_ref.at[part], field.at[part], field_sem.at[step])

    def fetch(ref, block):
        slot = lax.rem(block, RING)
        return pltpu.make_async_copy(ref.at[block], ring.at[slot], pair_sem.at[slot])

    for step in range(NG // GROUP):
        load(step).start()
    greet_all(count, me, place)

    lane = lax.broadcasted_iota(jnp.int32, (NG, LANES), 1)
    row = lax.broadcasted_iota(jnp.int32, (NG, LANES), 0)
    sign = jnp.where(lane < HALF, 1.0, -1.0).astype(f32)
    wave_z = lax.rem(lane, HALF).astype(f32)
    wave_x = jnp.where(row < NG // 2, row, row - NG).astype(f32)
    plane_sq = wave_x * wave_x + wave_z * wave_z
    factor = NG / (2.0 * math.pi) * (NG / (2.0 * math.pi))

    def both(shapes):
        top = jnp.concatenate([part.astype(bf) for part in shapes], axis=1)
        turned = [(pltpu.roll(part, HALF, 1) * sign).astype(bf) for part in shapes]
        return jnp.concatenate([top, jnp.concatenate(turned, axis=1)], axis=0)

    def cut(sheet, k):
        return sheet[:, k * LANES : (k + 1) * LANES]

    def forward(step, carry):
        first = step * GROUP
        load(step).wait()
        data = field[pl.ds(first, GROUP)].reshape(GROUP * NG, LANES)
        a = lax.dot_general(data, tz_ref[...], NN, preferred_element_type=f32).astype(bf)
        top = [a[k * NG : (k + 1) * NG, :LANES] for k in range(GROUP)]
        low = [a[k * NG : (k + 1) * NG, LANES:] for k in range(GROUP)]
        stack = jnp.concatenate(
            [jnp.concatenate(top, axis=1), jnp.concatenate(low, axis=1)], axis=0
        )
        b = lax.dot_general(ty_ref[...], stack, NN, preferred_element_type=f32)
        for k in range(GROUP):
            by_y[pl.ds(first + k, NG, stride=NG), :] = cut(b, k)
        return carry

    lax.fori_loop(0, NG // GROUP, forward, 0)

    def prime(block, carry):
        fetch(early_ref, block).start()
        return carry

    lax.fori_loop(0, EARLY, prime, 0)

    def middle(step, carry):
        first = step * GROUP
        rows = [by_y[pl.ds((first + k) * NG, NG), :] for k in range(GROUP)]
        h = lax.dot_general(ty_ref[...], both(rows), NN, preferred_element_type=f32)
        scaled = []
        for k in range(GROUP):
            index = first + k
            wave_y = jnp.where(index < NG // 2, index, index - NG).astype(f32)
            squared = plane_sq + wave_y * wave_y
            kernel = jnp.where(squared > 0.5, factor / (squared + SCREEN), 0.0)
            scaled.append(cut(h, k) * kernel)
        g = lax.dot_general(tyi_ref[...], both(scaled), NN, preferred_element_type=f32)
        for k in range(GROUP):
            by_x[pl.ds(first + k, NG, stride=NG), :] = cut(g, k)
        return carry

    lax.fori_loop(0, NG // GROUP, middle, 0)
    wait_greeted(count)

    def own(piece):
        return pltpu.make_async_copy(pot.at[piece, me], land.at[piece, me], own_sem.at[piece])

    def send_piece(piece):
        def body(step, carry):
            peer = lax.rem(me + step, count)
            pltpu.make_async_remote_copy(
                src_ref=pot.at[piece, peer],
                dst_ref=land.at[piece, me],
                send_sem=send_sem.at[piece],
                recv_sem=recv_sem.at[piece],
                device_id=place(peer),
                device_id_type=pl.DeviceIdType.MESH,
            ).start()
            return carry

        own(piece).start()
        lax.fori_loop(1, count, body, 0)

    quarter = NG // 4
    spot = lane[:quarter]

    def backward(local, carry):
        rows = [by_x[pl.ds((local + planes * k) * NG, NG), :] for k in range(count)]
        p = lax.dot_general(tyi_ref[...], both(rows), NN, preferred_element_type=f32).astype(bf)
        tall = jnp.concatenate([cut(p, k) for k in range(count)], axis=0)
        final = lax.dot_general(tall, tzi_ref[...], NN, preferred_element_type=f32)
        flat[...] = final * f32(1.0 / float(NG**3))
        for k in range(count):
            y0, y1, y2, y3 = [flat[pl.ds(k * NG + j, quarter, stride=4), :] for j in range(4)]
            y1, y2, y3 = pltpu.roll(y1, 96, 1), pltpu.roll(y2, 64, 1), pltpu.roll(y3, 32, 1)
            base = k % 4 * 3 * PIECE
            dense[pl.ds(base, quarter, stride=3), :] = jnp.where(spot < 96, y0, y1)
            dense[pl.ds(base + 1, quarter, stride=3), :] = jnp.where(spot < 64, y1, y2)
            dense[pl.ds(base + 2, quarter, stride=3), :] = jnp.where(spot < 32, y2, y3)
            for m in range(3):
                pot[local * 3 + m, k] = dense[base + m * PIECE : base + (m + 1) * PIECE, :].astype(bf)
        for m in range(3):
            send_piece(local * 3 + m)
        return carry

    lax.fori_loop(0, planes, backward, 0)
    total[...] = jnp.zeros_like(total)

    def work(piece, carry):
        own(piece).wait()
        others = land.at[piece, pl.ds(0, count - 1)]
        pltpu.make_async_copy(others, others, recv_sem.at[piece]).wait()
        wide[...] = land[piece].astype(f32).reshape(cols * PIECE, LANES)
        for half in range(per_piece):
            block = piece * per_piece + half
            slot = lax.rem(block, RING)
            pltpu.make_async_copy(ring.at[slot], ring.at[slot], pair_sem.at[slot]).wait()
            lines = [
                wide[pl.ds(half * strips + j, cols, stride=PIECE), :].astype(bf)
                for j in range(strips)
            ]
            total[...] += lax.dot_general(
                jnp.concatenate(lines, axis=1), ring[slot], NT, preferred_element_type=f32
            )

            @pl.when(block < rest)
            def _():
                fetch(pair_ref, block).start()

        return carry

    lax.fori_loop(0, pieces, work, 0)

    scale = f32(1.0 / math.sqrt(float(NG**3)))
    low_lane = lax.broadcasted_iota(jnp.int32, (cols // 2, LANES), 1) < share
    for k in range(npoints // LANES):
        tile = total[:, k * LANES : (k + 1) * LANES] * scale
        top, low = tile[: cols // 2], tile[cols // 2 :]
        parts[2 * k] = jnp.where(low_lane, top, pltpu.roll(low, share, 1))
        parts[2 * k + 1] = jnp.where(low_lane, pltpu.roll(top, share, 1), low)

    def part_copy(step, source, slot):
        peer = lax.rem(me + step, count)
        return pltpu.make_async_remote_copy(
            src_ref=parts.at[source],
            dst_ref=held.at[slot],
            send_sem=part_send.at[step],
            recv_sem=part_recv.at[step],
            device_id=place(peer),
            device_id_type=pl.DeviceIdType.MESH,
        )

    def part_start(step, carry):
        part_copy(step, lax.rem(me + step, count), me).start()
        return carry

    lax.fori_loop(1, count, part_start, 0)
    held[me] = parts[me]

    def drain_piece(piece, carry):
        sent = pot.at[piece, pl.ds(0, count - 1)]
        pltpu.make_async_copy(sent, sent, send_sem.at[piece]).wait()
        return carry

    lax.fori_loop(0, pieces, drain_piece, 0)

    def part_receive(step, carry):
        source = lax.rem(me + count - step, count)
        part_copy(step, source, source).wait_recv()
        return carry

    lax.fori_loop(1, count, part_receive, 0)
    summed = jnp.sum(held[...], axis=0)
    pile = jnp.concatenate([summed, pltpu.roll(summed, share, 1)], axis=0)
    o_ref[...] = pile[:, :share]

    def part_drain(step, carry):
        part_copy(step, lax.rem(me + step, count), me).wait_send()
        return carry

    lax.fori_loop(1, count, part_drain, 0)


def solve_and_project(field, early, pair, count):
    bf = jnp.bfloat16
    f32 = jnp.float32
    cos_tab, sin_tab = literal_tables(NG)
    keep = NG // 2 + 1

    def padded(table):
        return np.pad(table[:, :keep], ((0, LANES - NG), (0, HALF - keep)))

    cz, sz = padded(cos_tab), padded(sin_tab)
    tz = np.concatenate([cz, -sz, -sz, -cz], axis=1)
    ty = np.concatenate([cos_tab, sin_tab], axis=1)
    tyi = np.concatenate([cos_tab, -sin_tab], axis=1)
    spot = np.arange(HALF)[:, None]
    weight = np.where((spot == 0) | (spot == NG // 2), 1.0, 2.0).astype(bf)
    tzi = np.concatenate([cz.T * weight, -(sz.T * weight)], axis=0)
    tz, ty, tyi, tzi = [jnp.asarray(table, bf) for table in (tz, ty, tyi, tzi)]
    pieces = NG // count * 3
    blocks, npoints, span = pair.shape
    cols = count
    any_spec = pl.BlockSpec(memory_space=pl.ANY)
    vmem_spec = pl.BlockSpec(memory_space=pltpu.VMEM)
    return pl.pallas_call(
        solve_project_kernel,
        out_shape=jax.ShapeDtypeStruct((cols, npoints // count), f32),
        in_specs=[any_spec] + [vmem_spec] * 4 + [any_spec] * 2,
        out_specs=vmem_spec,
        scratch_shapes=[
            pltpu.VMEM((NG, NG, LANES), bf),
            pltpu.VMEM((NG * NG, LANES), f32),
            pltpu.VMEM((NG * NG, LANES), f32),
            pltpu.VMEM((count * NG, LANES), f32),
            pltpu.VMEM((4 * 3 * PIECE, LANES), f32),
            pltpu.VMEM((pieces, count, PIECE, LANES), bf),
            pltpu.VMEM((RING, npoints, span), bf),
            pltpu.VMEM((pieces, count, PIECE, LANES), bf),
            pltpu.VMEM((cols * PIECE, LANES), f32),
            pltpu.VMEM((cols, npoints), f32),
            pltpu.VMEM((count, cols // 2, LANES), f32),
            pltpu.VMEM((count, cols // 2, LANES), f32),
            pltpu.SemaphoreType.DMA((NG // GROUP,)),
            pltpu.SemaphoreType.DMA((pieces,)),
            pltpu.SemaphoreType.DMA((pieces,)),
            pltpu.SemaphoreType.DMA((pieces,)),
            pltpu.SemaphoreType.DMA((RING,)),
            pltpu.SemaphoreType.DMA((count,)),
            pltpu.SemaphoreType.DMA((count,)),
        ],
        compiler_params=pltpu.CompilerParams(
            collective_id=2, has_side_effects=True, vmem_limit_bytes=54 << 20
        ),
        name="solve_project",
    )(field.reshape(NG, NG, LANES), tz, ty, tyi, tzi, early, pair).T


def fits_planes(rows, npoints, cols, count):
    blocks = rows // SPAN
    return (
        cols == count
        and rows % (NG * NG) == 0
        and NG % (rows // (NG * NG)) == 0
        and blocks >= EARLY + 2 * JOIN
        and EARLY == JOIN + 1
        and npoints % (count * ROWS) == 0
        and NG // LINES % JOIN == 0
        and npoints % TAKE == 0
        and 2 * npoints == count * LANES
    )


def shards(orbitals, inverse_panel, points):
    bf = jnp.bfloat16
    row_count = orbitals.shape[0]
    grid_count = lax.axis_size("grid")
    vec_count = lax.axis_size("vec")
    npoints = points.shape[0]
    offset = (lax.axis_index("grid") * vec_count + lax.axis_index("vec")) * row_count
    picked = pick_rows(orbitals, points, offset)
    cols = inverse_panel.shape[1]
    if fits_planes(row_count, npoints, cols, grid_count * vec_count):
        panel = inverse_panel.T
        point_rows, early, *fits = share_rows(picked, grid_count, vec_count, panel, orbitals)
        pair, field = pair_and_fit(orbitals, point_rows, panel, *fits)
        return solve_and_project(field, early, pair, grid_count * vec_count)
    point_rows = share_rows(picked, grid_count, vec_count)

    def pair_block(block):
        correlation = lax.dot_general(
            block, point_rows, (((1,), (1,)), ((), ())), preferred_element_type=jnp.float32
        )
        return (correlation * correlation).astype(bf)

    pair = lax.map(pair_block, orbitals.reshape(4, row_count // 4, orbitals.shape[1])).reshape(
        row_count, npoints
    )
    fit_cols = lax.dot_general(
        inverse_panel, pair, (((0,), (1,)), ((), ())), preferred_element_type=jnp.float32
    ).astype(bf)
    slab = lax.all_to_all(fit_cols, "vec", split_axis=0, concat_axis=1, tiled=True)
    col_local = slab.shape[0]
    planes = NG // grid_count
    field = slab.reshape(col_local, planes, NG, NG)
    cos_tab, sin_tab = wave_tables(NG)
    z_re = mult(field, cos_tab, "vxyz,zk->vxyk").astype(bf)
    z_im = (-mult(field, sin_tab, "vxyz,zk->vxyk")).astype(bf)
    y_re = (mult(z_re, cos_tab, "vxyz,yk->vxkz") + mult(z_im, sin_tab, "vxyz,yk->vxkz")).astype(bf)
    y_im = (mult(z_im, cos_tab, "vxyz,yk->vxkz") - mult(z_re, sin_tab, "vxyz,yk->vxkz")).astype(bf)
    stacked = jnp.stack([y_re, y_im])
    waves = wavenumber(lax.iota(jnp.int32, NG), NG)
    y_waves = wavenumber(lax.axis_index("grid") * planes + lax.iota(jnp.int32, planes), NG)
    kernel = screened(waves, y_waves, waves)[None]
    piece = lax.all_to_all(stacked, "grid", split_axis=3, concat_axis=2, tiled=True)
    p_re = piece[0]
    p_im = piece[1]
    x_re = mult(p_re, cos_tab, "vxyz,xk->vkyz") + mult(p_im, sin_tab, "vxyz,xk->vkyz")
    x_im = mult(p_im, cos_tab, "vxyz,xk->vkyz") - mult(p_re, sin_tab, "vxyz,xk->vkyz")
    q_re = (x_re * kernel).astype(bf)
    q_im = (x_im * kernel).astype(bf)
    i_re = (mult(q_re, cos_tab, "vxyz,xk->vkyz") - mult(q_im, sin_tab, "vxyz,xk->vkyz")).astype(bf)
    i_im = (mult(q_im, cos_tab, "vxyz,xk->vkyz") + mult(q_re, sin_tab, "vxyz,xk->vkyz")).astype(bf)
    spectrum = lax.all_to_all(
        jnp.stack([i_re, i_im]), "grid", split_axis=2, concat_axis=3, tiled=True
    )
    s_re = spectrum[0]
    s_im = spectrum[1]
    h_re = (mult(s_re, cos_tab, "vxyz,yk->vxkz") - mult(s_im, sin_tab, "vxyz,yk->vxkz")).astype(bf)
    h_im = (mult(s_im, cos_tab, "vxyz,yk->vxkz") + mult(s_re, sin_tab, "vxyz,yk->vxkz")).astype(bf)
    final = mult(h_re, cos_tab, "vxyz,zk->vxyk") - mult(h_im, sin_tab, "vxyz,zk->vxyk")
    potential = (final / float(NG**3)).astype(bf).reshape(col_local, planes * NG * NG)
    pot_rows = lax.all_to_all(potential, "vec", split_axis=1, concat_axis=0, tiled=True)
    return project(pair, pot_rows)


def solution(mesh):
    in_specs = (P(("grid", "vec"), None), P(), P())
    out_specs = P(("grid", "vec"), None)
    return jax.shard_map(shards, mesh=mesh, in_specs=in_specs, out_specs=out_specs, check_vma=False)
```

```python
import math

import jax
import jax.numpy as jnp
import numpy as np
from jax import lax
from jax.experimental import pallas as pl
from jax.experimental.pallas import tpu as pltpu
from jax.sharding import PartitionSpec as P

NG = 96


SCREEN = 2.25


def wave_tables(count):
    index = lax.iota(jnp.int32, count)
    phase = index[:, None] * index[None, :] % count
    angle = phase.astype(jnp.float32) * (2.0 * math.pi / count)
    return (jnp.cos(angle).astype(jnp.bfloat16), jnp.sin(angle).astype(jnp.bfloat16))


def literal_tables(count):
    index = np.arange(count)
    phase = index[:, None] * index[None, :] % count
    angle = phase.astype(np.float32) * np.float32(2.0 * math.pi / count)
    return np.cos(angle).astype(jnp.bfloat16), np.sin(angle).astype(jnp.bfloat16)


def wavenumber(index, count):
    return jnp.where(index < count // 2, index, index - count).astype(jnp.float32)


def screened(wave_x, wave_y, wave_z):
    squared = (
        wave_x[:, None, None] * wave_x[:, None, None]
        + wave_y[None, :, None] * wave_y[None, :, None]
        + wave_z[None, None, :] * wave_z[None, None, :]
    )
    factor = NG / (2.0 * math.pi) * (NG / (2.0 * math.pi))
    return jnp.where(squared > 0.5, factor / (squared + SCREEN), jnp.float32(0.0))


def mult(data, table, form):
    return jnp.einsum(form, data, table, preferred_element_type=jnp.float32)


LANES = 128


def exchange_kernel(axes, total, gather, x_ref, o_ref, held, send_sem, recv_sem, own_sem):
    if len(axes) == 2:
        vec_count = lax.axis_size("vec")
        count = lax.axis_size("grid") * vec_count
        me = lax.axis_index("grid") * vec_count + lax.axis_index("vec")
    else:
        count = lax.axis_size(axes[0])
        me = lax.axis_index(axes[0])
    land = held if total else o_ref

    def place(index):
        if len(axes) == 2:
            return (index // vec_count, lax.rem(index, vec_count))
        if axes[0] == "grid":
            return (index, lax.axis_index("vec"))
        return (lax.axis_index("grid"), index)

    def part(index):
        return x_ref if gather else x_ref.at[index]

    barrier = pltpu.get_barrier_semaphore()

    def greet(step, carry):
        pl.semaphore_signal(
            barrier,
            inc=1,
            device_id=place(lax.rem(me + step, count)),
            device_id_type=pl.DeviceIdType.MESH,
        )
        return carry

    lax.fori_loop(1, count, greet, 0)
    own = pltpu.make_async_copy(part(me), land.at[me], own_sem)
    own.start()
    pl.semaphore_wait(barrier, count - 1)

    def copy(step, source, slot):
        peer = lax.rem(me + step, count)
        return pltpu.make_async_remote_copy(
            src_ref=part(source),
            dst_ref=land.at[slot],
            send_sem=send_sem.at[step],
            recv_sem=recv_sem.at[step],
            device_id=place(peer),
            device_id_type=pl.DeviceIdType.MESH,
        )

    def send(step, carry):
        copy(step, lax.rem(me + step, count), me).start()
        return carry

    lax.fori_loop(1, count, send, 0)
    own.wait()

    def receive(step, carry):
        source = lax.rem(me + count - step, count)
        copy(step, source, source).wait_recv()
        return carry

    lax.fori_loop(1, count, receive, 0)
    if total:
        o_ref[...] = jnp.sum(held[...].astype(jnp.float32), axis=0).astype(o_ref.dtype)

    def drain(step, carry):
        copy(step, lax.rem(me + step, count), me).wait_send()
        return carry

    lax.fori_loop(1, count, drain, 0)


def exchange(blocks, ident, total=False, axes=("grid", "vec"), gather=False):
    rows, lanes = blocks.shape[-2:]
    count = 1
    for axis in axes:
        count *= lax.axis_size(axis)
    shape = (rows, lanes) if total else (count, rows, lanes)
    held_shape = blocks.shape if total else (1, 8, LANES)

    def body(*refs):
        exchange_kernel(axes, total, gather, *refs)

    return pl.pallas_call(
        body,
        out_shape=jax.ShapeDtypeStruct(shape, blocks.dtype),
        in_specs=[pl.BlockSpec(memory_space=pltpu.VMEM)],
        out_specs=pl.BlockSpec(memory_space=pltpu.VMEM),
        scratch_shapes=[
            pltpu.VMEM(held_shape, blocks.dtype),
            pltpu.SemaphoreType.DMA((count,)),
            pltpu.SemaphoreType.DMA((count,)),
            pltpu.SemaphoreType.DMA(()),
        ],
        compiler_params=pltpu.CompilerParams(
            collective_id=ident, has_side_effects=True, vmem_limit_bytes=32 << 20
        ),
        name="exchange_total" if total else "exchange_gather" if gather else "exchange_blocks",
    )(blocks)


def share_kernel(chunks, early, refs):
    if early:
        x_ref, panel_ref, orb_ref, o_ref, early_ref, lines_ref, fit_ref = refs[:7]
        orbs, pairs, fit_rows, orb_sem, pair_sem = refs[-5:]
        near, wide, far, sum1, sum2, sum3, sends, recvs, own_sem = refs[7:-5]
    else:
        x_ref, o_ref, near, wide, far, sum1, sum2, sum3, sends, recvs, own_sem = refs
    bf = jnp.bfloat16
    f32 = jnp.float32
    vec_count = lax.axis_size("vec")
    deep = lax.axis_size("grid") // 2
    grid_at, mine = lax.axis_index("grid"), lax.axis_index("vec")
    level, core = grid_at // 2, lax.rem(grid_at, 2)
    other = 1 - core
    across = vec_count - 1

    def partner(step):
        return (level * 2 + other, mine)

    def beside(step):
        return (grid_at, lax.rem(mine + step, vec_count))

    def above(step):
        return (lax.rem(level + step, deep) * 2 + core, mine)

    peers = [partner(1)]
    peers += [beside(step) for step in range(1, vec_count)]
    peers += [above(step) for step in range(1, deep)]
    barrier = pltpu.get_barrier_semaphore()
    for peer in peers:
        pl.semaphore_signal(barrier, inc=1, device_id=peer, device_id_type=pl.DeviceIdType.MESH)
    pl.semaphore_wait(barrier, len(peers))

    def send(source, target, slot, peer):
        return pltpu.make_async_remote_copy(
            src_ref=source,
            dst_ref=target,
            send_sem=sends.at[slot],
            recv_sem=recvs.at[slot],
            device_id=peer,
            device_id_type=pl.DeviceIdType.MESH,
        )

    per_chunk = 2 + 2 * across + 2 * (deep - 1)

    def copies(stage, c):
        base = c * per_chunk
        if stage == 0:
            return [send(x_ref.at[c, other], near.at[c], base, partner(1))]
        if stage == 1:
            return [
                send(
                    sum1.at[c, lax.rem(mine + step, vec_count)],
                    wide.at[c, step - 1],
                    base + step,
                    beside(step),
                )
                for step in range(1, vec_count)
            ]
        if stage == 2:
            return [
                send(
                    sum2.at[c, lax.rem(level + step, deep)],
                    far.at[c, step - 1],
                    base + across + step,
                    above(step),
                )
                for step in range(1, deep)
            ]
        base += across + deep
        if stage == 3:
            spot = o_ref.at[c, core, mine, level]
            return [send(sum3.at[c], spot, base + step - 1, above(step)) for step in range(1, deep)]
        base += deep - 1
        if stage == 4:
            spot = o_ref.at[c, core, mine]
            return [send(spot, spot, base + step - 1, beside(step)) for step in range(1, vec_count)]
        spot = o_ref.at[c, core]
        return [send(spot, spot, base + across, partner(1))]

    def own(c):
        return pltpu.make_async_copy(sum3.at[c], o_ref.at[c, core, mine, level], own_sem.at[c])

    def prepare(stage, c):
        for move in copies(stage - 1, c):
            move.wait_recv()
        if stage == 1:
            sum1[c] = (x_ref[c, core].astype(f32) + near[c].astype(f32)).astype(bf)
        if stage == 2:
            total = sum1[c, mine].astype(f32)
            for step in range(across):
                total += wide[c, step].astype(f32)
            sum2[c] = total.astype(bf)
        if stage == 3:
            total = sum2[c, level].astype(f32)
            for step in range(deep - 1):
                total += far[c, step].astype(f32)
            sum3[c] = total.astype(bf)
            own(c).start()
        if stage == 4:
            own(c).wait()

    def fetch():
        return pltpu.make_async_copy(orb_ref.at[pl.ds(0, early)], orbs, orb_sem)

    def keep(c):
        height = pairs.shape[1] // chunks
        part = pl.ds(c * height, height)
        return pltpu.make_async_copy(
            pairs.at[:, part], early_ref.at[:, part], pair_sem.at[c]
        )

    def multiply(c):
        height = pairs.shape[1] // chunks
        rows = o_ref[c].reshape(height, o_ref.shape[-1])

        def body(e, carry):
            part = lax.dot_general(rows, orbs[e], NT, preferred_element_type=f32)
            pairs[e, c * height : (c + 1) * height, :] = (part * part).astype(bf)
            return carry

        lax.fori_loop(0, early, body, 0)

    if early:
        fetch().start()
    for tick in range(chunks + 6):
        for stage in range(6, -1, -1):
            c = tick - stage
            if 0 <= c < chunks:
                if stage > 0:
                    prepare(stage, c)
                if stage < 6:
                    for move in copies(stage, c):
                        move.start()
        if early and tick >= 6:
            if tick == 6:
                fetch().wait()
            multiply(tick - 6)
            keep(tick - 6).start()
    if early:

        fit_ref[...] = jnp.zeros_like(fit_ref)

        def fit(e, carry):
            begin = pl.multiple_of(jnp.maximum(e - 1, 0) * LINES, LINES)
            lines_ref[:, pl.ds(begin, LINES), :] = split_lines(fit_ref, fit_rows)
            fit_ref[...] = lax.dot_general(
                panel_ref[...], pairs[e], NN, preferred_element_type=f32
            )
            return carry

        lax.fori_loop(0, early, fit, 0)
        for c in range(chunks):
            keep(c).wait()
    for c in range(chunks):
        for stage in range(6):
            for move in copies(stage, c):
                move.wait_send()


ROWS = 16


def share_rows(picked, grid_count, vec_count, panel=None, orbitals=None):
    bf = jnp.bfloat16
    npoints, norb = picked.shape
    count = grid_count * vec_count
    if npoints % (count * ROWS) != 0 or grid_count % 2 != 0:
        return lax.psum(picked.astype(jnp.float32), ("grid", "vec")).astype(picked.dtype)
    early = 0 if panel is None else EARLY
    chunks = npoints // (count * ROWS)
    deep = grid_count // 2
    shape = (chunks, 2, vec_count, deep, ROWS, norb)
    slots = chunks * (2 + 2 * (vec_count - 1) + 2 * (deep - 1))
    vmem_spec = pl.BlockSpec(memory_space=pltpu.VMEM)
    any_spec = pl.BlockSpec(memory_space=pl.ANY)
    args = [picked.reshape(shape)]
    in_specs, out_specs = [vmem_spec], [vmem_spec]
    out_shape = [jax.ShapeDtypeStruct(shape, bf)]
    scratch = [
        pltpu.VMEM((chunks, vec_count, deep, ROWS, norb), bf),
        pltpu.VMEM((chunks, vec_count - 1, deep, ROWS, norb), bf),
        pltpu.VMEM((chunks, deep - 1, ROWS, norb), bf),
        pltpu.VMEM((chunks, vec_count, deep, ROWS, norb), bf),
        pltpu.VMEM((chunks, deep, ROWS, norb), bf),
        pltpu.VMEM((chunks, ROWS, norb), bf),
        pltpu.SemaphoreType.DMA((slots,)),
        pltpu.SemaphoreType.DMA((slots,)),
        pltpu.SemaphoreType.DMA((chunks,)),
    ]
    if early:
        cols = panel.shape[0]
        args += [panel, orbitals.reshape(-1, SPAN, norb)]
        in_specs += [vmem_spec, any_spec]
        out_specs += [any_spec, vmem_spec, vmem_spec]
        out_shape += [
            jax.ShapeDtypeStruct((early, npoints, SPAN), bf),
            jax.ShapeDtypeStruct((cols, (early - 1) * LINES, LANES), bf),
            jax.ShapeDtypeStruct((cols, SPAN), jnp.float32),
        ]
        scratch += [
            pltpu.VMEM((early, SPAN, norb), bf),
            pltpu.VMEM((early, npoints, SPAN), bf),
            pltpu.VMEM((cols * LINES, LANES), jnp.float32),
            pltpu.SemaphoreType.DMA(()),
            pltpu.SemaphoreType.DMA((chunks,)),
        ]

    def body(*refs):
        share_kernel(chunks, early, refs)

    outs = pl.pallas_call(
        body,
        out_shape=out_shape,
        in_specs=in_specs,
        out_specs=out_specs,
        scratch_shapes=scratch,
        compiler_params=pltpu.CompilerParams(
            collective_id=4, has_side_effects=True, vmem_limit_bytes=46 << 20
        ),
        name="share_rows",
    )(*args)
    rows = outs[0].reshape(npoints, norb)
    return (rows, *outs[1:]) if early else rows


OCTET = 8


def pick_kernel(points_ref, flags_ref, offset_ref, orb_ref, o_ref, found, where, spare, sheet, sem):
    octets, _, norb = orb_ref.shape
    limit = octets * OCTET
    npoints = o_ref.shape[0]
    offset = offset_ref[0]
    sheet[...] = jnp.zeros_like(sheet)

    def fetch(slot, octet):
        return pltpu.make_async_copy(orb_ref.at[octet], found.at[slot], sem)

    def look(i, held):
        position = points_ref[i] - offset
        inside = (position >= 0) & (position < limit)

        @pl.when(inside)
        def _():
            fetch(held, position // OCTET).start()
            where[held] = i
            spare[held] = lax.rem(position, OCTET)

        return held + inside.astype(jnp.int32)

    def scan(group, held):
        return lax.cond(
            flags_ref[group] > 0,
            lambda h: lax.fori_loop(
                0, OCTET, lambda k, n: look(group * OCTET + k, n), h, unroll=True
            ),
            lambda h: h,
            held,
        )

    held = lax.fori_loop(0, npoints // OCTET, scan, 0)

    def settle(slot, carry):
        fetch(slot, 0).wait()
        return carry

    lax.fori_loop(0, held, settle, 0)
    line = lax.broadcasted_iota(jnp.int32, (OCTET, norb), 0)

    def place(slot, carry):
        octet = found[slot].astype(jnp.float32)
        row = jnp.sum(jnp.where(line == spare[slot], octet, 0.0), axis=0, keepdims=True)
        sheet[pl.ds(where[slot], 1), :] = row
        return carry

    lax.fori_loop(0, held, place, 0)
    o_ref[...] = sheet[...].astype(o_ref.dtype)


def pick_rows(orbitals, points, offset):
    rows, norb = orbitals.shape
    npoints = points.shape[0]
    position = points - offset
    if rows % OCTET != 0 or npoints % OCTET != 0:
        inside = (position >= 0) & (position < rows)
        picked = jnp.take(orbitals, jnp.clip(position, 0, rows - 1), axis=0)
        return jnp.where(inside[:, None], picked, jnp.zeros_like(picked))
    inside = (position >= 0) & (position < rows)
    flags = jnp.max(inside.reshape(-1, OCTET).astype(jnp.int32), axis=1)
    return pl.pallas_call(
        pick_kernel,
        out_shape=jax.ShapeDtypeStruct((npoints, norb), orbitals.dtype),
        in_specs=[
            pl.BlockSpec(memory_space=pltpu.SMEM),
            pl.BlockSpec(memory_space=pltpu.SMEM),
            pl.BlockSpec(memory_space=pltpu.SMEM),
            pl.BlockSpec(memory_space=pl.ANY),
        ],
        out_specs=pl.BlockSpec(memory_space=pltpu.VMEM),
        scratch_shapes=[
            pltpu.VMEM((npoints, OCTET, norb), orbitals.dtype),
            pltpu.SMEM((npoints,), jnp.int32),
            pltpu.SMEM((npoints,), jnp.int32),
            pltpu.VMEM((npoints, norb), jnp.float32),
            pltpu.SemaphoreType.DMA(()),
        ],
        compiler_params=pltpu.CompilerParams(vmem_limit_bytes=28 << 20),
        name="pick_rows",
    )(points, flags, offset[None].astype(jnp.int32), orbitals.reshape(rows // OCTET, OCTET, norb))


def project(pair, pot_rows):
    scale = 1.0 / math.sqrt(float(NG**3))
    term = lax.dot_general(
        pair, pot_rows, (((0,), (1,)), ((), ())), preferred_element_type=jnp.float32
    )
    term = term * jnp.float32(scale)
    npoints, cols = term.shape
    count = lax.axis_size("grid") * lax.axis_size("vec")
    share = npoints // count
    if share * cols % LANES == 0:
        blocks = term.reshape(count, share * cols // LANES, LANES)
        return exchange(blocks, 3, True).reshape(share, cols)
    partial_block = lax.psum_scatter(term, "grid", scatter_dimension=0, tiled=True)
    return lax.psum_scatter(partial_block, "vec", scatter_dimension=0, tiled=True)


def peers_of():
    vec_count = lax.axis_size("vec")
    count = lax.axis_size("grid") * vec_count
    me = lax.axis_index("grid") * vec_count + lax.axis_index("vec")

    def place(index):
        return (index // vec_count, lax.rem(index, vec_count))

    return count, me, place


def greet_all(count, me, place):
    barrier = pltpu.get_barrier_semaphore()

    def greet(step, carry):
        pl.semaphore_signal(
            barrier,
            inc=1,
            device_id=place(lax.rem(me + step, count)),
            device_id_type=pl.DeviceIdType.MESH,
        )
        return carry

    lax.fori_loop(1, count, greet, 0)


def wait_greeted(count):
    pl.semaphore_wait(pltpu.get_barrier_semaphore(), count - 1)


NT = (((1,), (1,)), ((), ()))
NN = (((1,), (0,)), ((), ()))
LINES = 16
SPAN = LINES * NG
TAKE = 512
JOIN = NG // LINES
TAIL = (3, 4, 5)
EARLY = 4


def split_lines(fit_ref, fit_rows):
    cols = fit_ref.shape[0]
    for line in range(LINES):
        begin = line * NG
        low = begin // LANES * LANES
        turn = begin - low
        wide = fit_ref[:, low : min(low + 2 * LANES, SPAN)]
        if wide.shape[1] == LANES:
            wide = jnp.concatenate([wide, wide], axis=1)
        if turn:
            wide = pltpu.roll(wide, 2 * LANES - turn, 1)
        fit_rows[pl.ds(line, cols, stride=LINES), :] = wide[:, :LANES]
    return fit_rows[...].astype(jnp.bfloat16).reshape(cols, LINES, LANES)


def pair_fit_kernel(
    orb_ref, rows_ref, panel_ref, early_ref, last_ref, pair_ref, field_ref, fit_buf, fit_rows, out_buf,
    send_sem, recv_sem, own_sem,
):
    bf = jnp.bfloat16
    block = pl.program_id(0) + EARLY
    blocks = pl.num_programs(0) + EARLY
    count, me, place = peers_of()
    npoints = rows_ref.shape[0]
    cols = panel_ref.shape[0]
    per_plane = NG // LINES
    groups = blocks // JOIN
    tall = JOIN * LINES

    def send(group, begin, lines):
        slot = lax.rem(group, 2)
        start = pl.multiple_of(lax.rem(group * JOIN, per_plane) * LINES + begin, LINES)
        target = field_ref.at[me, group * JOIN // per_plane, pl.ds(start, lines)]

        def body(step, carry):
            peer = lax.rem(me + step, count)
            pltpu.make_async_remote_copy(
                src_ref=out_buf.at[slot, peer, pl.ds(begin, lines)],
                dst_ref=target,
                send_sem=send_sem.at[slot],
                recv_sem=recv_sem.at[me],
                device_id=place(peer),
                device_id_type=pl.DeviceIdType.MESH,
            ).start()
            return carry

        pltpu.make_async_copy(
            out_buf.at[slot, me, pl.ds(begin, lines)], target, own_sem.at[slot]
        ).start()
        lax.fori_loop(1, count, body, 0, unroll=True)

    def drain(group):
        slot = lax.rem(group, 2)
        sent = out_buf.at[slot, pl.ds(0, count - 1)]
        mine = out_buf.at[slot, me]
        pltpu.make_async_copy(mine, mine, own_sem.at[slot]).wait()
        pltpu.make_async_copy(sent, sent, send_sem.at[slot]).wait()

    @pl.when(block == EARLY)
    def _():
        greet_all(count, me, place)

    before = block - 1

    @pl.when((block > 2 * JOIN) & (lax.rem(before, JOIN) == 0))
    def _():
        drain(before // JOIN - 2)

    def multiply(first):
        part = lax.dot_general(
            rows_ref[first : first + TAKE, :], orb_ref[...], NT, preferred_element_type=jnp.float32
        )
        pair_ref[0, first : first + TAKE, :] = (part * part).astype(bf)

    def arrange(index):
        begin = pl.multiple_of(lax.rem(index, JOIN) * LINES, LINES)
        out_buf[lax.rem(index // JOIN, 2), :, pl.ds(begin, LINES), :] = split_lines(
            fit_buf, fit_rows
        )

    @pl.when(block == EARLY)
    def _():
        fit_buf[...] = last_ref[...]
        out_buf[0, :, : (EARLY - 1) * LINES, :] = early_ref[...]

    multiply(0)
    arrange(before)
    for first in range(TAKE, npoints // 2, TAKE):
        multiply(first)

    @pl.when(block == EARLY + 1)
    def _():
        wait_greeted(count)

    @pl.when((block > EARLY) & (lax.rem(block, JOIN) == 0))
    def _():
        send(block // JOIN - 1, 0, tall)

    for start, stop in zip((0,) + TAIL, TAIL):

        @pl.when(block == blocks - JOIN + stop)
        def _(start=start, stop=stop):
            send(groups - 1, start * LINES, (stop - start) * LINES)

    for first in range(npoints // 2, npoints, TAKE):
        multiply(first)
    fit_buf[...] = lax.dot_general(
        panel_ref[...], pair_ref[0], NN, preferred_element_type=jnp.float32
    )

    @pl.when(block == blocks - 1)
    def _():
        arrange(block)
        send(groups - 1, TAIL[-1] * LINES, (JOIN - TAIL[-1]) * LINES)

        def receive(step, carry):
            source = lax.rem(me + count - step, count)
            land = field_ref.at[source]
            pltpu.make_async_copy(land, land, recv_sem.at[source]).wait()
            return carry

        lax.fori_loop(1, count, receive, 0)
        drain(groups - 2)
        drain(groups - 1)


def pair_and_fit(orbitals, point_rows, panel, early_fit, last_fit):
    bf = jnp.bfloat16
    rows, norb = orbitals.shape
    npoints = point_rows.shape[0]
    cols = panel.shape[0]
    blocks = rows // SPAN - EARLY
    planes = rows // (NG * NG)
    count = lax.axis_size("grid") * lax.axis_size("vec")
    return pl.pallas_call(
        pair_fit_kernel,
        grid=(blocks,),
        in_specs=[
            pl.BlockSpec((SPAN, norb), lambda i: (i + EARLY, 0)),
            pl.BlockSpec((npoints, norb), lambda i: (0, 0)),
            pl.BlockSpec((cols, npoints), lambda i: (0, 0)),
            pl.BlockSpec((cols, (EARLY - 1) * LINES, LANES), lambda i: (0, 0, 0)),
            pl.BlockSpec((cols, SPAN), lambda i: (0, 0)),
        ],
        out_specs=[
            pl.BlockSpec((1, npoints, SPAN), lambda i: (i, 0, 0)),
            pl.BlockSpec(memory_space=pltpu.HBM),
        ],
        out_shape=[
            jax.ShapeDtypeStruct((blocks, npoints, SPAN), bf),
            jax.ShapeDtypeStruct((count, planes, NG, LANES), bf),
        ],
        scratch_shapes=[
            pltpu.VMEM((cols, SPAN), jnp.float32),
            pltpu.VMEM((cols * LINES, LANES), jnp.float32),
            pltpu.VMEM((2, cols, JOIN * LINES, LANES), bf),
            pltpu.SemaphoreType.DMA((2,)),
            pltpu.SemaphoreType.DMA((count,)),
            pltpu.SemaphoreType.DMA((2,)),
        ],
        compiler_params=pltpu.CompilerParams(
            collective_id=1, has_side_effects=True, vmem_limit_bytes=50 << 20
        ),
        name="pair_fit_send",
    )(orbitals, point_rows, panel, early_fit, last_fit)


GROUP = 24
HALF = 64
THIRDS = 3
PIECE = NG * NG // LANES // THIRDS
RING = EARLY


def solve_project_kernel(
    field_ref, tz_ref, ty_ref, tyi_ref, tzi_ref, early_ref, pair_ref, o_ref,
    field, by_y, by_x, flat, dense, pot, ring, land, wide, total, parts, held,
    field_sem, send_sem, recv_sem, own_sem, pair_sem, part_send, part_recv,
):
    bf = jnp.bfloat16
    f32 = jnp.float32
    count, me, place = peers_of()
    rest, npoints, _ = pair_ref.shape
    blocks = rest + EARLY
    pieces = pot.shape[0]
    cols = count
    share = npoints // count
    planes = NG // count
    per_piece = blocks // pieces
    strips = SPAN // LANES

    def load(step):
        part = pl.ds(step * GROUP, GROUP)
        return pltpu.make_async_copy(field_ref.at[part], field.at[part], field_sem.at[step])

    def fetch(ref, block):
        slot = lax.rem(block, RING)
        return pltpu.make_async_copy(ref.at[block], ring.at[slot], pair_sem.at[slot])

    for step in range(NG // GROUP):
        load(step).start()
    greet_all(count, me, place)

    lane = lax.broadcasted_iota(jnp.int32, (NG, LANES), 1)
    row = lax.broadcasted_iota(jnp.int32, (NG, LANES), 0)
    sign = jnp.where(lane < HALF, 1.0, -1.0).astype(f32)
    wave_z = lax.rem(lane, HALF).astype(f32)
    wave_x = jnp.where(row < NG // 2, row, row - NG).astype(f32)
    plane_sq = wave_x * wave_x + wave_z * wave_z
    factor = NG / (2.0 * math.pi) * (NG / (2.0 * math.pi))

    def both(shapes):
        top = jnp.concatenate([part.astype(bf) for part in shapes], axis=1)
        turned = [(pltpu.roll(part, HALF, 1) * sign).astype(bf) for part in shapes]
        return jnp.concatenate([top, jnp.concatenate(turned, axis=1)], axis=0)

    def cut(sheet, k):
        return sheet[:, k * LANES : (k + 1) * LANES]

    def forward(step, carry):
        first = step * GROUP
        load(step).wait()
        data = field[pl.ds(first, GROUP)].reshape(GROUP * NG, LANES)
        a = lax.dot_general(data, tz_ref[...], NN, preferred_element_type=f32).astype(bf)
        top = [a[k * NG : (k + 1) * NG, :LANES] for k in range(GROUP)]
        low = [a[k * NG : (k + 1) * NG, LANES:] for k in range(GROUP)]
        stack = jnp.concatenate(
            [jnp.concatenate(top, axis=1), jnp.concatenate(low, axis=1)], axis=0
        )
        b = lax.dot_general(ty_ref[...], stack, NN, preferred_element_type=f32)
        for k in range(GROUP):
            by_y[pl.ds(first + k, NG, stride=NG), :] = cut(b, k)
        return carry

    lax.fori_loop(0, NG // GROUP, forward, 0)

    def prime(block, carry):
        fetch(early_ref, block).start()
        return carry

    lax.fori_loop(0, EARLY, prime, 0)

    def middle(step, carry):
        first = step * GROUP
        rows = [by_y[pl.ds((first + k) * NG, NG), :] for k in range(GROUP)]
        h = lax.dot_general(ty_ref[...], both(rows), NN, preferred_element_type=f32)
        scaled = []
        for k in range(GROUP):
            index = first + k
            wave_y = jnp.where(index < NG // 2, index, index - NG).astype(f32)
            squared = plane_sq + wave_y * wave_y
            kernel = jnp.where(squared > 0.5, factor / (squared + SCREEN), 0.0)
            scaled.append(cut(h, k) * kernel)
        g = lax.dot_general(tyi_ref[...], both(scaled), NN, preferred_element_type=f32)
        for k in range(GROUP):
            by_x[pl.ds(first + k, NG, stride=NG), :] = cut(g, k)
        return carry

    lax.fori_loop(0, NG // GROUP, middle, 0)
    wait_greeted(count)

    whole = (planes - 1) * THIRDS

    def own(part, piece):
        return pltpu.make_async_copy(pot.at[part, me], land.at[part, me], own_sem.at[piece])

    def send_pieces(part, piece):
        def body(step, carry):
            peer = lax.rem(me + step, count)
            pltpu.make_async_remote_copy(
                src_ref=pot.at[part, peer],
                dst_ref=land.at[part, me],
                send_sem=send_sem.at[piece],
                recv_sem=recv_sem.at[piece],
                device_id=place(peer),
                device_id_type=pl.DeviceIdType.MESH,
            ).start()
            return carry

        own(part, piece).start()
        lax.fori_loop(1, count, body, 0, unroll=True)

    def arrive(part, piece):
        own(part, piece).wait()
        others = land.at[part, pl.ds(0, count - 1)]
        pltpu.make_async_copy(others, others, recv_sem.at[piece]).wait()

    def leave(part, piece):
        sent = pot.at[part, pl.ds(0, count - 1)]
        pltpu.make_async_copy(sent, sent, send_sem.at[piece]).wait()

    quarter = NG // 4
    spot = lane[:quarter]

    def backward(local, carry):
        rows = [by_x[pl.ds((local + planes * k) * NG, NG), :] for k in range(count)]
        p = lax.dot_general(tyi_ref[...], both(rows), NN, preferred_element_type=f32).astype(bf)
        tall = jnp.concatenate([cut(p, k) for k in range(count)], axis=0)
        final = lax.dot_general(tall, tzi_ref[...], NN, preferred_element_type=f32)
        flat[...] = final * f32(1.0 / float(NG**3))
        for k in range(count):
            y0, y1, y2, y3 = [flat[pl.ds(k * NG + j, quarter, stride=4), :] for j in range(4)]
            y1, y2, y3 = pltpu.roll(y1, 96, 1), pltpu.roll(y2, 64, 1), pltpu.roll(y3, 32, 1)
            base = k % 4 * 3 * PIECE
            dense[pl.ds(base, quarter, stride=3), :] = jnp.where(spot < 96, y0, y1)
            dense[pl.ds(base + 1, quarter, stride=3), :] = jnp.where(spot < 64, y1, y2)
            dense[pl.ds(base + 2, quarter, stride=3), :] = jnp.where(spot < 32, y2, y3)
            for m in range(3):
                pot[local * 3 + m, k] = dense[base + m * PIECE : base + (m + 1) * PIECE, :].astype(bf)
        @pl.when(local < planes - 1)
        def _():
            send_pieces(pl.ds(local * THIRDS, 2), local * THIRDS)

        @pl.when(local == planes - 1)
        def _():
            for m in range(THIRDS - 1):
                send_pieces(pl.ds(whole + m, 1), whole + m)

        last = local * THIRDS + 2
        send_pieces(pl.ds(last, 1), last)
        return carry

    lax.fori_loop(0, planes, backward, 0)
    total[...] = jnp.zeros_like(total)

    def work(piece, carry):
        third = lax.rem(piece, THIRDS)

        @pl.when((piece < whole) & (third == 0))
        def _():
            arrive(pl.ds(piece, 2), piece)

        @pl.when((piece >= whole) | (third == 2))
        def _():
            arrive(pl.ds(piece, 1), piece)

        wide[...] = land[piece].astype(f32).reshape(cols * PIECE, LANES)
        for half in range(per_piece):
            block = piece * per_piece + half
            slot = lax.rem(block, RING)
            pltpu.make_async_copy(ring.at[slot], ring.at[slot], pair_sem.at[slot]).wait()
            lines = [
                wide[pl.ds(half * strips + j, cols, stride=PIECE), :].astype(bf)
                for j in range(strips)
            ]
            total[...] += lax.dot_general(
                jnp.concatenate(lines, axis=1), ring[slot], NT, preferred_element_type=f32
            )

            @pl.when(block < rest)
            def _():
                fetch(pair_ref, block).start()

        return carry

    lax.fori_loop(0, pieces, work, 0)

    scale = f32(1.0 / math.sqrt(float(NG**3)))
    low_lane = lax.broadcasted_iota(jnp.int32, (cols // 2, LANES), 1) < share
    for k in range(npoints // LANES):
        tile = total[:, k * LANES : (k + 1) * LANES] * scale
        top, low = tile[: cols // 2], tile[cols // 2 :]
        parts[2 * k] = jnp.where(low_lane, top, pltpu.roll(low, share, 1))
        parts[2 * k + 1] = jnp.where(low_lane, pltpu.roll(top, share, 1), low)

    def part_copy(step, source, slot):
        peer = lax.rem(me + step, count)
        return pltpu.make_async_remote_copy(
            src_ref=parts.at[source],
            dst_ref=held.at[slot],
            send_sem=part_send.at[step],
            recv_sem=part_recv.at[step],
            device_id=place(peer),
            device_id_type=pl.DeviceIdType.MESH,
        )

    def part_start(step, carry):
        part_copy(step, lax.rem(me + step, count), me).start()
        return carry

    lax.fori_loop(1, count, part_start, 0)
    held[me] = parts[me]

    for piece in range(pieces):
        if piece >= whole or piece % THIRDS == 2:
            leave(pl.ds(piece, 1), piece)
        elif piece % THIRDS == 0:
            leave(pl.ds(piece, 2), piece)

    def part_receive(step, carry):
        source = lax.rem(me + count - step, count)
        part_copy(step, source, source).wait_recv()
        return carry

    lax.fori_loop(1, count, part_receive, 0)
    summed = jnp.sum(held[...], axis=0)
    pile = jnp.concatenate([summed, pltpu.roll(summed, share, 1)], axis=0)
    o_ref[...] = pile[:, :share]

    def part_drain(step, carry):
        part_copy(step, lax.rem(me + step, count), me).wait_send()
        return carry

    lax.fori_loop(1, count, part_drain, 0)


def solve_and_project(field, early, pair, count):
    bf = jnp.bfloat16
    f32 = jnp.float32
    cos_tab, sin_tab = literal_tables(NG)
    keep = NG // 2 + 1

    def padded(table):
        return np.pad(table[:, :keep], ((0, LANES - NG), (0, HALF - keep)))

    cz, sz = padded(cos_tab), padded(sin_tab)
    tz = np.concatenate([cz, -sz, -sz, -cz], axis=1)
    ty = np.concatenate([cos_tab, sin_tab], axis=1)
    tyi = np.concatenate([cos_tab, -sin_tab], axis=1)
    spot = np.arange(HALF)[:, None]
    weight = np.where((spot == 0) | (spot == NG // 2), 1.0, 2.0).astype(bf)
    tzi = np.concatenate([cz.T * weight, -(sz.T * weight)], axis=0)
    tz, ty, tyi, tzi = [jnp.asarray(table, bf) for table in (tz, ty, tyi, tzi)]
    pieces = NG // count * 3
    blocks, npoints, span = pair.shape
    cols = count
    any_spec = pl.BlockSpec(memory_space=pl.ANY)
    vmem_spec = pl.BlockSpec(memory_space=pltpu.VMEM)
    return pl.pallas_call(
        solve_project_kernel,
        out_shape=jax.ShapeDtypeStruct((cols, npoints // count), f32),
        in_specs=[any_spec] + [vmem_spec] * 4 + [any_spec] * 2,
        out_specs=vmem_spec,
        scratch_shapes=[
            pltpu.VMEM((NG, NG, LANES), bf),
            pltpu.VMEM((NG * NG, LANES), f32),
            pltpu.VMEM((NG * NG, LANES), f32),
            pltpu.VMEM((count * NG, LANES), f32),
            pltpu.VMEM((4 * 3 * PIECE, LANES), f32),
            pltpu.VMEM((pieces, count, PIECE, LANES), bf),
            pltpu.VMEM((RING, npoints, span), bf),
            pltpu.VMEM((pieces, count, PIECE, LANES), bf),
            pltpu.VMEM((cols * PIECE, LANES), f32),
            pltpu.VMEM((cols, npoints), f32),
            pltpu.VMEM((count, cols // 2, LANES), f32),
            pltpu.VMEM((count, cols // 2, LANES), f32),
            pltpu.SemaphoreType.DMA((NG // GROUP,)),
            pltpu.SemaphoreType.DMA((pieces,)),
            pltpu.SemaphoreType.DMA((pieces,)),
            pltpu.SemaphoreType.DMA((pieces,)),
            pltpu.SemaphoreType.DMA((RING,)),
            pltpu.SemaphoreType.DMA((count,)),
            pltpu.SemaphoreType.DMA((count,)),
        ],
        compiler_params=pltpu.CompilerParams(
            collective_id=2, has_side_effects=True, vmem_limit_bytes=54 << 20
        ),
        name="solve_project",
    )(field.reshape(NG, NG, LANES), tz, ty, tyi, tzi, early, pair).T


def fits_planes(rows, npoints, cols, count):
    blocks = rows // SPAN
    return (
        cols == count
        and rows % (NG * NG) == 0
        and NG % (rows // (NG * NG)) == 0
        and blocks >= 3 * JOIN
        and EARLY + 1 < JOIN
        and npoints % (count * ROWS) == 0
        and NG // LINES % JOIN == 0
        and npoints % TAKE == 0
        and 2 * npoints == count * LANES
    )


def shards(orbitals, inverse_panel, points):
    bf = jnp.bfloat16
    row_count = orbitals.shape[0]
    grid_count = lax.axis_size("grid")
    vec_count = lax.axis_size("vec")
    npoints = points.shape[0]
    offset = (lax.axis_index("grid") * vec_count + lax.axis_index("vec")) * row_count
    picked = pick_rows(orbitals, points, offset)
    cols = inverse_panel.shape[1]
    if fits_planes(row_count, npoints, cols, grid_count * vec_count):
        panel = inverse_panel.T
        point_rows, early, *fits = share_rows(picked, grid_count, vec_count, panel, orbitals)
        pair, field = pair_and_fit(orbitals, point_rows, panel, *fits)
        return solve_and_project(field, early, pair, grid_count * vec_count)
    point_rows = share_rows(picked, grid_count, vec_count)

    def pair_block(block):
        correlation = lax.dot_general(
            block, point_rows, (((1,), (1,)), ((), ())), preferred_element_type=jnp.float32
        )
        return (correlation * correlation).astype(bf)

    pair = lax.map(pair_block, orbitals.reshape(4, row_count // 4, orbitals.shape[1])).reshape(
        row_count, npoints
    )
    fit_cols = lax.dot_general(
        inverse_panel, pair, (((0,), (1,)), ((), ())), preferred_element_type=jnp.float32
    ).astype(bf)
    slab = lax.all_to_all(fit_cols, "vec", split_axis=0, concat_axis=1, tiled=True)
    col_local = slab.shape[0]
    planes = NG // grid_count
    field = slab.reshape(col_local, planes, NG, NG)
    cos_tab, sin_tab = wave_tables(NG)
    z_re = mult(field, cos_tab, "vxyz,zk->vxyk").astype(bf)
    z_im = (-mult(field, sin_tab, "vxyz,zk->vxyk")).astype(bf)
    y_re = (mult(z_re, cos_tab, "vxyz,yk->vxkz") + mult(z_im, sin_tab, "vxyz,yk->vxkz")).astype(bf)
    y_im = (mult(z_im, cos_tab, "vxyz,yk->vxkz") - mult(z_re, sin_tab, "vxyz,yk->vxkz")).astype(bf)
    stacked = jnp.stack([y_re, y_im])
    waves = wavenumber(lax.iota(jnp.int32, NG), NG)
    y_waves = wavenumber(lax.axis_index("grid") * planes + lax.iota(jnp.int32, planes), NG)
    kernel = screened(waves, y_waves, waves)[None]
    piece = lax.all_to_all(stacked, "grid", split_axis=3, concat_axis=2, tiled=True)
    p_re = piece[0]
    p_im = piece[1]
    x_re = mult(p_re, cos_tab, "vxyz,xk->vkyz") + mult(p_im, sin_tab, "vxyz,xk->vkyz")
    x_im = mult(p_im, cos_tab, "vxyz,xk->vkyz") - mult(p_re, sin_tab, "vxyz,xk->vkyz")
    q_re = (x_re * kernel).astype(bf)
    q_im = (x_im * kernel).astype(bf)
    i_re = (mult(q_re, cos_tab, "vxyz,xk->vkyz") - mult(q_im, sin_tab, "vxyz,xk->vkyz")).astype(bf)
    i_im = (mult(q_im, cos_tab, "vxyz,xk->vkyz") + mult(q_re, sin_tab, "vxyz,xk->vkyz")).astype(bf)
    spectrum = lax.all_to_all(
        jnp.stack([i_re, i_im]), "grid", split_axis=2, concat_axis=3, tiled=True
    )
    s_re = spectrum[0]
    s_im = spectrum[1]
    h_re = (mult(s_re, cos_tab, "vxyz,yk->vxkz") - mult(s_im, sin_tab, "vxyz,yk->vxkz")).astype(bf)
    h_im = (mult(s_im, cos_tab, "vxyz,yk->vxkz") + mult(s_re, sin_tab, "vxyz,yk->vxkz")).astype(bf)
    final = mult(h_re, cos_tab, "vxyz,zk->vxyk") - mult(h_im, sin_tab, "vxyz,zk->vxyk")
    potential = (final / float(NG**3)).astype(bf).reshape(col_local, planes * NG * NG)
    pot_rows = lax.all_to_all(potential, "vec", split_axis=1, concat_axis=0, tiled=True)
    return project(pair, pot_rows)


def solution(mesh):
    in_specs = (P(("grid", "vec"), None), P(), P())
    out_specs = P(("grid", "vec"), None)
    return jax.shard_map(shards, mesh=mesh, in_specs=in_specs, out_specs=out_specs, check_vma=False)
```

```python
import math

import jax
import jax.numpy as jnp
import numpy as np
from jax import lax
from jax.experimental import pallas as pl
from jax.experimental.pallas import tpu as pltpu
from jax.sharding import PartitionSpec as P

NG = 96


SCREEN = 2.25


def wave_tables(count):
    index = lax.iota(jnp.int32, count)
    phase = index[:, None] * index[None, :] % count
    angle = phase.astype(jnp.float32) * (2.0 * math.pi / count)
    return (jnp.cos(angle).astype(jnp.bfloat16), jnp.sin(angle).astype(jnp.bfloat16))


def literal_tables(count):
    index = np.arange(count)
    phase = index[:, None] * index[None, :] % count
    angle = phase.astype(np.float32) * np.float32(2.0 * math.pi / count)
    return np.cos(angle).astype(jnp.bfloat16), np.sin(angle).astype(jnp.bfloat16)


def wavenumber(index, count):
    return jnp.where(index < count // 2, index, index - count).astype(jnp.float32)


def screened(wave_x, wave_y, wave_z):
    squared = (
        wave_x[:, None, None] * wave_x[:, None, None]
        + wave_y[None, :, None] * wave_y[None, :, None]
        + wave_z[None, None, :] * wave_z[None, None, :]
    )
    factor = NG / (2.0 * math.pi) * (NG / (2.0 * math.pi))
    return jnp.where(squared > 0.5, factor / (squared + SCREEN), jnp.float32(0.0))


def mult(data, table, form):
    return jnp.einsum(form, data, table, preferred_element_type=jnp.float32)


LANES = 128


def exchange_kernel(axes, total, gather, x_ref, o_ref, held, send_sem, recv_sem, own_sem):
    if len(axes) == 2:
        vec_count = lax.axis_size("vec")
        count = lax.axis_size("grid") * vec_count
        me = lax.axis_index("grid") * vec_count + lax.axis_index("vec")
    else:
        count = lax.axis_size(axes[0])
        me = lax.axis_index(axes[0])
    land = held if total else o_ref

    def place(index):
        if len(axes) == 2:
            return (index // vec_count, lax.rem(index, vec_count))
        if axes[0] == "grid":
            return (index, lax.axis_index("vec"))
        return (lax.axis_index("grid"), index)

    def part(index):
        return x_ref if gather else x_ref.at[index]

    barrier = pltpu.get_barrier_semaphore()

    def greet(step, carry):
        pl.semaphore_signal(
            barrier,
            inc=1,
            device_id=place(lax.rem(me + step, count)),
            device_id_type=pl.DeviceIdType.MESH,
        )
        return carry

    lax.fori_loop(1, count, greet, 0)
    own = pltpu.make_async_copy(part(me), land.at[me], own_sem)
    own.start()
    pl.semaphore_wait(barrier, count - 1)

    def copy(step, source, slot):
        peer = lax.rem(me + step, count)
        return pltpu.make_async_remote_copy(
            src_ref=part(source),
            dst_ref=land.at[slot],
            send_sem=send_sem.at[step],
            recv_sem=recv_sem.at[step],
            device_id=place(peer),
            device_id_type=pl.DeviceIdType.MESH,
        )

    def send(step, carry):
        copy(step, lax.rem(me + step, count), me).start()
        return carry

    lax.fori_loop(1, count, send, 0)
    own.wait()

    def receive(step, carry):
        source = lax.rem(me + count - step, count)
        copy(step, source, source).wait_recv()
        return carry

    lax.fori_loop(1, count, receive, 0)
    if total:
        o_ref[...] = jnp.sum(held[...].astype(jnp.float32), axis=0).astype(o_ref.dtype)

    def drain(step, carry):
        copy(step, lax.rem(me + step, count), me).wait_send()
        return carry

    lax.fori_loop(1, count, drain, 0)


def exchange(blocks, ident, total=False, axes=("grid", "vec"), gather=False):
    rows, lanes = blocks.shape[-2:]
    count = 1
    for axis in axes:
        count *= lax.axis_size(axis)
    shape = (rows, lanes) if total else (count, rows, lanes)
    held_shape = blocks.shape if total else (1, 8, LANES)

    def body(*refs):
        exchange_kernel(axes, total, gather, *refs)

    return pl.pallas_call(
        body,
        out_shape=jax.ShapeDtypeStruct(shape, blocks.dtype),
        in_specs=[pl.BlockSpec(memory_space=pltpu.VMEM)],
        out_specs=pl.BlockSpec(memory_space=pltpu.VMEM),
        scratch_shapes=[
            pltpu.VMEM(held_shape, blocks.dtype),
            pltpu.SemaphoreType.DMA((count,)),
            pltpu.SemaphoreType.DMA((count,)),
            pltpu.SemaphoreType.DMA(()),
        ],
        compiler_params=pltpu.CompilerParams(
            collective_id=ident, has_side_effects=True, vmem_limit_bytes=32 << 20
        ),
        name="exchange_total" if total else "exchange_gather" if gather else "exchange_blocks",
    )(blocks)


def share_kernel(chunks, early, refs):
    if early:
        x_ref, panel_ref, orb_ref, o_ref, early_ref, lines_ref, fit_ref = refs[:7]
        orbs, pairs, fit_rows, orb_sem, pair_sem = refs[-5:]
        near, wide, far, sum1, sum2, sum3, sends, recvs, own_sem = refs[7:-5]
    else:
        x_ref, o_ref, near, wide, far, sum1, sum2, sum3, sends, recvs, own_sem = refs
    bf = jnp.bfloat16
    f32 = jnp.float32
    vec_count = lax.axis_size("vec")
    deep = lax.axis_size("grid") // 2
    grid_at, mine = lax.axis_index("grid"), lax.axis_index("vec")
    level, core = grid_at // 2, lax.rem(grid_at, 2)
    other = 1 - core
    across = vec_count - 1

    def partner(step):
        return (level * 2 + other, mine)

    def beside(step):
        return (grid_at, lax.rem(mine + step, vec_count))

    def above(step):
        return (lax.rem(level + step, deep) * 2 + core, mine)

    peers = [partner(1)]
    peers += [beside(step) for step in range(1, vec_count)]
    peers += [above(step) for step in range(1, deep)]
    barrier = pltpu.get_barrier_semaphore()
    for peer in peers:
        pl.semaphore_signal(barrier, inc=1, device_id=peer, device_id_type=pl.DeviceIdType.MESH)
    pl.semaphore_wait(barrier, len(peers))

    def send(source, target, slot, peer):
        return pltpu.make_async_remote_copy(
            src_ref=source,
            dst_ref=target,
            send_sem=sends.at[slot],
            recv_sem=recvs.at[slot],
            device_id=peer,
            device_id_type=pl.DeviceIdType.MESH,
        )

    per_chunk = 2 + 2 * across + 2 * (deep - 1)

    def copies(stage, c):
        base = c * per_chunk
        if stage == 0:
            return [send(x_ref.at[c, other], near.at[c], base, partner(1))]
        if stage == 1:
            return [
                send(
                    sum1.at[c, lax.rem(mine + step, vec_count)],
                    wide.at[c, step - 1],
                    base + step,
                    beside(step),
                )
                for step in range(1, vec_count)
            ]
        if stage == 2:
            return [
                send(
                    sum2.at[c, lax.rem(level + step, deep)],
                    far.at[c, step - 1],
                    base + across + step,
                    above(step),
                )
                for step in range(1, deep)
            ]
        base += across + deep
        if stage == 3:
            spot = o_ref.at[c, core, mine, level]
            return [send(sum3.at[c], spot, base + step - 1, above(step)) for step in range(1, deep)]
        base += deep - 1
        if stage == 4:
            spot = o_ref.at[c, core, mine]
            return [send(spot, spot, base + step - 1, beside(step)) for step in range(1, vec_count)]
        spot = o_ref.at[c, core]
        return [send(spot, spot, base + across, partner(1))]

    def own(c):
        return pltpu.make_async_copy(sum3.at[c], o_ref.at[c, core, mine, level], own_sem.at[c])

    def prepare(stage, c):
        for move in copies(stage - 1, c):
            move.wait_recv()
        if stage == 1:
            sum1[c] = (x_ref[c, core].astype(f32) + near[c].astype(f32)).astype(bf)
        if stage == 2:
            total = sum1[c, mine].astype(f32)
            for step in range(across):
                total += wide[c, step].astype(f32)
            sum2[c] = total.astype(bf)
        if stage == 3:
            total = sum2[c, level].astype(f32)
            for step in range(deep - 1):
                total += far[c, step].astype(f32)
            sum3[c] = total.astype(bf)
            own(c).start()
        if stage == 4:
            own(c).wait()

    def fetch():
        return pltpu.make_async_copy(orb_ref.at[pl.ds(0, early)], orbs, orb_sem)

    def keep(c):
        height = pairs.shape[1] // chunks
        part = pl.ds(c * height, height)
        return pltpu.make_async_copy(
            pairs.at[:, part], early_ref.at[:, part], pair_sem.at[c]
        )

    def multiply(c):
        height = pairs.shape[1] // chunks
        rows = o_ref[c].reshape(height, o_ref.shape[-1])

        def body(e, carry):
            part = lax.dot_general(rows, orbs[e], NT, preferred_element_type=f32)
            pairs[e, c * height : (c + 1) * height, :] = (part * part).astype(bf)
            return carry

        lax.fori_loop(0, early, body, 0)

    if early:
        fetch().start()
    for tick in range(chunks + 6):
        for stage in range(6, -1, -1):
            c = tick - stage
            if 0 <= c < chunks:
                if stage > 0:
                    prepare(stage, c)
                if stage < 6:
                    for move in copies(stage, c):
                        move.start()
        if early and tick >= 6:
            if tick == 6:
                fetch().wait()
            multiply(tick - 6)
            keep(tick - 6).start()
    if early:

        fit_ref[...] = jnp.zeros_like(fit_ref)

        def fit(e, carry):
            begin = pl.multiple_of(jnp.maximum(e - 1, 0) * LINES, LINES)
            lines_ref[:, pl.ds(begin, LINES), :] = split_lines(fit_ref, fit_rows)
            fit_ref[...] = lax.dot_general(
                panel_ref[...], pairs[e], NN, preferred_element_type=f32
            )
            return carry

        lax.fori_loop(0, early, fit, 0)
        for c in range(chunks):
            keep(c).wait()
    for c in range(chunks):
        for stage in range(6):
            for move in copies(stage, c):
                move.wait_send()


ROWS = 16


def share_rows(picked, grid_count, vec_count, panel=None, orbitals=None):
    bf = jnp.bfloat16
    npoints, norb = picked.shape
    count = grid_count * vec_count
    if npoints % (count * ROWS) != 0 or grid_count % 2 != 0:
        return lax.psum(picked.astype(jnp.float32), ("grid", "vec")).astype(picked.dtype)
    early = 0 if panel is None else EARLY
    chunks = npoints // (count * ROWS)
    deep = grid_count // 2
    shape = (chunks, 2, vec_count, deep, ROWS, norb)
    slots = chunks * (2 + 2 * (vec_count - 1) + 2 * (deep - 1))
    vmem_spec = pl.BlockSpec(memory_space=pltpu.VMEM)
    any_spec = pl.BlockSpec(memory_space=pl.ANY)
    args = [picked.reshape(shape)]
    in_specs, out_specs = [vmem_spec], [vmem_spec]
    out_shape = [jax.ShapeDtypeStruct(shape, bf)]
    scratch = [
        pltpu.VMEM((chunks, vec_count, deep, ROWS, norb), bf),
        pltpu.VMEM((chunks, vec_count - 1, deep, ROWS, norb), bf),
        pltpu.VMEM((chunks, deep - 1, ROWS, norb), bf),
        pltpu.VMEM((chunks, vec_count, deep, ROWS, norb), bf),
        pltpu.VMEM((chunks, deep, ROWS, norb), bf),
        pltpu.VMEM((chunks, ROWS, norb), bf),
        pltpu.SemaphoreType.DMA((slots,)),
        pltpu.SemaphoreType.DMA((slots,)),
        pltpu.SemaphoreType.DMA((chunks,)),
    ]
    if early:
        cols = panel.shape[0]
        args += [panel, orbitals.reshape(-1, SPAN, norb)]
        in_specs += [vmem_spec, any_spec]
        out_specs += [any_spec, vmem_spec, vmem_spec]
        out_shape += [
            jax.ShapeDtypeStruct((early, npoints, SPAN), bf),
            jax.ShapeDtypeStruct((cols, (early - 1) * LINES, LANES), bf),
            jax.ShapeDtypeStruct((cols, SPAN), jnp.float32),
        ]
        scratch += [
            pltpu.VMEM((early, SPAN, norb), bf),
            pltpu.VMEM((early, npoints, SPAN), bf),
            pltpu.VMEM(((cols + 1) * LINES, LANES), jnp.float32),
            pltpu.SemaphoreType.DMA(()),
            pltpu.SemaphoreType.DMA((chunks,)),
        ]

    def body(*refs):
        share_kernel(chunks, early, refs)

    outs = pl.pallas_call(
        body,
        out_shape=out_shape,
        in_specs=in_specs,
        out_specs=out_specs,
        scratch_shapes=scratch,
        compiler_params=pltpu.CompilerParams(
            collective_id=4, has_side_effects=True, vmem_limit_bytes=46 << 20
        ),
        name="share_rows",
    )(*args)
    rows = outs[0].reshape(npoints, norb)
    return (rows, *outs[1:]) if early else rows


OCTET = 8


def pick_kernel(points_ref, flags_ref, offset_ref, orb_ref, o_ref, found, where, spare, sheet, sem):
    octets, _, norb = orb_ref.shape
    limit = octets * OCTET
    npoints = o_ref.shape[0]
    offset = offset_ref[0]
    sheet[...] = jnp.zeros_like(sheet)

    def fetch(slot, octet):
        return pltpu.make_async_copy(orb_ref.at[octet], found.at[slot], sem)

    def look(i, held):
        position = points_ref[i] - offset
        inside = (position >= 0) & (position < limit)

        @pl.when(inside)
        def _():
            fetch(held, position // OCTET).start()
            where[held] = i
            spare[held] = lax.rem(position, OCTET)

        return held + inside.astype(jnp.int32)

    def scan(group, held):
        return lax.cond(
            flags_ref[group] > 0,
            lambda h: lax.fori_loop(
                0, OCTET, lambda k, n: look(group * OCTET + k, n), h, unroll=True
            ),
            lambda h: h,
            held,
        )

    held = lax.fori_loop(0, npoints // OCTET, scan, 0)

    def settle(slot, carry):
        fetch(slot, 0).wait()
        return carry

    lax.fori_loop(0, held, settle, 0)
    line = lax.broadcasted_iota(jnp.int32, (OCTET, norb), 0)

    def place(slot, carry):
        octet = found[slot].astype(jnp.float32)
        row = jnp.sum(jnp.where(line == spare[slot], octet, 0.0), axis=0, keepdims=True)
        sheet[pl.ds(where[slot], 1), :] = row
        return carry

    lax.fori_loop(0, held, place, 0)
    o_ref[...] = sheet[...].astype(o_ref.dtype)


def pick_rows(orbitals, points, offset):
    rows, norb = orbitals.shape
    npoints = points.shape[0]
    position = points - offset
    if rows % OCTET != 0 or npoints % OCTET != 0:
        inside = (position >= 0) & (position < rows)
        picked = jnp.take(orbitals, jnp.clip(position, 0, rows - 1), axis=0)
        return jnp.where(inside[:, None], picked, jnp.zeros_like(picked))
    inside = (position >= 0) & (position < rows)
    flags = jnp.max(inside.reshape(-1, OCTET).astype(jnp.int32), axis=1)
    return pl.pallas_call(
        pick_kernel,
        out_shape=jax.ShapeDtypeStruct((npoints, norb), orbitals.dtype),
        in_specs=[
            pl.BlockSpec(memory_space=pltpu.SMEM),
            pl.BlockSpec(memory_space=pltpu.SMEM),
            pl.BlockSpec(memory_space=pltpu.SMEM),
            pl.BlockSpec(memory_space=pl.ANY),
        ],
        out_specs=pl.BlockSpec(memory_space=pltpu.VMEM),
        scratch_shapes=[
            pltpu.VMEM((npoints, OCTET, norb), orbitals.dtype),
            pltpu.SMEM((npoints,), jnp.int32),
            pltpu.SMEM((npoints,), jnp.int32),
            pltpu.VMEM((npoints, norb), jnp.float32),
            pltpu.SemaphoreType.DMA(()),
        ],
        compiler_params=pltpu.CompilerParams(vmem_limit_bytes=28 << 20),
        name="pick_rows",
    )(points, flags, offset[None].astype(jnp.int32), orbitals.reshape(rows // OCTET, OCTET, norb))


def project(pair, pot_rows):
    scale = 1.0 / math.sqrt(float(NG**3))
    term = lax.dot_general(
        pair, pot_rows, (((0,), (1,)), ((), ())), preferred_element_type=jnp.float32
    )
    term = term * jnp.float32(scale)
    npoints, cols = term.shape
    count = lax.axis_size("grid") * lax.axis_size("vec")
    share = npoints // count
    if share * cols % LANES == 0:
        blocks = term.reshape(count, share * cols // LANES, LANES)
        return exchange(blocks, 3, True).reshape(share, cols)
    partial_block = lax.psum_scatter(term, "grid", scatter_dimension=0, tiled=True)
    return lax.psum_scatter(partial_block, "vec", scatter_dimension=0, tiled=True)


def peers_of():
    vec_count = lax.axis_size("vec")
    count = lax.axis_size("grid") * vec_count
    me = lax.axis_index("grid") * vec_count + lax.axis_index("vec")

    def place(index):
        return (index // vec_count, lax.rem(index, vec_count))

    return count, me, place


def greet_all(count, me, place):
    barrier = pltpu.get_barrier_semaphore()

    def greet(step, carry):
        pl.semaphore_signal(
            barrier,
            inc=1,
            device_id=place(lax.rem(me + step, count)),
            device_id_type=pl.DeviceIdType.MESH,
        )
        return carry

    lax.fori_loop(1, count, greet, 0)


def wait_greeted(count):
    pl.semaphore_wait(pltpu.get_barrier_semaphore(), count - 1)


NT = (((1,), (1,)), ((), ()))
NN = (((1,), (0,)), ((), ()))
LINES = 16
SPAN = LINES * NG
TAKE = 512
JOIN = 3
EARLY = 4


def split_lines(fit_ref, fit_rows):
    cols = fit_ref.shape[0]
    for line in range(LINES):
        begin = line * NG
        low = begin // LANES * LANES
        turn = begin - low
        wide = fit_ref[:, low : min(low + 2 * LANES, SPAN)]
        if wide.shape[1] == LANES:
            wide = jnp.concatenate([wide, wide], axis=1)
        if turn:
            wide = pltpu.roll(wide, 2 * LANES - turn, 1)
        fit_rows[pl.ds(line, cols, stride=LINES), :] = wide[:, :LANES]
    return fit_rows[: cols * LINES].astype(jnp.bfloat16).reshape(cols, LINES, LANES)


def pair_fit_kernel(
    orb_ref, rows_ref, panel_ref, early_ref, last_ref, pair_ref, field_ref, fit_buf, fit_rows, out_buf,
    send_sem, recv_sem, own_sem,
):
    bf = jnp.bfloat16
    block = pl.program_id(0) + EARLY
    blocks = pl.num_programs(0) + EARLY
    count, me, place = peers_of()
    npoints = rows_ref.shape[0]
    cols = panel_ref.shape[0]
    per_plane = NG // LINES
    groups = blocks // JOIN
    tall = JOIN * LINES

    def send(group, begin, lines, source=None):
        slot = lax.rem(group, 2)
        source = out_buf.at[slot] if source is None else source
        start = pl.multiple_of(lax.rem(group * JOIN, per_plane) * LINES + begin, LINES)
        target = field_ref.at[me, group * JOIN // per_plane, pl.ds(start, lines)]

        def body(step, carry):
            peer = lax.rem(me + step, count)
            pltpu.make_async_remote_copy(
                src_ref=source.at[peer, pl.ds(begin, lines)],
                dst_ref=target,
                send_sem=send_sem.at[slot],
                recv_sem=recv_sem.at[me],
                device_id=place(peer),
                device_id_type=pl.DeviceIdType.MESH,
            ).start()
            return carry

        pltpu.make_async_copy(
            source.at[me, pl.ds(begin, lines)], target, own_sem.at[slot]
        ).start()
        lax.fori_loop(1, count, body, 0, unroll=True)

    def drain(group):
        slot = lax.rem(group, 2)
        sent = out_buf.at[slot, pl.ds(0, count - 1)]
        mine = out_buf.at[slot, me]
        pltpu.make_async_copy(mine, mine, own_sem.at[slot]).wait()
        pltpu.make_async_copy(sent, sent, send_sem.at[slot]).wait()

    @pl.when(block == EARLY)
    def _():
        greet_all(count, me, place)

    before = block - 1

    @pl.when((block > 2 * JOIN) & (lax.rem(before, JOIN) == 0))
    def _():
        drain(before // JOIN - 2)

    def multiply(first):
        part = lax.dot_general(
            rows_ref[first : first + TAKE, :], orb_ref[...], NT, preferred_element_type=jnp.float32
        )
        pair_ref[0, first : first + TAKE, :] = (part * part).astype(bf)

    def arrange(index):
        begin = pl.multiple_of(lax.rem(index, JOIN) * LINES, LINES)
        out_buf[lax.rem(index // JOIN, 2), :, pl.ds(begin, LINES), :] = split_lines(
            fit_buf, fit_rows
        )

    @pl.when(block == EARLY)
    def _():
        fit_buf[...] = last_ref[...]

    multiply(0)
    arrange(before)
    for first in range(TAKE, npoints // 2, TAKE):
        multiply(first)

    @pl.when(block == EARLY)
    def _():
        wait_greeted(count)
        send(0, 0, tall, early_ref)

    @pl.when((block > EARLY) & (lax.rem(block, JOIN) == 0))
    def _():
        send(block // JOIN - 1, 0, tall)

    for late in range(JOIN - 1):

        @pl.when(block == blocks - JOIN + 1 + late)
        def _(late=late):
            send(groups - 1, late * LINES, LINES)

    for first in range(npoints // 2, npoints, TAKE):
        multiply(first)
    fit_buf[...] = lax.dot_general(
        panel_ref[...], pair_ref[0], NN, preferred_element_type=jnp.float32
    )

    @pl.when(block == blocks - 1)
    def _():
        arrange(block)
        send(groups - 1, (JOIN - 1) * LINES, LINES)

        def receive(step, carry):
            source = lax.rem(me + count - step, count)
            land = field_ref.at[source]
            pltpu.make_async_copy(land, land, recv_sem.at[source]).wait()
            return carry

        lax.fori_loop(1, count, receive, 0)
        drain(groups - 2)
        drain(groups - 1)


def pair_and_fit(orbitals, point_rows, panel, early_fit, last_fit):
    bf = jnp.bfloat16
    rows, norb = orbitals.shape
    npoints = point_rows.shape[0]
    cols = panel.shape[0]
    blocks = rows // SPAN - EARLY
    planes = rows // (NG * NG)
    count = lax.axis_size("grid") * lax.axis_size("vec")
    return pl.pallas_call(
        pair_fit_kernel,
        grid=(blocks,),
        in_specs=[
            pl.BlockSpec((SPAN, norb), lambda i: (i + EARLY, 0)),
            pl.BlockSpec((npoints, norb), lambda i: (0, 0)),
            pl.BlockSpec((cols, npoints), lambda i: (0, 0)),
            pl.BlockSpec((cols, JOIN * LINES, LANES), lambda i: (0, 0, 0)),
            pl.BlockSpec((cols, SPAN), lambda i: (0, 0)),
        ],
        out_specs=[
            pl.BlockSpec((1, npoints, SPAN), lambda i: (i, 0, 0)),
            pl.BlockSpec(memory_space=pltpu.HBM),
        ],
        out_shape=[
            jax.ShapeDtypeStruct((blocks, npoints, SPAN), bf),
            jax.ShapeDtypeStruct((count, planes, NG, LANES), bf),
        ],
        scratch_shapes=[
            pltpu.VMEM((cols, SPAN), jnp.float32),
            pltpu.VMEM(((cols + 1) * LINES, LANES), jnp.float32),
            pltpu.VMEM((2, cols, JOIN * LINES, LANES), bf),
            pltpu.SemaphoreType.DMA((2,)),
            pltpu.SemaphoreType.DMA((count,)),
            pltpu.SemaphoreType.DMA((2,)),
        ],
        compiler_params=pltpu.CompilerParams(
            collective_id=1, has_side_effects=True, vmem_limit_bytes=50 << 20
        ),
        name="pair_fit_send",
    )(orbitals, point_rows, panel, early_fit, last_fit)


GROUP = 24
HALF = 64
PIECE = NG * NG // LANES // 3
RING = EARLY


def solve_project_kernel(
    field_ref, tz_ref, ty_ref, tyi_ref, tzi_ref, early_ref, pair_ref, o_ref,
    field, by_y, by_x, flat, dense, pot, ring, land, wide, total, parts, held,
    field_sem, send_sem, recv_sem, own_sem, pair_sem, part_send, part_recv,
):
    bf = jnp.bfloat16
    f32 = jnp.float32
    count, me, place = peers_of()
    rest, npoints, _ = pair_ref.shape
    blocks = rest + EARLY
    pieces = pot.shape[0]
    cols = count
    share = npoints // count
    planes = NG // count
    per_piece = blocks // pieces
    strips = SPAN // LANES

    def load(step):
        part = pl.ds(step * GROUP, GROUP)
        return pltpu.make_async_copy(field_ref.at[part], field.at[part], field_sem.at[step])

    def fetch(ref, block):
        slot = lax.rem(block, RING)
        return pltpu.make_async_copy(ref.at[block], ring.at[slot], pair_sem.at[slot])

    for step in range(NG // GROUP):
        load(step).start()
    greet_all(count, me, place)

    lane = lax.broadcasted_iota(jnp.int32, (NG, LANES), 1)
    row = lax.broadcasted_iota(jnp.int32, (NG, LANES), 0)
    sign = jnp.where(lane < HALF, 1.0, -1.0).astype(f32)
    wave_z = lax.rem(lane, HALF).astype(f32)
    wave_x = jnp.where(row < NG // 2, row, row - NG).astype(f32)
    plane_sq = wave_x * wave_x + wave_z * wave_z
    factor = NG / (2.0 * math.pi) * (NG / (2.0 * math.pi))

    def both(shapes):
        top = jnp.concatenate([part.astype(bf) for part in shapes], axis=1)
        turned = [(pltpu.roll(part, HALF, 1) * sign).astype(bf) for part in shapes]
        return jnp.concatenate([top, jnp.concatenate(turned, axis=1)], axis=0)

    def cut(sheet, k):
        return sheet[:, k * LANES : (k + 1) * LANES]

    def forward(step, carry):
        first = step * GROUP
        load(step).wait()
        data = field[pl.ds(first, GROUP)].reshape(GROUP * NG, LANES)
        a = lax.dot_general(data, tz_ref[...], NN, preferred_element_type=f32).astype(bf)
        top = [a[k * NG : (k + 1) * NG, :LANES] for k in range(GROUP)]
        low = [a[k * NG : (k + 1) * NG, LANES:] for k in range(GROUP)]
        stack = jnp.concatenate(
            [jnp.concatenate(top, axis=1), jnp.concatenate(low, axis=1)], axis=0
        )
        b = lax.dot_general(ty_ref[...], stack, NN, preferred_element_type=f32)
        for k in range(GROUP):
            by_y[pl.ds(first + k, NG, stride=NG), :] = cut(b, k)
        return carry

    lax.fori_loop(0, NG // GROUP, forward, 0)

    def prime(block, carry):
        fetch(early_ref, block).start()
        return carry

    lax.fori_loop(0, EARLY, prime, 0)

    def middle(step, carry):
        first = step * GROUP
        rows = [by_y[pl.ds((first + k) * NG, NG), :] for k in range(GROUP)]
        h = lax.dot_general(ty_ref[...], both(rows), NN, preferred_element_type=f32)
        scaled = []
        for k in range(GROUP):
            index = first + k
            wave_y = jnp.where(index < NG // 2, index, index - NG).astype(f32)
            squared = plane_sq + wave_y * wave_y
            kernel = jnp.where(squared > 0.5, factor / (squared + SCREEN), 0.0)
            scaled.append(cut(h, k) * kernel)
        g = lax.dot_general(tyi_ref[...], both(scaled), NN, preferred_element_type=f32)
        for k in range(GROUP):
            by_x[pl.ds(first + k, NG, stride=NG), :] = cut(g, k)
        return carry

    lax.fori_loop(0, NG // GROUP, middle, 0)
    wait_greeted(count)

    def own(piece):
        return pltpu.make_async_copy(pot.at[piece, me], land.at[piece, me], own_sem.at[piece])

    def send_piece(piece):
        def body(step, carry):
            peer = lax.rem(me + step, count)
            pltpu.make_async_remote_copy(
                src_ref=pot.at[piece, peer],
                dst_ref=land.at[piece, me],
                send_sem=send_sem.at[piece],
                recv_sem=recv_sem.at[piece],
                device_id=place(peer),
                device_id_type=pl.DeviceIdType.MESH,
            ).start()
            return carry

        own(piece).start()
        lax.fori_loop(1, count, body, 0)

    quarter = NG // 4
    spot = lane[:quarter]

    def backward(local, carry):
        rows = [by_x[pl.ds((local + planes * k) * NG, NG), :] for k in range(count)]
        p = lax.dot_general(tyi_ref[...], both(rows), NN, preferred_element_type=f32).astype(bf)
        tall = jnp.concatenate([cut(p, k) for k in range(count)], axis=0)
        final = lax.dot_general(tall, tzi_ref[...], NN, preferred_element_type=f32)
        flat[: count * NG] = final * f32(1.0 / float(NG**3))
        for k in range(count):
            y0, y1, y2, y3 = [flat[pl.ds(k * NG + j, quarter, stride=4), :] for j in range(4)]
            y1, y2, y3 = pltpu.roll(y1, 96, 1), pltpu.roll(y2, 64, 1), pltpu.roll(y3, 32, 1)
            base = k % 4 * 3 * PIECE
            dense[pl.ds(base, quarter, stride=3), :] = jnp.where(spot < 96, y0, y1)
            dense[pl.ds(base + 1, quarter, stride=3), :] = jnp.where(spot < 64, y1, y2)
            dense[pl.ds(base + 2, quarter, stride=3), :] = jnp.where(spot < 32, y2, y3)
            for m in range(3):
                pot[local * 3 + m, k] = dense[base + m * PIECE : base + (m + 1) * PIECE, :].astype(bf)
        for m in range(3):
            send_piece(local * 3 + m)
        return carry

    lax.fori_loop(0, planes, backward, 0)
    total[...] = jnp.zeros_like(total)

    def work(piece, carry):
        own(piece).wait()
        others = land.at[piece, pl.ds(0, count - 1)]
        pltpu.make_async_copy(others, others, recv_sem.at[piece]).wait()
        wide[: cols * PIECE] = land[piece].astype(f32).reshape(cols * PIECE, LANES)
        for half in range(per_piece):
            block = piece * per_piece + half
            slot = lax.rem(block, RING)
            pltpu.make_async_copy(ring.at[slot], ring.at[slot], pair_sem.at[slot]).wait()
            lines = [
                wide[pl.ds(half * strips + j, cols, stride=PIECE), :].astype(bf)
                for j in range(strips)
            ]
            total[...] += lax.dot_general(
                jnp.concatenate(lines, axis=1), ring[slot], NT, preferred_element_type=f32
            )

            @pl.when(block < rest)
            def _():
                fetch(pair_ref, block).start()

        return carry

    lax.fori_loop(0, pieces, work, 0)

    scale = f32(1.0 / math.sqrt(float(NG**3)))
    low_lane = lax.broadcasted_iota(jnp.int32, (cols // 2, LANES), 1) < share
    for k in range(npoints // LANES):
        tile = total[:, k * LANES : (k + 1) * LANES] * scale
        top, low = tile[: cols // 2], tile[cols // 2 :]
        parts[2 * k] = jnp.where(low_lane, top, pltpu.roll(low, share, 1))
        parts[2 * k + 1] = jnp.where(low_lane, pltpu.roll(top, share, 1), low)

    def part_copy(step, source, slot):
        peer = lax.rem(me + step, count)
        return pltpu.make_async_remote_copy(
            src_ref=parts.at[source],
            dst_ref=held.at[slot],
            send_sem=part_send.at[step],
            recv_sem=part_recv.at[step],
            device_id=place(peer),
            device_id_type=pl.DeviceIdType.MESH,
        )

    def part_start(step, carry):
        part_copy(step, lax.rem(me + step, count), me).start()
        return carry

    lax.fori_loop(1, count, part_start, 0)
    held[me] = parts[me]

    def drain_piece(piece, carry):
        sent = pot.at[piece, pl.ds(0, count - 1)]
        pltpu.make_async_copy(sent, sent, send_sem.at[piece]).wait()
        return carry

    lax.fori_loop(0, pieces, drain_piece, 0)

    def part_receive(step, carry):
        source = lax.rem(me + count - step, count)
        part_copy(step, source, source).wait_recv()
        return carry

    lax.fori_loop(1, count, part_receive, 0)
    summed = jnp.sum(held[...], axis=0)
    pile = jnp.concatenate([summed, pltpu.roll(summed, share, 1)], axis=0)
    o_ref[...] = pile[:, :share]

    def part_drain(step, carry):
        part_copy(step, lax.rem(me + step, count), me).wait_send()
        return carry

    lax.fori_loop(1, count, part_drain, 0)


def solve_and_project(field, early, pair, count):
    bf = jnp.bfloat16
    f32 = jnp.float32
    cos_tab, sin_tab = literal_tables(NG)
    keep = NG // 2 + 1

    def padded(table):
        return np.pad(table[:, :keep], ((0, LANES - NG), (0, HALF - keep)))

    cz, sz = padded(cos_tab), padded(sin_tab)
    tz = np.concatenate([cz, -sz, -sz, -cz], axis=1)
    ty = np.concatenate([cos_tab, sin_tab], axis=1)
    tyi = np.concatenate([cos_tab, -sin_tab], axis=1)
    spot = np.arange(HALF)[:, None]
    weight = np.where((spot == 0) | (spot == NG // 2), 1.0, 2.0).astype(bf)
    tzi = np.concatenate([cz.T * weight, -(sz.T * weight)], axis=0)
    tz, ty, tyi, tzi = [jnp.asarray(table, bf) for table in (tz, ty, tyi, tzi)]
    pieces = NG // count * 3
    blocks, npoints, span = pair.shape
    cols = count
    any_spec = pl.BlockSpec(memory_space=pl.ANY)
    vmem_spec = pl.BlockSpec(memory_space=pltpu.VMEM)
    return pl.pallas_call(
        solve_project_kernel,
        out_shape=jax.ShapeDtypeStruct((cols, npoints // count), f32),
        in_specs=[any_spec] + [vmem_spec] * 4 + [any_spec] * 2,
        out_specs=vmem_spec,
        scratch_shapes=[
            pltpu.VMEM((NG, NG, LANES), bf),
            pltpu.VMEM(((NG + 1) * NG, LANES), f32),
            pltpu.VMEM(((NG + 1) * NG, LANES), f32),
            pltpu.VMEM((count * NG + 8, LANES), f32),
            pltpu.VMEM((4 * 3 * PIECE + 8, LANES), f32),
            pltpu.VMEM((pieces, count, PIECE, LANES), bf),
            pltpu.VMEM((RING, npoints, span), bf),
            pltpu.VMEM((pieces, count, PIECE, LANES), bf),
            pltpu.VMEM(((cols + 1) * PIECE, LANES), f32),
            pltpu.VMEM((cols, npoints), f32),
            pltpu.VMEM((count, cols // 2, LANES), f32),
            pltpu.VMEM((count, cols // 2, LANES), f32),
            pltpu.SemaphoreType.DMA((NG // GROUP,)),
            pltpu.SemaphoreType.DMA((pieces,)),
            pltpu.SemaphoreType.DMA((pieces,)),
            pltpu.SemaphoreType.DMA((pieces,)),
            pltpu.SemaphoreType.DMA((RING,)),
            pltpu.SemaphoreType.DMA((count,)),
            pltpu.SemaphoreType.DMA((count,)),
        ],
        compiler_params=pltpu.CompilerParams(
            collective_id=2, has_side_effects=True, vmem_limit_bytes=54 << 20
        ),
        name="solve_project",
    )(field.reshape(NG, NG, LANES), tz, ty, tyi, tzi, early, pair).T


def fits_planes(rows, npoints, cols, count):
    blocks = rows // SPAN
    return (
        cols == count
        and rows % (NG * NG) == 0
        and NG % (rows // (NG * NG)) == 0
        and blocks >= EARLY + 2 * JOIN
        and EARLY == JOIN + 1
        and npoints % (count * ROWS) == 0
        and NG // LINES % JOIN == 0
        and npoints % TAKE == 0
        and 2 * npoints == count * LANES
    )


def shards(orbitals, inverse_panel, points):
    bf = jnp.bfloat16
    row_count = orbitals.shape[0]
    grid_count = lax.axis_size("grid")
    vec_count = lax.axis_size("vec")
    npoints = points.shape[0]
    offset = (lax.axis_index("grid") * vec_count + lax.axis_index("vec")) * row_count
    picked = pick_rows(orbitals, points, offset)
    cols = inverse_panel.shape[1]
    if fits_planes(row_count, npoints, cols, grid_count * vec_count):
        panel = inverse_panel.T
        point_rows, early, *fits = share_rows(picked, grid_count, vec_count, panel, orbitals)
        pair, field = pair_and_fit(orbitals, point_rows, panel, *fits)
        return solve_and_project(field, early, pair, grid_count * vec_count)
    point_rows = share_rows(picked, grid_count, vec_count)

    def pair_block(block):
        correlation = lax.dot_general(
            block, point_rows, (((1,), (1,)), ((), ())), preferred_element_type=jnp.float32
        )
        return (correlation * correlation).astype(bf)

    pair = lax.map(pair_block, orbitals.reshape(4, row_count // 4, orbitals.shape[1])).reshape(
        row_count, npoints
    )
    fit_cols = lax.dot_general(
        inverse_panel, pair, (((0,), (1,)), ((), ())), preferred_element_type=jnp.float32
    ).astype(bf)
    slab = lax.all_to_all(fit_cols, "vec", split_axis=0, concat_axis=1, tiled=True)
    col_local = slab.shape[0]
    planes = NG // grid_count
    field = slab.reshape(col_local, planes, NG, NG)
    cos_tab, sin_tab = wave_tables(NG)
    z_re = mult(field, cos_tab, "vxyz,zk->vxyk").astype(bf)
    z_im = (-mult(field, sin_tab, "vxyz,zk->vxyk")).astype(bf)
    y_re = (mult(z_re, cos_tab, "vxyz,yk->vxkz") + mult(z_im, sin_tab, "vxyz,yk->vxkz")).astype(bf)
    y_im = (mult(z_im, cos_tab, "vxyz,yk->vxkz") - mult(z_re, sin_tab, "vxyz,yk->vxkz")).astype(bf)
    stacked = jnp.stack([y_re, y_im])
    waves = wavenumber(lax.iota(jnp.int32, NG), NG)
    y_waves = wavenumber(lax.axis_index("grid") * planes + lax.iota(jnp.int32, planes), NG)
    kernel = screened(waves, y_waves, waves)[None]
    piece = lax.all_to_all(stacked, "grid", split_axis=3, concat_axis=2, tiled=True)
    p_re = piece[0]
    p_im = piece[1]
    x_re = mult(p_re, cos_tab, "vxyz,xk->vkyz") + mult(p_im, sin_tab, "vxyz,xk->vkyz")
    x_im = mult(p_im, cos_tab, "vxyz,xk->vkyz") - mult(p_re, sin_tab, "vxyz,xk->vkyz")
    q_re = (x_re * kernel).astype(bf)
    q_im = (x_im * kernel).astype(bf)
    i_re = (mult(q_re, cos_tab, "vxyz,xk->vkyz") - mult(q_im, sin_tab, "vxyz,xk->vkyz")).astype(bf)
    i_im = (mult(q_im, cos_tab, "vxyz,xk->vkyz") + mult(q_re, sin_tab, "vxyz,xk->vkyz")).astype(bf)
    spectrum = lax.all_to_all(
        jnp.stack([i_re, i_im]), "grid", split_axis=2, concat_axis=3, tiled=True
    )
    s_re = spectrum[0]
    s_im = spectrum[1]
    h_re = (mult(s_re, cos_tab, "vxyz,yk->vxkz") - mult(s_im, sin_tab, "vxyz,yk->vxkz")).astype(bf)
    h_im = (mult(s_im, cos_tab, "vxyz,yk->vxkz") + mult(s_re, sin_tab, "vxyz,yk->vxkz")).astype(bf)
    final = mult(h_re, cos_tab, "vxyz,zk->vxyk") - mult(h_im, sin_tab, "vxyz,zk->vxyk")
    potential = (final / float(NG**3)).astype(bf).reshape(col_local, planes * NG * NG)
    pot_rows = lax.all_to_all(potential, "vec", split_axis=1, concat_axis=0, tiled=True)
    return project(pair, pot_rows)


def solution(mesh):
    in_specs = (P(("grid", "vec"), None), P(), P())
    out_specs = P(("grid", "vec"), None)
    return jax.shard_map(shards, mesh=mesh, in_specs=in_specs, out_specs=out_specs, check_vma=False)
```
